256 devices in a mesh: branch: 2 (over x_lo), row: 8 (over y, core), col: 16 (over x_hi, z).
Axes of the slice: x: 4 (x_hi: 2, x_lo: 2; x = x_hi * 2 + x_lo), y: 4, z: 8, core: 2. Of those that a mesh axis runs over, the one named last changes fastest.
Arguments:
- homolog_embedding: bfloat16 [256, 512, 256], P(('branch', 'row'), 'col'), may hold values from -6 to 6
- pair_representation: bfloat16 [512, 512, 128], P('col', ('branch', 'row')), may hold values from -6 to 6
- alignment_entry_mask: int32 [256, 512], P(('branch', 'row'), 'col'), may hold values 0 or 1
- residue_presence_mask: int32 [512], replicated, may hold values 0 or 1
- residue_chain_index: int32 [512], replicated, may hold values from 0 to 3, as said below
- row_projection_weights: bfloat16 [256, 1024], replicated, may hold values from -25 to 25
- horizontal_attend_merge: bfloat16 [256, 256], replicated, may hold values from -0.375 to 0.375
- pair_bias_matrix: bfloat16 [128, 8], replicated, may hold values from -0.5 to 0.5
- same_chain_bias: float32 [8], replicated, may hold values from -5 to 5
- column_projection_weights: bfloat16 [256, 1024], replicated, may hold values from -25 to 25
- vertical_attend_merge: bfloat16 [256, 256], replicated, may hold values from -0.375 to 0.375
- homolog_mlp_expand: bfloat16 [256, 1024], replicated, may hold values from -0.375 to 0.375
- homolog_mlp_contract: bfloat16 [1024, 256], replicated, may hold values from -0.1875 to 0.1875
- tensor_product_linear: bfloat16 [256, 64], replicated, may hold values from -0.375 to 0.375
- outer_output_matrix: bfloat16 [1024, 128], replicated, may hold values from -1 to 1
- triangle_input_weights: bfloat16 [128, 640], replicated, may hold values from -0.5 to 0.5
- triangle_output_matrix: bfloat16 [128, 128], replicated, may hold values from -2 to 2
- pair_up_weight: bfloat16 [128, 512], replicated, may hold values from -0.5 to 0.5
- pair_down_weight: bfloat16 [512, 128], replicated, may hold values from -0.25 to 0.25
Outputs:
- msa_out: bfloat16 [256, 512, 256], P(('branch', 'row'), 'col')
- updated_pair_state: bfloat16 [512, 512, 128], P('col', ('branch', 'row'))
The draws below stay inside these ranges and needn't reach their ends.
Inputs may be any that keep to these rules, and one draw needn't show every extreme that they name: `residue_chain_index`: chain numbers never fall along the residues.
All inputs are finite; a program needn't handle non-finite values. No bound on the sum of `alignment_entry_mask` on one device may be relied on, other than what follows from the above.
Results may differ from the reference program's by a relative error of at most 0.025.
The reference program's roundings to bfloat16 on the way count: a program that leaves them out, or rounds other values in their place, can miss the bound.
Values may be sent and summed in bfloat16 or wider, within the bound.
A program may use at most 128 MiB of HBM per device.

```python
import math
import jax
import jax.numpy as jnp
from jax import lax

ALIGNED_FEATURES = 256
HEADS = 8
PER_HEAD_WIDTH = 32
CZ = 128
PRODUCT_FEATURES = 32
ALIGNED_MLP_SIZE = 1024
PAIR_TRANS = 512
HOMOLOG_NUMBER = 256
AMINO_ACIDS = 512


def query_weights(key):
    starting_offset = jax.random.normal(jax.random.fold_in(key, 11), (ALIGNED_FEATURES, 4 * ALIGNED_FEATURES), jnp.float32)
    starting_offset = jnp.clip(starting_offset, -4.0, 4.0) / math.sqrt(ALIGNED_FEATURES)
    return starting_offset


def draw_row_projection_weights(key, part):
    return query_weights(jax.random.fold_in(key, 101)).astype(jnp.bfloat16)


def draw_column_projection_weights(key, part):
    return query_weights(jax.random.fold_in(key, 202)).astype(jnp.bfloat16)


def draw_residue_chain_index(key, part):
    cuts = jax.random.randint(jax.random.fold_in(key, 303), (3,), 1, AMINO_ACIDS)
    places = jnp.arange(AMINO_ACIDS, dtype=jnp.int32)
    return jnp.sum((places[:, None] >= cuts[None, :]).astype(jnp.int32), axis=1)


def set_ends(entries, key, low, top_value):
    extent = entries.shape
    place = [jax.random.randint(jax.random.fold_in(key, axis), (), 0, extent[axis]) for axis in range(len(extent))]
    entries = entries.at[tuple(place)].set(low)
    longest = extent.index(max(extent))
    place[longest] = (place[longest] + 1) % extent[longest]
    return entries.at[tuple(place)].set(top_value)


def block_levels(stream_key, extent, pieces, least, largest):
    def one(axis_at, blocks):
        draws = jax.random.uniform(jax.random.fold_in(jax.random.fold_in(stream_key, 6), axis_at), (blocks,), jnp.float32, least / len(pieces), largest / len(pieces))
        return jnp.repeat(jnp.exp(draws), extent[axis_at] // blocks).reshape((-1,) + (1,) * (len(extent) - axis_at - 1))

    gain = one(*pieces[0])
    for cut in pieces[1:]:
        gain = gain * one(*cut)
    return gain


def centred(rng, dims, width, bound, split=(), kind=jnp.bfloat16):
    factor_of = block_levels(rng, dims, split, -0.22, 0.18) if split else 1.0
    drawn = jax.random.normal(rng, dims, jnp.float32) * width * factor_of
    return jnp.minimum(jnp.maximum(drawn, -bound), bound).astype(kind)


def setup_inputs(seed: int = 0) -> dict:
    splits = jax.random.split(jax.random.key(seed), 20)
    homolog_embedding = centred(splits[0], (HOMOLOG_NUMBER, AMINO_ACIDS, ALIGNED_FEATURES), 1.0, 6.0, ((0, 16), (1, 16)))
    pair_representation = centred(splits[1], (AMINO_ACIDS, AMINO_ACIDS, CZ), 0.5, 6.0, ((0, 16), (1, 16)))
    alignment_entry_mask = set_ends((jax.random.randint(splits[2], (HOMOLOG_NUMBER, AMINO_ACIDS), 0, 8) < 7).astype(jnp.int32), jax.random.fold_in(splits[2], 1), 0, 1)
    residue_presence_mask = set_ends((jax.random.randint(splits[3], (AMINO_ACIDS,), 0, 16) < 15).astype(jnp.int32), jax.random.fold_in(splits[3], 1), 0, 1)
    residue_chain_index = draw_residue_chain_index(jax.random.fold_in(splits[19], 71), 0)
    row_projection_weights = draw_row_projection_weights(jax.random.fold_in(splits[19], 71), 0)
    horizontal_attend_merge = centred(splits[6], (ALIGNED_FEATURES, ALIGNED_FEATURES), ALIGNED_FEATURES ** -0.5, 0.375)
    pair_bias_matrix = centred(splits[7], (CZ, HEADS), CZ ** -0.5, 0.5)
    same_chain_bias = jnp.clip(jax.random.uniform(splits[8], (HEADS,), jnp.float32, -5.0, 5.0), -5.0, 5.0)
    column_projection_weights = draw_column_projection_weights(jax.random.fold_in(splits[19], 71), 0)
    vertical_attend_merge = centred(splits[10], (ALIGNED_FEATURES, ALIGNED_FEATURES), ALIGNED_FEATURES ** -0.5, 0.375)
    homolog_mlp_expand = centred(splits[11], (ALIGNED_FEATURES, ALIGNED_MLP_SIZE), ALIGNED_FEATURES ** -0.5, 0.375)
    homolog_mlp_contract = centred(splits[12], (ALIGNED_MLP_SIZE, ALIGNED_FEATURES), ALIGNED_MLP_SIZE ** -0.5, 0.1875)
    tensor_product_linear = centred(splits[13], (ALIGNED_FEATURES, 2 * PRODUCT_FEATURES), ALIGNED_FEATURES ** -0.5, 0.375)
    outer_output_matrix = centred(splits[14], (PRODUCT_FEATURES * PRODUCT_FEATURES, CZ), PRODUCT_FEATURES ** -0.5, 1.0)
    triangle_input_weights = centred(splits[15], (CZ, 5 * CZ), CZ ** -0.5, 0.5)
    triangle_output_matrix = centred(splits[16], (CZ, CZ), (CZ // 16) ** -0.5, 2.0)
    pair_up_weight = centred(splits[17], (CZ, PAIR_TRANS), CZ ** -0.5, 0.5)
    pair_down_weight = centred(splits[18], (PAIR_TRANS, CZ), PAIR_TRANS ** -0.5, 0.25)
    return {"homolog_embedding": homolog_embedding, "pair_representation": pair_representation, "alignment_entry_mask": alignment_entry_mask, "residue_presence_mask": residue_presence_mask, "residue_chain_index": residue_chain_index, "row_projection_weights": row_projection_weights, "horizontal_attend_merge": horizontal_attend_merge, "pair_bias_matrix": pair_bias_matrix, "same_chain_bias": same_chain_bias, "column_projection_weights": column_projection_weights, "vertical_attend_merge": vertical_attend_merge, "homolog_mlp_expand": homolog_mlp_expand, "homolog_mlp_contract": homolog_mlp_contract, "tensor_product_linear": tensor_product_linear, "outer_output_matrix": outer_output_matrix, "triangle_input_weights": triangle_input_weights, "triangle_output_matrix": triangle_output_matrix, "pair_up_weight": pair_up_weight, "pair_down_weight": pair_down_weight}


EPSILON = 1e-05
NEGATIVE = -1000000000.0

def cast_to_halfprecision(tensor):
    return lax.optimization_barrier(tensor.astype(jnp.bfloat16))

def layer_normalize(tensor):
    tensor = tensor.astype(jnp.float32)
    centre = tensor - lax.optimization_barrier(jnp.mean(tensor, axis=-1, keepdims=True))
    spread = lax.optimization_barrier(jnp.mean(centre * centre, axis=-1, keepdims=True))
    return centre * lax.rsqrt(spread + EPSILON)

def split_blocks(normed, weights):
    projected = jnp.dot(normed, weights, preferred_element_type=jnp.float32)
    lead = projected.shape[:-1]
    parts = projected.reshape(lead + (4, HEADS, PER_HEAD_WIDTH))
    queries = cast_to_halfprecision(parts[..., 0, :, :] * PER_HEAD_WIDTH ** (-0.5))
    key_rows = cast_to_halfprecision(parts[..., 1, :, :])
    value_rows = cast_to_halfprecision(parts[..., 2, :, :])
    gating = jax.nn.sigmoid(projected[..., 3 * HEADS * PER_HEAD_WIDTH:])
    return (queries, key_rows, value_rows, gating)

def attend(queries, key_rows, value_rows, bias, key_presence_mask):
    scores = jnp.einsum('ihd,jhd->hij', queries.astype(jnp.float32), key_rows.astype(jnp.float32)) + bias
    scores = jnp.where(key_presence_mask[None, None, :] > 0, scores, NEGATIVE)
    highest = lax.optimization_barrier(jnp.max(scores, axis=-1, keepdims=True))
    powers = jnp.exp(scores - highest)
    totals = lax.optimization_barrier(jnp.sum(powers, axis=-1))
    summed = jnp.einsum('hij,jhd->ihd', cast_to_halfprecision(powers).astype(jnp.float32), value_rows.astype(jnp.float32))
    return summed / jnp.transpose(totals)[:, :, None]

def reference(homolog_embedding, pair_representation, alignment_entry_mask, residue_presence_mask, residue_chain_index, row_projection_weights, horizontal_attend_merge, pair_bias_matrix, same_chain_bias, column_projection_weights, vertical_attend_merge, homolog_mlp_expand, homolog_mlp_contract, tensor_product_linear, outer_output_matrix, triangle_input_weights, triangle_output_matrix, pair_up_weight, pair_down_weight):
    key_presence_mask = alignment_entry_mask.astype(jnp.float32)
    pair_normed = cast_to_halfprecision(layer_normalize(pair_representation))
    same_chain = (residue_chain_index[:, None] == residue_chain_index[None, :]).astype(jnp.float32)
    bias_terms = jnp.dot(pair_normed, pair_bias_matrix, preferred_element_type=jnp.float32) + same_chain_bias[None, None, :].astype(jnp.float32) * same_chain[:, :, None]
    pair_bias = cast_to_halfprecision(jnp.transpose(bias_terms, (2, 0, 1))).astype(jnp.float32)
    row_normed_input = cast_to_halfprecision(layer_normalize(homolog_embedding))

    def single_row_attention(inputs):
        normed_row, mask_row = inputs
        queries, key_rows, value_rows, gating = split_blocks(normed_row, row_projection_weights)
        attended = attend(queries, key_rows, value_rows, pair_bias, mask_row)
        gated = cast_to_halfprecision(attended.reshape(attended.shape[0], HEADS * PER_HEAD_WIDTH) * gating)
        return jnp.dot(gated, horizontal_attend_merge, preferred_element_type=jnp.float32)
    alignment_row_state = homolog_embedding.astype(jnp.float32) + lax.map(single_row_attention, (row_normed_input, key_presence_mask))
    column_normed_input = cast_to_halfprecision(layer_normalize(alignment_row_state))

    def col_one(inputs):
        normed_col, mask_col = inputs
        queries, key_rows, value_rows, gating = split_blocks(normed_col, column_projection_weights)
        attended = attend(queries, key_rows, value_rows, jnp.zeros((), jnp.float32), mask_col)
        gated = cast_to_halfprecision(attended.reshape(attended.shape[0], HEADS * PER_HEAD_WIDTH) * gating)
        return jnp.dot(gated, vertical_attend_merge, preferred_element_type=jnp.float32)
    column_update_term = lax.map(col_one, (jnp.transpose(column_normed_input, (1, 0, 2)), jnp.transpose(key_presence_mask)))
    alignment_column_state = alignment_row_state + jnp.transpose(column_update_term, (1, 0, 2))
    transition_normed_input = cast_to_halfprecision(layer_normalize(alignment_column_state))
    alignment_hidden_units = cast_to_halfprecision(jax.nn.relu(jnp.dot(transition_normed_input, homolog_mlp_expand, preferred_element_type=jnp.float32)))
    alignment_final_state = alignment_column_state + jnp.dot(alignment_hidden_units, homolog_mlp_contract, preferred_element_type=jnp.float32)
    outer_normed_input = cast_to_halfprecision(layer_normalize(alignment_final_state))
    factors = jnp.dot(outer_normed_input, tensor_product_linear, preferred_element_type=jnp.float32) * key_presence_mask[:, :, None]
    left_factor = cast_to_halfprecision(factors[..., :PRODUCT_FEATURES]).astype(jnp.float32)
    right_factor = cast_to_halfprecision(factors[..., PRODUCT_FEATURES:]).astype(jnp.float32)

    def opm_one(left_column):
        outer_sum = jnp.einsum('sx,sjy->jxy', left_column, right_factor)
        outer_mean = cast_to_halfprecision((outer_sum / HOMOLOG_NUMBER).reshape(AMINO_ACIDS, PRODUCT_FEATURES * PRODUCT_FEATURES))
        return jnp.dot(outer_mean, outer_output_matrix, preferred_element_type=jnp.float32)
    pair_opm = pair_representation.astype(jnp.float32) + lax.map(opm_one, jnp.transpose(left_factor, (1, 0, 2)))
    tri_normed = cast_to_halfprecision(layer_normalize(pair_opm))
    projected = jnp.dot(tri_normed, triangle_input_weights, preferred_element_type=jnp.float32)
    residue_keep = residue_presence_mask.astype(jnp.float32)
    pair_keep = (residue_keep[:, None] * residue_keep[None, :])[:, :, None]
    tri_left = cast_to_halfprecision(pair_keep * jax.nn.sigmoid(projected[..., :CZ]) * projected[..., CZ:2 * CZ])
    tri_right = cast_to_halfprecision(pair_keep * jax.nn.sigmoid(projected[..., 2 * CZ:3 * CZ]) * projected[..., 3 * CZ:4 * CZ])
    tri_gate = jax.nn.sigmoid(projected[..., 4 * CZ:])
    tri_mixed = jnp.einsum('ikc,jkc->ijc', tri_left.astype(jnp.float32), tri_right.astype(jnp.float32))
    mixed_normed = cast_to_halfprecision(layer_normalize(tri_mixed))
    pair_tri = pair_opm + tri_gate * jnp.dot(mixed_normed, triangle_output_matrix, preferred_element_type=jnp.float32)
    pair_trans_in = cast_to_halfprecision(layer_normalize(pair_tri))
    pair_hidden = cast_to_halfprecision(jax.nn.relu(jnp.dot(pair_trans_in, pair_up_weight, preferred_element_type=jnp.float32)))
    updated_pair_state = (pair_tri + jnp.dot(pair_hidden, pair_down_weight, preferred_element_type=jnp.float32)).astype(jnp.bfloat16)
    return (alignment_final_state.astype(jnp.bfloat16), updated_pair_state)
```

```python
import jax
import jax.numpy as jnp
from jax import lax
from jax.experimental import pallas as pl
from jax.experimental.pallas import tpu as pltpu
from jax.sharding import Mesh
from jax.sharding import PartitionSpec as P

HEADS = 8
PER_HEAD_WIDTH = 32
CZ = 128
PRODUCT_FEATURES = 32
COL = ("col_0", "col_1")


EPSILON = 1e-05
NEGATIVE = -1000000000.0


MESH = pl.DeviceIdType.MESH
GROUP = 16
RING = 8


def place():
    axes = [lax.axis_index(a) for a in ("branch", "row", *COL)]
    return (*axes, axes[0] * 8 + axes[1], axes[2] * 8 + axes[3])


def across(b, c):
    return (b // 8, lax.rem(b, 8), c // 8, lax.rem(c, 8))


def remote(src, dst, send, recv, to):
    return pltpu.make_async_remote_copy(
        src_ref=src, dst_ref=dst, send_sem=send, recv_sem=recv, device_id=to, device_id_type=MESH
    )


def call_exchange(kernel, out_shape, scratch, collective_id, sent, *args):
    return pl.pallas_call(
        kernel,
        out_shape=out_shape,
        in_specs=[pl.BlockSpec(memory_space=pltpu.VMEM)] * len(args),
        out_specs=jax.tree.map(lambda _: pl.BlockSpec(memory_space=pltpu.VMEM), out_shape),
        scratch_shapes=scratch,
        compiler_params=pltpu.CompilerParams(
            collective_id=collective_id, has_side_effects=True, vmem_limit_bytes=48 << 20
        ),
        cost_estimate=pl.CostEstimate(flops=0, bytes_accessed=2 * sent, transcendentals=0),
    )(*args)


class Pushes:
    def __init__(self, over, ins, outs, picks, puts, send, recv):
        b, c = place()[4:]
        self.me = b if over == "b" else c
        self.device = (lambda k: across(k, c)) if over == "b" else (lambda k: across(b, k))
        self.parts = list(zip(ins, outs, picks, puts))
        self.send, self.recv = send, recv

    def greet(self, barrier):
        def one(d, carry):
            pl.semaphore_signal(
                barrier, inc=1, device_id=self.device(lax.rem(self.me + d, GROUP)), device_id_type=MESH
            )
            return carry

        lax.fori_loop(1, GROUP, one, 0)

    def copies(self, d, sender):
        peer = lax.rem(self.me + (GROUP - d if sender else d), GROUP)
        for k, (src, dst, pick, put) in enumerate(self.parts):
            yield remote(
                pick(src, self.me if sender else peer),
                put(dst, peer if sender else self.me),
                self.send.at[k, d],
                self.recv.at[k, d],
                self.device(peer),
            )

    def start(self):
        def one(d, carry):
            for copy in self.copies(d, False):
                copy.start()
            return carry

        lax.fori_loop(1, GROUP, one, 0)
        for src, dst, pick, put in self.parts:
            put(dst, self.me)[...] = pick(src, self.me)[...]

    def finish(self):
        def one(d, carry):
            for copy in self.copies(d, True):
                copy.wait_recv()
            for copy in self.copies(d, False):
                copy.wait_send()
            return carry

        lax.fori_loop(1, GROUP, one, 0)


def exchange(over, arrays, shapes, picks, puts, collective_id):
    n = len(arrays)

    def kernel(*refs):
        pushes = Pushes(over, refs[:n], refs[n : 2 * n], picks, puts, refs[2 * n], refs[2 * n + 1])
        barrier = pltpu.get_barrier_semaphore()
        pushes.greet(barrier)
        pl.semaphore_wait(barrier, GROUP - 1)
        pushes.start()
        pushes.finish()

    out_shape = [jax.ShapeDtypeStruct(s, jnp.bfloat16) for s in shapes]
    scratch = [pltpu.SemaphoreType.DMA((n, GROUP))] * 2
    return call_exchange(kernel, out_shape, scratch, collective_id, 1 << 18, *arrays)


def ring_gather(start, whole, own, view, twins, greeted, send, recv):
    br, ro, x, z, _, c = place()
    at = lambda xx, zz: xx * RING + lax.rem(zz + RING, RING)
    right = (br, ro, x, lax.rem(z + 1, RING))
    left = (br, ro, x, lax.rem(z + RING - 1, RING))
    cross = (br, ro, 1 - x, z)
    twin = (br, ro + 1 - 2 * lax.rem(ro, 2), x, z)
    core = lax.rem(ro, 2)
    copies, handed = [], []

    def push(src, block, half, to):
        k = len(copies)
        copies.append(remote(src, view(whole, block, half, core), send.at[k], recv.at[k], to))
        copies[-1].start()
        return k

    def arrived(k, block, half):
        there = view(whole, block, half, core)
        remote(there, there, send.at[k], recv.at[k], right).wait_recv()

    def hand(block, half):
        if twins:
            handed.append((push(view(whole, block, half, core), block, half, twin), block, half))

    mine = own(start, core)
    k_cross = push(mine, c, None, cross)
    going = {(0, +1): push(mine, c, None, right), (0, -1): push(mine, c, None, left)}
    greeted()
    there = at(1 - x, z)
    arrived(k_cross, there, None)
    for way, to in ((+1, right), (-1, left)):
        going[1, way] = push(view(whole, there, None, core), there, None, to)
    hand(there, None)
    for step in (1, 2, 3):
        coming = {}
        for other in (0, 1):
            for way, to in ((+1, right), (-1, left)):
                block = at((1 - x) if other else x, z - way * step)
                arrived(going[other, way], block, None)
                half = None if step < 3 else (0 if way > 0 else 1)
                coming[other, way] = push(view(whole, block, half, core), block, half, to)
                hand(block, None)
        going = coming
    for other in (0, 1):
        for way in (+1, -1):
            block, half = at((1 - x) if other else x, z - way * 4), 0 if way > 0 else 1
            arrived(going[other, way], block, half)
            hand(block, half)
    for k, block, half in handed:
        there = view(whole, block, half, 1 - core)
        remote(there, there, send.at[k], recv.at[k], twin).wait_recv()
    for copy in copies:
        copy.wait_send()


def ring_copies(twins):
    return 19 + (17 if twins else 0)


def greet_ring(barrier, twins, cross_and_ring):
    br, ro, x, z, _, _ = place()
    to = []
    if cross_and_ring:
        to += [
            (br, ro, x, lax.rem(z + 1, RING)),
            (br, ro, x, lax.rem(z + RING - 1, RING)),
            (br, ro, 1 - x, z),
        ]
    if twins:
        to.append((br, ro + 1 - 2 * lax.rem(ro, 2), x, z))
    for device in to:
        pl.semaphore_signal(barrier, inc=1, device_id=device, device_id_type=MESH)
    return len(to)


def gather_bias_and_rows(bias, rows, mask):
    heads, some, all_ = bias.shape
    half_heads = heads // 2

    def own(ref, core):
        return ref.at[pl.ds(core * half_heads, half_heads)]

    def view(ref, block, half, core):
        first, count = core * half_heads, half_heads
        if half is not None:
            count = half_heads // 2
            first = first + half * count
        return ref.at[pl.ds(first, count), pl.ds(pl.multiple_of(block * some, some), some)]

    picks = [lambda ref, k: ref.at[k]] * 2
    puts = [
        lambda ref, k: ref.at[pl.ds(pl.multiple_of(k * some, some), some)],
        lambda ref, k: ref.at[k],
    ]

    def kernel(b_ref, r_ref, m_ref, ob_ref, or_ref, om_ref, psend, precv, rsend, rrecv):
        pushes = Pushes("c", (r_ref, m_ref), (or_ref, om_ref), picks, puts, psend, precv)
        barrier = pltpu.get_barrier_semaphore()
        pushes.greet(barrier)
        more = greet_ring(barrier, True, False)
        pl.semaphore_wait(barrier, GROUP - 1 + more)
        c = place()[5]

        def meanwhile():
            pushes.start()
            ob_ref[:, pl.ds(pl.multiple_of(c * some, some), some)] = b_ref[...]

        ring_gather(b_ref, ob_ref, own, view, True, meanwhile, rsend, rrecv)
        pushes.finish()

    out_shape = [
        jax.ShapeDtypeStruct((heads, GROUP * some, all_), jnp.bfloat16),
        jax.ShapeDtypeStruct((GROUP * some, rows.shape[2]), jnp.bfloat16),
        jax.ShapeDtypeStruct(mask.shape, jnp.bfloat16),
    ]
    scratch = [pltpu.SemaphoreType.DMA((2, GROUP))] * 2
    scratch += [pltpu.SemaphoreType.DMA((ring_copies(True),))] * 2
    return call_exchange(kernel, out_shape, scratch, 1, 4 << 20, bias, rows, mask)


def gather_factors(left, right):
    rows = left.shape[0]

    def kernel(l_ref, r_ref, ol_ref, or_ref, lsend, lrecv, rsend, rrecv):
        put = lambda ref, k: ref.at[pl.ds(pl.multiple_of(k * rows, rows), rows)]
        b, c = place()[4:]
        pushes = Pushes("b", (l_ref,), (ol_ref,), [lambda ref, k: ref], [put], lsend, lrecv)
        barrier = pltpu.get_barrier_semaphore()
        pushes.greet(barrier)

        def others(act):
            def one(d, carry):
                k = lax.rem(c + d, GROUP)

                @pl.when(jnp.logical_or(b != c, k != c))
                def _():
                    act(k)

                return carry

            lax.fori_loop(0, GROUP, one, 0)

        def senders(act):
            def one(d, carry):
                k = lax.rem(b + d, GROUP)

                @pl.when(jnp.logical_or(b != c, k != b))
                def _():
                    act(k)

                return carry

            lax.fori_loop(0, GROUP, one, 0)

        others(
            lambda k: pl.semaphore_signal(
                barrier, inc=1, device_id=across(c, k), device_id_type=MESH
            )
        )
        senders(
            lambda k: pl.semaphore_signal(
                barrier, inc=1, device_id=across(k, b), device_id_type=MESH
            )
        )
        pl.semaphore_wait(barrier, GROUP - 1 + 2 * jnp.where(b == c, GROUP - 1, GROUP))

        def copy(k):
            return remote(r_ref, put(or_ref, b), rsend.at[k], rrecv.at[b], across(c, k))

        def coming(k):
            there = put(or_ref, k)
            return remote(r_ref, there, rsend.at[k], rrecv.at[k], across(k, b))

        others(lambda k: copy(k).start())
        pushes.start()

        @pl.when(b == c)
        def _():
            put(or_ref, b)[...] = r_ref[...]

        pushes.finish()
        senders(lambda k: coming(k).wait_recv())
        others(lambda k: copy(k).wait_send())

    shape = jax.ShapeDtypeStruct((GROUP * rows, left.shape[1]), jnp.bfloat16)
    scratch = [pltpu.SemaphoreType.DMA((1, GROUP))] * 2 + [pltpu.SemaphoreType.DMA((GROUP,))] * 2
    return call_exchange(kernel, [shape, shape], scratch, 6, 1 << 20, left, right)


def gather_in_order(x, axes, turns):
    blocks = x[None]
    for k in turns:
        blocks = lax.all_gather(blocks, axes[k], axis=0, tiled=True)
    carried = [lax.axis_size(axes[k]) for k in reversed(turns)]
    blocks = blocks.reshape(*carried, *x.shape)
    turned = sorted(range(len(turns)), key=lambda place: turns[len(turns) - 1 - place])
    return blocks.transpose(*turned, *range(len(turns), blocks.ndim)).reshape(-1, *x.shape)


def gathered_by_axis(x, axes, turns, dim):
    blocks = gather_in_order(x, axes, turns)
    dims = list(blocks.shape[1:])
    dims[dim] *= blocks.shape[0]
    return jnp.moveaxis(blocks, 0, dim).reshape(dims)


def layer_normalize(tensor):
    tensor = tensor.astype(jnp.float32)
    centre = tensor - jnp.mean(tensor, axis=-1, keepdims=True)
    spread = jnp.mean(centre * centre, axis=-1, keepdims=True)
    return centre * lax.rsqrt(spread + EPSILON)


def split_blocks(normed, weights):
    projected = jnp.dot(normed, weights, preferred_element_type=jnp.float32)
    channel_count = weights.shape[0]
    queries = (projected[..., :channel_count] * PER_HEAD_WIDTH ** (-0.5)).astype(jnp.bfloat16)
    key_rows = projected[..., channel_count : 2 * channel_count].astype(jnp.bfloat16)
    value_rows = projected[..., 2 * channel_count : 3 * channel_count].astype(jnp.bfloat16)
    gating = jax.nn.sigmoid(projected[..., 3 * channel_count :])
    return (queries, key_rows, value_rows, gating)


def on_device(
    homolog_embedding,
    pair_representation,
    alignment_entry_mask,
    residue_presence_mask,
    residue_chain_index,
    row_projection_weights,
    horizontal_attend_merge,
    pair_bias_matrix,
    same_chain_bias,
    column_projection_weights,
    vertical_attend_merge,
    homolog_mlp_expand,
    homolog_mlp_contract,
    tensor_product_linear,
    outer_output_matrix,
    triangle_input_weights,
    triangle_output_matrix,
    pair_up_weight,
    pair_down_weight,
):
    device_local_rows, residue_total, channel_count = homolog_embedding.shape
    pair_cols = pair_representation.shape[1]
    row_place = lax.axis_index(COL)
    col_place = lax.axis_index(("branch", "row"))
    chain_here = lax.dynamic_slice_in_dim(
        residue_chain_index, row_place * residue_total, residue_total
    )
    chain_there = lax.dynamic_slice_in_dim(residue_chain_index, col_place * pair_cols, pair_cols)
    residue_keep = residue_presence_mask.astype(jnp.float32)
    keep_here = lax.dynamic_slice_in_dim(residue_keep, row_place * residue_total, residue_total)
    keep_there = lax.dynamic_slice_in_dim(residue_keep, col_place * pair_cols, pair_cols)
    pair_normed = layer_normalize(pair_representation).astype(jnp.bfloat16)
    same_chain = (chain_here[:, None] == chain_there[None, :]).astype(jnp.float32)
    weights = lax.dot_general(
        pair_bias_matrix,
        pair_normed.reshape(residue_total * pair_cols, -1),
        (((0,), (1,)), ((), ())),
        preferred_element_type=jnp.float32,
    )
    bias_tile = (
        weights + same_chain_bias[:, None] * same_chain.reshape(1, residue_total * pair_cols)
    ).astype(jnp.bfloat16)
    group_count = GROUP
    residue_piece = residue_total // group_count
    key_presence_mask = alignment_entry_mask.astype(jnp.bfloat16)
    row_presence = jnp.pad(key_presence_mask[:, None, :], ((0, 0), (0, 7), (0, 96)))
    col_presence = jnp.transpose(
        key_presence_mask.reshape(device_local_rows, group_count, residue_piece), (1, 2, 0)
    )
    col_presence = jnp.pad(
        col_presence, ((0, 0), (0, 8 - residue_piece), (0, 128 - device_local_rows))
    )
    bias_blocks, mask_cols = exchange(
        "b",
        (bias_tile, col_presence),
        ((GROUP, *bias_tile.shape), col_presence.shape),
        [lambda ref, k: ref, lambda ref, k: ref.at[k]],
        [lambda ref, k: ref.at[k]] * 2,
        0,
    )
    pair_bias = jnp.transpose(
        bias_blocks.reshape(GROUP, HEADS, residue_total, pair_cols), (1, 2, 0, 3)
    ).reshape(HEADS, residue_total, GROUP * pair_cols)
    mask_cols = jnp.transpose(
        mask_cols[:, :residue_piece, :device_local_rows], (1, 0, 2)
    ).reshape(residue_piece, GROUP * device_local_rows)
    row_normed_input = layer_normalize(homolog_embedding).astype(jnp.bfloat16)
    full_bias, normed_whole, mask_whole = gather_bias_and_rows(
        pair_bias, row_normed_input, row_presence
    )
    normed_whole = normed_whole[None]
    mask_whole = mask_whole[:, 0, :residue_total].reshape(1, GROUP * residue_total)
    full_bias = full_bias.astype(jnp.float32)
    few_rows, all_residues = mask_whole.shape
    queries, key_rows, value_rows, gating = split_blocks(normed_whole, row_projection_weights)
    query_heads = queries.reshape(few_rows, all_residues, HEADS, PER_HEAD_WIDTH)
    key_heads = key_rows.reshape(few_rows, all_residues, HEADS, PER_HEAD_WIDTH)
    value_heads = value_rows.reshape(few_rows, all_residues, HEADS, PER_HEAD_WIDTH)
    scores = (
        jnp.einsum("sihd,sjhd->shij", query_heads, key_heads, preferred_element_type=jnp.float32)
        + full_bias[None]
    )
    scores = jnp.where(mask_whole[:, None, None, :] > 0, scores, NEGATIVE)
    highest = jnp.max(scores, axis=-1, keepdims=True)
    powers = jnp.exp(scores - highest)
    totals = jnp.sum(powers, axis=-1)
    summed = jnp.einsum(
        "shij,sjhd->sihd",
        powers.astype(jnp.bfloat16),
        value_heads,
        preferred_element_type=jnp.float32,
    )
    attended = (summed / jnp.transpose(totals, (0, 2, 1))[..., None]).reshape(
        few_rows, all_residues, channel_count
    )
    gated_whole = (attended * gating).astype(jnp.bfloat16)
    (row_gated,) = exchange(
        "c",
        (gated_whole[0],),
        ((GROUP, residue_total, channel_count),),
        [lambda ref, k: ref.at[pl.ds(pl.multiple_of(k * residue_total, residue_total), residue_total)]],
        [lambda ref, k: ref.at[k]],
        2,
    )
    alignment_row_state = homolog_embedding.astype(jnp.float32) + jnp.dot(
        row_gated, horizontal_attend_merge, preferred_element_type=jnp.float32
    )
    column_normed_input = layer_normalize(alignment_row_state).astype(jnp.bfloat16)
    split_input = jnp.transpose(column_normed_input, (1, 0, 2))
    rows_of = lambda ref, k: ref.at[
        :, pl.ds(pl.multiple_of(k * device_local_rows, device_local_rows), device_local_rows)
    ]
    residues_of = lambda ref, k: ref.at[pl.ds(k * residue_piece, residue_piece)]
    (normed_cols,) = exchange(
        "b",
        (split_input,),
        ((residue_piece, GROUP * device_local_rows, channel_count),),
        [residues_of],
        [rows_of],
        3,
    )
    residue_count, total_rows = mask_cols.shape
    normed_flat = normed_cols
    col_queries, col_keys, col_values, col_gating = split_blocks(
        normed_flat, column_projection_weights
    )
    query_part = col_queries.reshape(residue_count, total_rows, HEADS, PER_HEAD_WIDTH)
    key_part = col_keys.reshape(residue_count, total_rows, HEADS, PER_HEAD_WIDTH)
    value_part = col_values.reshape(residue_count, total_rows, HEADS, PER_HEAD_WIDTH)
    scores = jnp.einsum("ishd,ithd->ihst", query_part, key_part, preferred_element_type=jnp.float32)
    scores = jnp.where(mask_cols[:, None, None, :] > 0, scores, NEGATIVE)
    highest = jnp.max(scores, axis=-1, keepdims=True)
    powers = jnp.exp(scores - highest)
    totals = jnp.sum(powers, axis=-1)
    summed = jnp.einsum(
        "ihst,ithd->ihsd",
        powers.astype(jnp.bfloat16),
        value_part,
        preferred_element_type=jnp.float32,
    )
    attended = jnp.transpose(summed / totals[..., None], (0, 2, 1, 3)).reshape(
        residue_count, total_rows, channel_count
    )
    gated = (attended * col_gating).astype(jnp.bfloat16)
    (returned,) = exchange(
        "b",
        (gated,),
        ((residue_total, device_local_rows, channel_count),),
        [rows_of],
        [residues_of],
        4,
    )
    column_gated_output = jnp.transpose(returned, (1, 0, 2))
    alignment_column_state = alignment_row_state + jnp.dot(
        column_gated_output, vertical_attend_merge, preferred_element_type=jnp.float32
    )
    transition_normed_input = layer_normalize(alignment_column_state).astype(jnp.bfloat16)
    alignment_hidden_units = jax.nn.relu(
        jnp.dot(transition_normed_input, homolog_mlp_expand, preferred_element_type=jnp.float32)
    ).astype(jnp.bfloat16)
    alignment_final_state = alignment_column_state + jnp.dot(
        alignment_hidden_units, homolog_mlp_contract, preferred_element_type=jnp.float32
    )
    outer_normed_input = layer_normalize(alignment_final_state).astype(jnp.bfloat16)
    factors = (
        jnp.dot(outer_normed_input, tensor_product_linear, preferred_element_type=jnp.float32)
        * alignment_entry_mask.astype(jnp.float32)[:, :, None]
    )
    left_factor = (
        factors[..., :PRODUCT_FEATURES]
        .astype(jnp.bfloat16)
        .reshape(device_local_rows, residue_total * PRODUCT_FEATURES)
    )
    right_factor = (
        factors[..., PRODUCT_FEATURES:]
        .astype(jnp.bfloat16)
        .reshape(device_local_rows, residue_total * PRODUCT_FEATURES)
    )
    left_all, right_rows = gather_factors(left_factor, right_factor)
    seq_total = left_all.shape[0]
    outer_sum = lax.dot_general(
        left_all, right_rows, (((0,), (0,)), ((), ())), preferred_element_type=jnp.float32
    )
    outer_sum = jnp.transpose(
        outer_sum.reshape(residue_total, PRODUCT_FEATURES, pair_cols, PRODUCT_FEATURES),
        (0, 2, 1, 3),
    ).reshape(residue_total, pair_cols, PRODUCT_FEATURES * PRODUCT_FEATURES)
    outer_mean = (outer_sum / seq_total).astype(jnp.bfloat16)
    pair_opm = pair_representation.astype(jnp.float32) + jnp.dot(
        outer_mean, outer_output_matrix, preferred_element_type=jnp.float32
    )
    tri_normed = layer_normalize(pair_opm).astype(jnp.bfloat16)
    projected = jnp.dot(tri_normed, triangle_input_weights, preferred_element_type=jnp.float32)
    pair_keep = (keep_here[:, None] * keep_there[None, :])[:, :, None]
    tri_left = (
        pair_keep * jax.nn.sigmoid(projected[..., :CZ]) * projected[..., CZ : 2 * CZ]
    ).astype(jnp.bfloat16)
    tri_right = (
        pair_keep
        * jax.nn.sigmoid(projected[..., 2 * CZ : 3 * CZ])
        * projected[..., 3 * CZ : 4 * CZ]
    ).astype(jnp.bfloat16)
    tri_gate = jax.nn.sigmoid(projected[..., 4 * CZ :])
    right_all = gathered_by_axis(tri_right, COL, (0, 1), 0)
    turned = lax.psum_scatter(
        jnp.einsum("ikc,jkc->jic", tri_left, right_all, preferred_element_type=jnp.float32).astype(
            jnp.bfloat16
        ),
        ("branch", "row"),
        scatter_dimension=0,
        tiled=True,
    ).astype(jnp.float32)
    tri_mixed = jnp.transpose(turned, (1, 0, 2))
    mixed_normed = layer_normalize(tri_mixed).astype(jnp.bfloat16)
    pair_tri = pair_opm + tri_gate * jnp.dot(
        mixed_normed, triangle_output_matrix, preferred_element_type=jnp.float32
    )
    pair_trans_in = layer_normalize(pair_tri).astype(jnp.bfloat16)
    pair_hidden = jax.nn.relu(
        jnp.dot(pair_trans_in, pair_up_weight, preferred_element_type=jnp.float32)
    ).astype(jnp.bfloat16)
    updated_pair_state = (
        pair_tri + jnp.dot(pair_hidden, pair_down_weight, preferred_element_type=jnp.float32)
    ).astype(jnp.bfloat16)
    return (alignment_final_state.astype(jnp.bfloat16), updated_pair_state)


def solution(mesh):
    split = Mesh(
        mesh.devices.reshape(mesh.shape["branch"], mesh.shape["row"], 2, 8),
        ("branch", "row", "col_0", "col_1"),
    )
    in_specs = (
        P(("branch", "row"), COL, None),
        P(COL, ("branch", "row"), None),
        P(("branch", "row"), COL),
        P(),
        P(),
        P(),
        P(),
        P(),
        P(),
        P(),
        P(),
        P(),
        P(),
        P(),
        P(),
        P(),
        P(),
        P(),
        P(),
    )
    out_specs = (P(("branch", "row"), COL, None), P(COL, ("branch", "row"), None))
    return jax.shard_map(
        on_device, mesh=split, in_specs=in_specs, out_specs=out_specs, check_vma=False
    )
```

```python
import jax
import jax.numpy as jnp
from jax import lax
from jax.experimental import pallas as pl
from jax.experimental.pallas import tpu as pltpu
from jax.sharding import Mesh
from jax.sharding import PartitionSpec as P

HEADS = 8
PER_HEAD_WIDTH = 32
CZ = 128
PRODUCT_FEATURES = 32
COL = ("col_0", "col_1")


EPSILON = 1e-05
NEGATIVE = -1000000000.0


MESH = pl.DeviceIdType.MESH
GROUP = 16
RING = 8


def place():
    axes = [lax.axis_index(a) for a in ("branch", "row", *COL)]
    return (*axes, axes[0] * 8 + axes[1], axes[2] * 8 + axes[3])


def across(b, c):
    return (b // 8, lax.rem(b, 8), c // 8, lax.rem(c, 8))


def remote(src, dst, send, recv, to):
    return pltpu.make_async_remote_copy(
        src_ref=src, dst_ref=dst, send_sem=send, recv_sem=recv, device_id=to, device_id_type=MESH
    )


def call_exchange(kernel, out_shape, scratch, collective_id, sent, *args):
    return pl.pallas_call(
        kernel,
        out_shape=out_shape,
        in_specs=[pl.BlockSpec(memory_space=pltpu.VMEM)] * len(args),
        out_specs=jax.tree.map(lambda _: pl.BlockSpec(memory_space=pltpu.VMEM), out_shape),
        scratch_shapes=scratch,
        compiler_params=pltpu.CompilerParams(
            collective_id=collective_id, has_side_effects=True, vmem_limit_bytes=48 << 20
        ),
        cost_estimate=pl.CostEstimate(flops=0, bytes_accessed=2 * sent, transcendentals=0),
    )(*args)


class Pushes:
    def __init__(self, over, ins, outs, picks, puts, send, recv):
        b, c = place()[4:]
        self.me = b if over == "b" else c
        self.device = (lambda k: across(k, c)) if over == "b" else (lambda k: across(b, k))
        self.parts = list(zip(ins, outs, picks, puts))
        self.send, self.recv = send, recv

    def greet(self, barrier):
        def one(d, carry):
            pl.semaphore_signal(
                barrier, inc=1, device_id=self.device(lax.rem(self.me + d, GROUP)), device_id_type=MESH
            )
            return carry

        lax.fori_loop(1, GROUP, one, 0)

    def copies(self, d, sender):
        peer = lax.rem(self.me + (GROUP - d if sender else d), GROUP)
        for k, (src, dst, pick, put) in enumerate(self.parts):
            yield remote(
                pick(src, self.me if sender else peer),
                put(dst, peer if sender else self.me),
                self.send.at[k, d],
                self.recv.at[k, d],
                self.device(peer),
            )

    def start(self):
        def one(d, carry):
            for copy in self.copies(d, False):
                copy.start()
            return carry

        lax.fori_loop(1, GROUP, one, 0)
        for src, dst, pick, put in self.parts:
            put(dst, self.me)[...] = pick(src, self.me)[...]

    def finish(self):
        def one(d, carry):
            for copy in self.copies(d, True):
                copy.wait_recv()
            for copy in self.copies(d, False):
                copy.wait_send()
            return carry

        lax.fori_loop(1, GROUP, one, 0)


def exchange(over, arrays, shapes, picks, puts, collective_id):
    n = len(arrays)

    def kernel(*refs):
        pushes = Pushes(over, refs[:n], refs[n : 2 * n], picks, puts, refs[2 * n], refs[2 * n + 1])
        barrier = pltpu.get_barrier_semaphore()
        pushes.greet(barrier)
        pl.semaphore_wait(barrier, GROUP - 1)
        pushes.start()
        pushes.finish()

    out_shape = [jax.ShapeDtypeStruct(s, jnp.bfloat16) for s in shapes]
    scratch = [pltpu.SemaphoreType.DMA((n, GROUP))] * 2
    return call_exchange(kernel, out_shape, scratch, collective_id, 1 << 18, *arrays)


def ring_gather(start, whole, own, view, twins, greeted, send, recv):
    br, ro, x, z, _, c = place()
    at = lambda xx, zz: xx * RING + lax.rem(zz + RING, RING)
    right = (br, ro, x, lax.rem(z + 1, RING))
    left = (br, ro, x, lax.rem(z + RING - 1, RING))
    cross = (br, ro, 1 - x, z)
    twin = (br, ro + 1 - 2 * lax.rem(ro, 2), x, z)
    core = lax.rem(ro, 2)
    copies, handed = [], []

    def push(src, block, half, to):
        k = len(copies)
        copies.append(remote(src, view(whole, block, half, core), send.at[k], recv.at[k], to))
        copies[-1].start()
        return k

    def arrived(k, block, half):
        there = view(whole, block, half, core)
        remote(there, there, send.at[k], recv.at[k], right).wait_recv()

    def hand(block, half):
        if twins:
            handed.append((push(view(whole, block, half, core), block, half, twin), block, half))

    mine = own(start, core)
    k_cross = push(mine, c, None, cross)
    going = {(0, +1): push(mine, c, None, right), (0, -1): push(mine, c, None, left)}
    greeted()
    there = at(1 - x, z)
    arrived(k_cross, there, None)
    for way, to in ((+1, right), (-1, left)):
        going[1, way] = push(view(whole, there, None, core), there, None, to)
    hand(there, None)
    for step in (1, 2, 3):
        coming = {}
        for other in (0, 1):
            for way, to in ((+1, right), (-1, left)):
                block = at((1 - x) if other else x, z - way * step)
                arrived(going[other, way], block, None)
                half = None if step < 3 else (0 if way > 0 else 1)
                coming[other, way] = push(view(whole, block, half, core), block, half, to)
                hand(block, None)
        going = coming
    for other in (0, 1):
        for way in (+1, -1):
            block, half = at((1 - x) if other else x, z - way * 4), 0 if way > 0 else 1
            arrived(going[other, way], block, half)
            hand(block, half)
    for k, block, half in handed:
        there = view(whole, block, half, 1 - core)
        remote(there, there, send.at[k], recv.at[k], twin).wait_recv()
    for copy in copies:
        copy.wait_send()


def ring_copies(twins):
    return 19 + (17 if twins else 0)


def greet_ring(barrier, twins, cross_and_ring):
    br, ro, x, z, _, _ = place()
    to = []
    if cross_and_ring:
        to += [
            (br, ro, x, lax.rem(z + 1, RING)),
            (br, ro, x, lax.rem(z + RING - 1, RING)),
            (br, ro, 1 - x, z),
        ]
    if twins:
        to.append((br, ro + 1 - 2 * lax.rem(ro, 2), x, z))
    for device in to:
        pl.semaphore_signal(barrier, inc=1, device_id=device, device_id_type=MESH)
    return len(to)


def gather_bias_and_rows(bias, rows, mask):
    heads, some, all_ = bias.shape
    half_heads = heads // 2

    def own(ref, core):
        return ref.at[pl.ds(core * half_heads, half_heads)]

    def view(ref, block, half, core):
        first, count = core * half_heads, half_heads
        if half is not None:
            count = half_heads // 2
            first = first + half * count
        return ref.at[pl.ds(first, count), pl.ds(pl.multiple_of(block * some, some), some)]

    picks = [lambda ref, k: ref.at[k]] * 2
    puts = [
        lambda ref, k: ref.at[pl.ds(pl.multiple_of(k * some, some), some)],
        lambda ref, k: ref.at[k],
    ]

    def kernel(b_ref, r_ref, m_ref, ob_ref, or_ref, om_ref, psend, precv, rsend, rrecv):
        pushes = Pushes("c", (r_ref, m_ref), (or_ref, om_ref), picks, puts, psend, precv)
        barrier = pltpu.get_barrier_semaphore()
        pushes.greet(barrier)
        more = greet_ring(barrier, True, False)
        pl.semaphore_wait(barrier, GROUP - 1 + more)
        c = place()[5]

        def meanwhile():
            pushes.start()
            ob_ref[:, pl.ds(pl.multiple_of(c * some, some), some)] = b_ref[...]

        ring_gather(b_ref, ob_ref, own, view, True, meanwhile, rsend, rrecv)
        pushes.finish()

    out_shape = [
        jax.ShapeDtypeStruct((heads, GROUP * some, all_), jnp.bfloat16),
        jax.ShapeDtypeStruct((GROUP * some, rows.shape[2]), jnp.bfloat16),
        jax.ShapeDtypeStruct(mask.shape, jnp.bfloat16),
    ]
    scratch = [pltpu.SemaphoreType.DMA((2, GROUP))] * 2
    scratch += [pltpu.SemaphoreType.DMA((ring_copies(True),))] * 2
    return call_exchange(kernel, out_shape, scratch, 1, 4 << 20, bias, rows, mask)


def gather_factors(left, right):
    rows = left.shape[0]

    def kernel(l_ref, r_ref, ol_ref, or_ref, lsend, lrecv, rsend, rrecv):
        put = lambda ref, k: ref.at[pl.ds(pl.multiple_of(k * rows, rows), rows)]
        b, c = place()[4:]
        pushes = Pushes("b", (l_ref,), (ol_ref,), [lambda ref, k: ref], [put], lsend, lrecv)
        barrier = pltpu.get_barrier_semaphore()
        pushes.greet(barrier)

        def others(act):
            def one(d, carry):
                k = lax.rem(c + d, GROUP)

                @pl.when(jnp.logical_or(b != c, k != c))
                def _():
                    act(k)

                return carry

            lax.fori_loop(0, GROUP, one, 0)

        def senders(act):
            def one(d, carry):
                k = lax.rem(b + d, GROUP)

                @pl.when(jnp.logical_or(b != c, k != b))
                def _():
                    act(k)

                return carry

            lax.fori_loop(0, GROUP, one, 0)

        others(
            lambda k: pl.semaphore_signal(
                barrier, inc=1, device_id=across(c, k), device_id_type=MESH
            )
        )
        senders(
            lambda k: pl.semaphore_signal(
                barrier, inc=1, device_id=across(k, b), device_id_type=MESH
            )
        )
        pl.semaphore_wait(barrier, GROUP - 1 + 2 * jnp.where(b == c, GROUP - 1, GROUP))

        def copy(k):
            return remote(r_ref, put(or_ref, b), rsend.at[k], rrecv.at[b], across(c, k))

        def coming(k):
            there = put(or_ref, k)
            return remote(r_ref, there, rsend.at[k], rrecv.at[k], across(k, b))

        others(lambda k: copy(k).start())
        pushes.start()

        @pl.when(b == c)
        def _():
            put(or_ref, b)[...] = r_ref[...]

        pushes.finish()
        senders(lambda k: coming(k).wait_recv())
        others(lambda k: copy(k).wait_send())

    shape = jax.ShapeDtypeStruct((GROUP * rows, left.shape[1]), jnp.bfloat16)
    scratch = [pltpu.SemaphoreType.DMA((1, GROUP))] * 2 + [pltpu.SemaphoreType.DMA((GROUP,))] * 2
    return call_exchange(kernel, [shape, shape], scratch, 6, 1 << 20, left, right)


def norm_channels(x):
    centre = x - jnp.mean(x, axis=0, keepdims=True)
    spread = jnp.mean(centre * centre, axis=0, keepdims=True)
    return centre * lax.rsqrt(spread + EPSILON)


def pair_front(left, right, pair, mix, weights, keep):
    rows, wide = left.shape
    channels = pair.shape[0]
    lanes = 128
    per = lanes // PRODUCT_FEATURES
    some = 8
    chunk = some * PRODUCT_FEATURES
    count = wide // chunk
    groups = channels // 8

    def kernel(l_ref, r_ref, p_ref, m_ref, w_ref, k_ref, opm_ref, tl_ref, tr_ref, gate_ref):
        lane = lax.broadcasted_iota(jnp.int32, (channels, lanes), 1) // PRODUCT_FEATURES

        def one(g, carry):
            cols = pl.ds(pl.multiple_of(g * chunk, chunk), chunk)
            outer = lax.dot_general(
                l_ref[:, cols], r_ref[...], (((0,), (0,)), ((), ())), preferred_element_type=jnp.float32
            )
            outer = (outer * (1.0 / rows)).astype(jnp.bfloat16)
            stacked = jnp.concatenate(
                [
                    jnp.concatenate(
                        [
                            outer[
                                i * PRODUCT_FEATURES : (i + 1) * PRODUCT_FEATURES,
                                q * lanes : (q + 1) * lanes,
                            ]
                            for q in range(wide // lanes)
                        ],
                        axis=0,
                    )
                    for i in range(some)
                ],
                axis=1,
            )
            mixed = lax.dot_general(
                m_ref[...], stacked, (((0,), (0,)), ((), ())), preferred_element_type=jnp.float32
            )
            pieces = []
            for h in range(some // per):
                piece = jnp.zeros((channels, lanes), jnp.float32)
                for i in range(per):
                    at = (h * per + i) * lanes
                    total = None
                    for y in range(per):
                        part = mixed[y * channels : (y + 1) * channels, at : at + lanes]
                        shift = (PRODUCT_FEATURES * (i - y)) % lanes
                        part = pltpu.roll(part, shift, 1) if shift else part
                        total = part if total is None else total + part
                    piece = jnp.where(lane == i, total, piece)
                pieces.append(piece)
            opm = p_ref[:, cols].astype(jnp.float32) + jnp.concatenate(pieces, axis=1)
            opm_ref[:, cols] = opm
            normed = norm_channels(opm).astype(jnp.bfloat16)
            projected = lax.dot_general(
                w_ref[...], normed, (((0,), (0,)), ((), ())), preferred_element_type=jnp.float32
            )
            block = lambda k: projected[k * channels : (k + 1) * channels]
            here = k_ref[:, cols]
            tri_left = (here * jax.nn.sigmoid(block(0)) * block(1)).astype(jnp.bfloat16)
            tri_right = (here * jax.nn.sigmoid(block(2)) * block(3)).astype(jnp.bfloat16)
            tl_ref[:, :, cols] = tri_left.reshape(groups, 8, chunk)
            tr_ref[:, :, cols] = tri_right.reshape(groups, 8, chunk)
            gate_ref[:, cols] = jax.nn.sigmoid(block(4))
            return carry

        lax.fori_loop(0, count, one, 0)

    tokens = pair.shape[1]
    return pl.pallas_call(
        kernel,
        out_shape=[
            jax.ShapeDtypeStruct((channels, tokens), jnp.float32),
            jax.ShapeDtypeStruct((groups, 8, tokens), jnp.bfloat16),
            jax.ShapeDtypeStruct((groups, 8, tokens), jnp.bfloat16),
            jax.ShapeDtypeStruct((channels, tokens), jnp.float32),
        ],
        in_specs=[pl.BlockSpec(memory_space=pltpu.VMEM)] * 6,
        out_specs=[pl.BlockSpec(memory_space=pltpu.VMEM)] * 4,
        compiler_params=pltpu.CompilerParams(vmem_limit_bytes=40 << 20),
    )(left, right, pair, mix, weights, keep)


def triangle(tri_left, tri_right):
    groups, few, tokens = tri_left.shape
    side = int(tokens**0.5)
    at = lambda ref, k: ref.at[k]
    split = (few, 2, GROUP // 2, tokens)
    left, right = exchange("c", (tri_left, tri_right), (tri_left.shape,) * 2, [at] * 2, [at] * 2, 7)
    left = jnp.transpose(left, (1, 0, 2)).reshape(split)
    right = jnp.transpose(right, (1, 0, 2)).reshape(split)
    left, right = exchange(
        "b",
        (left, right),
        ((GROUP, *split[2:]), (GROUP, *split[1:])),
        [lambda ref, k: ref.at[k // 2, lax.rem(k, 2)], lambda ref, k: ref.at[k // 2]],
        [at] * 2,
        8,
    )
    whole = GROUP * side
    left = jnp.transpose(left.reshape(GROUP, GROUP // 2, side, side), (1, 2, 0, 3))
    right = jnp.transpose(right.reshape(GROUP, GROUP, side, side), (1, 2, 0, 3))
    mixed = lax.dot_general(
        left.reshape(whole // 2, whole),
        right.reshape(whole, whole),
        (((1,), (1,)), ((), ())),
        preferred_element_type=jnp.float32,
    ).astype(jnp.bfloat16)
    mixed = jnp.transpose(mixed.reshape(GROUP // 2, side, GROUP, side), (2, 0, 1, 3))
    (mixed,) = exchange(
        "b",
        (mixed.reshape(GROUP, GROUP // 2, tokens),),
        (split,),
        [at],
        [lambda ref, k: ref.at[k // 2, lax.rem(k, 2)]],
        9,
    )
    mixed = jnp.transpose(mixed.reshape(few, GROUP, tokens), (1, 0, 2))
    (mixed,) = exchange("c", (mixed,), ((GROUP, few, tokens),), [at], [at], 10)
    return mixed.reshape(groups * few, tokens)


def layer_normalize(tensor):
    tensor = tensor.astype(jnp.float32)
    centre = tensor - jnp.mean(tensor, axis=-1, keepdims=True)
    spread = jnp.mean(centre * centre, axis=-1, keepdims=True)
    return centre * lax.rsqrt(spread + EPSILON)


def split_blocks(normed, weights):
    projected = jnp.dot(normed, weights, preferred_element_type=jnp.float32)
    channel_count = weights.shape[0]
    queries = (projected[..., :channel_count] * PER_HEAD_WIDTH ** (-0.5)).astype(jnp.bfloat16)
    key_rows = projected[..., channel_count : 2 * channel_count].astype(jnp.bfloat16)
    value_rows = projected[..., 2 * channel_count : 3 * channel_count].astype(jnp.bfloat16)
    gating = jax.nn.sigmoid(projected[..., 3 * channel_count :])
    return (queries, key_rows, value_rows, gating)


def on_device(
    homolog_embedding,
    pair_representation,
    alignment_entry_mask,
    residue_presence_mask,
    residue_chain_index,
    row_projection_weights,
    horizontal_attend_merge,
    pair_bias_matrix,
    same_chain_bias,
    column_projection_weights,
    vertical_attend_merge,
    homolog_mlp_expand,
    homolog_mlp_contract,
    tensor_product_linear,
    outer_output_matrix,
    triangle_input_weights,
    triangle_output_matrix,
    pair_up_weight,
    pair_down_weight,
):
    device_local_rows, residue_total, channel_count = homolog_embedding.shape
    pair_cols = pair_representation.shape[1]
    row_place = lax.axis_index(COL)
    col_place = lax.axis_index(("branch", "row"))
    chain_here = lax.dynamic_slice_in_dim(
        residue_chain_index, row_place * residue_total, residue_total
    )
    chain_there = lax.dynamic_slice_in_dim(residue_chain_index, col_place * pair_cols, pair_cols)
    residue_keep = residue_presence_mask.astype(jnp.float32)
    keep_here = lax.dynamic_slice_in_dim(residue_keep, row_place * residue_total, residue_total)
    keep_there = lax.dynamic_slice_in_dim(residue_keep, col_place * pair_cols, pair_cols)
    pair_normed = layer_normalize(pair_representation).astype(jnp.bfloat16)
    same_chain = (chain_here[:, None] == chain_there[None, :]).astype(jnp.float32)
    weights = lax.dot_general(
        pair_bias_matrix,
        pair_normed.reshape(residue_total * pair_cols, -1),
        (((0,), (1,)), ((), ())),
        preferred_element_type=jnp.float32,
    )
    bias_tile = (
        weights + same_chain_bias[:, None] * same_chain.reshape(1, residue_total * pair_cols)
    ).astype(jnp.bfloat16)
    group_count = GROUP
    residue_piece = residue_total // group_count
    key_presence_mask = alignment_entry_mask.astype(jnp.bfloat16)
    row_presence = jnp.pad(key_presence_mask[:, None, :], ((0, 0), (0, 7), (0, 96)))
    col_presence = jnp.transpose(
        key_presence_mask.reshape(device_local_rows, group_count, residue_piece), (1, 2, 0)
    )
    col_presence = jnp.pad(
        col_presence, ((0, 0), (0, 8 - residue_piece), (0, 128 - device_local_rows))
    )
    bias_blocks, mask_cols = exchange(
        "b",
        (bias_tile, col_presence),
        ((GROUP, *bias_tile.shape), col_presence.shape),
        [lambda ref, k: ref, lambda ref, k: ref.at[k]],
        [lambda ref, k: ref.at[k]] * 2,
        0,
    )
    pair_bias = jnp.transpose(
        bias_blocks.reshape(GROUP, HEADS, residue_total, pair_cols), (1, 2, 0, 3)
    ).reshape(HEADS, residue_total, GROUP * pair_cols)
    mask_cols = jnp.transpose(
        mask_cols[:, :residue_piece, :device_local_rows], (1, 0, 2)
    ).reshape(residue_piece, GROUP * device_local_rows)
    row_normed_input = layer_normalize(homolog_embedding).astype(jnp.bfloat16)
    full_bias, normed_whole, mask_whole = gather_bias_and_rows(
        pair_bias, row_normed_input, row_presence
    )
    normed_whole = normed_whole[None]
    mask_whole = mask_whole[:, 0, :residue_total].reshape(1, GROUP * residue_total)
    full_bias = full_bias.astype(jnp.float32)
    few_rows, all_residues = mask_whole.shape
    queries, key_rows, value_rows, gating = split_blocks(normed_whole, row_projection_weights)
    query_heads = queries.reshape(few_rows, all_residues, HEADS, PER_HEAD_WIDTH)
    key_heads = key_rows.reshape(few_rows, all_residues, HEADS, PER_HEAD_WIDTH)
    value_heads = value_rows.reshape(few_rows, all_residues, HEADS, PER_HEAD_WIDTH)
    scores = (
        jnp.einsum("sihd,sjhd->shij", query_heads, key_heads, preferred_element_type=jnp.float32)
        + full_bias[None]
    )
    scores = jnp.where(mask_whole[:, None, None, :] > 0, scores, NEGATIVE)
    highest = jnp.max(scores, axis=-1, keepdims=True)
    powers = jnp.exp(scores - highest)
    totals = jnp.sum(powers, axis=-1)
    summed = jnp.einsum(
        "shij,sjhd->sihd",
        powers.astype(jnp.bfloat16),
        value_heads,
        preferred_element_type=jnp.float32,
    )
    attended = (summed / jnp.transpose(totals, (0, 2, 1))[..., None]).reshape(
        few_rows, all_residues, channel_count
    )
    gated_whole = (attended * gating).astype(jnp.bfloat16)
    (row_gated,) = exchange(
        "c",
        (gated_whole[0],),
        ((GROUP, residue_total, channel_count),),
        [lambda ref, k: ref.at[pl.ds(pl.multiple_of(k * residue_total, residue_total), residue_total)]],
        [lambda ref, k: ref.at[k]],
        2,
    )
    alignment_row_state = homolog_embedding.astype(jnp.float32) + jnp.dot(
        row_gated, horizontal_attend_merge, preferred_element_type=jnp.float32
    )
    column_normed_input = layer_normalize(alignment_row_state).astype(jnp.bfloat16)
    split_input = jnp.transpose(column_normed_input, (1, 0, 2))
    rows_of = lambda ref, k: ref.at[
        :, pl.ds(pl.multiple_of(k * device_local_rows, device_local_rows), device_local_rows)
    ]
    residues_of = lambda ref, k: ref.at[pl.ds(k * residue_piece, residue_piece)]
    (normed_cols,) = exchange(
        "b",
        (split_input,),
        ((residue_piece, GROUP * device_local_rows, channel_count),),
        [residues_of],
        [rows_of],
        3,
    )
    residue_count, total_rows = mask_cols.shape
    normed_flat = normed_cols
    col_queries, col_keys, col_values, col_gating = split_blocks(
        normed_flat, column_projection_weights
    )
    query_part = col_queries.reshape(residue_count, total_rows, HEADS, PER_HEAD_WIDTH)
    key_part = col_keys.reshape(residue_count, total_rows, HEADS, PER_HEAD_WIDTH)
    value_part = col_values.reshape(residue_count, total_rows, HEADS, PER_HEAD_WIDTH)
    scores = jnp.einsum("ishd,ithd->ihst", query_part, key_part, preferred_element_type=jnp.float32)
    scores = jnp.where(mask_cols[:, None, None, :] > 0, scores, NEGATIVE)
    highest = jnp.max(scores, axis=-1, keepdims=True)
    powers = jnp.exp(scores - highest)
    totals = jnp.sum(powers, axis=-1)
    summed = jnp.einsum(
        "ihst,ithd->ihsd",
        powers.astype(jnp.bfloat16),
        value_part,
        preferred_element_type=jnp.float32,
    )
    attended = jnp.transpose(summed / totals[..., None], (0, 2, 1, 3)).reshape(
        residue_count, total_rows, channel_count
    )
    gated = (attended * col_gating).astype(jnp.bfloat16)
    (returned,) = exchange(
        "b",
        (gated,),
        ((residue_total, device_local_rows, channel_count),),
        [rows_of],
        [residues_of],
        4,
    )
    column_gated_output = jnp.transpose(returned, (1, 0, 2))
    alignment_column_state = alignment_row_state + jnp.dot(
        column_gated_output, vertical_attend_merge, preferred_element_type=jnp.float32
    )
    transition_normed_input = layer_normalize(alignment_column_state).astype(jnp.bfloat16)
    alignment_hidden_units = jax.nn.relu(
        jnp.dot(transition_normed_input, homolog_mlp_expand, preferred_element_type=jnp.float32)
    ).astype(jnp.bfloat16)
    alignment_final_state = alignment_column_state + jnp.dot(
        alignment_hidden_units, homolog_mlp_contract, preferred_element_type=jnp.float32
    )
    outer_normed_input = layer_normalize(alignment_final_state).astype(jnp.bfloat16)
    factors = (
        jnp.dot(outer_normed_input, tensor_product_linear, preferred_element_type=jnp.float32)
        * alignment_entry_mask.astype(jnp.float32)[:, :, None]
    )
    left_factor = (
        factors[..., :PRODUCT_FEATURES]
        .astype(jnp.bfloat16)
        .reshape(device_local_rows, residue_total * PRODUCT_FEATURES)
    )
    right_factor = jnp.transpose(
        factors[..., PRODUCT_FEATURES:].astype(jnp.bfloat16), (0, 2, 1)
    ).reshape(device_local_rows, residue_total * PRODUCT_FEATURES)
    left_all, right_rows = gather_factors(left_factor, right_factor)
    tokens = residue_total * pair_cols
    pair_first = jnp.transpose(pair_representation.reshape(tokens, CZ))
    mix = jnp.transpose(
        outer_output_matrix.reshape(PRODUCT_FEATURES, PRODUCT_FEATURES // 4, 4 * CZ), (1, 0, 2)
    ).reshape(PRODUCT_FEATURES * PRODUCT_FEATURES // 4, 4 * CZ)
    pair_keep = (keep_here[:, None] * keep_there[None, :]).reshape(1, tokens)
    pair_opm, tri_left, tri_right, tri_gate = pair_front(
        left_all, right_rows, pair_first, mix, triangle_input_weights, pair_keep
    )
    tri_mixed = triangle(tri_left, tri_right).astype(jnp.float32)
    contract = (((0,), (0,)), ((), ()))
    mixed_normed = norm_channels(tri_mixed).astype(jnp.bfloat16)
    pair_tri = pair_opm + tri_gate * lax.dot_general(
        triangle_output_matrix, mixed_normed, contract, preferred_element_type=jnp.float32
    )
    pair_trans_in = norm_channels(pair_tri).astype(jnp.bfloat16)
    pair_hidden = jax.nn.relu(
        lax.dot_general(pair_up_weight, pair_trans_in, contract, preferred_element_type=jnp.float32)
    ).astype(jnp.bfloat16)
    updated_pair_state = (
        jnp.transpose(pair_tri)
        + lax.dot_general(pair_hidden, pair_down_weight, contract, preferred_element_type=jnp.float32)
    ).astype(jnp.bfloat16)
    updated_pair_state = updated_pair_state.reshape(residue_total, pair_cols, CZ)
    return (alignment_final_state.astype(jnp.bfloat16), updated_pair_state)


def solution(mesh):
    split = Mesh(
        mesh.devices.reshape(mesh.shape["branch"], mesh.shape["row"], 2, 8),
        ("branch", "row", "col_0", "col_1"),
    )
    in_specs = (
        P(("branch", "row"), COL, None),
        P(COL, ("branch", "row"), None),
        P(("branch", "row"), COL),
        P(),
        P(),
        P(),
        P(),
        P(),
        P(),
        P(),
        P(),
        P(),
        P(),
        P(),
        P(),
        P(),
        P(),
        P(),
        P(),
    )
    out_specs = (P(("branch", "row"), COL, None), P(COL, ("branch", "row"), None))
    return jax.shard_map(
        on_device, mesh=split, in_specs=in_specs, out_specs=out_specs, check_vma=False
    )
```

```python
import jax
import jax.numpy as jnp
from jax import lax
from jax.experimental import pallas as pl
from jax.experimental.pallas import tpu as pltpu
from jax.sharding import Mesh
from jax.sharding import PartitionSpec as P

HEADS = 8
PER_HEAD_WIDTH = 32
CZ = 128
PRODUCT_FEATURES = 32
COL = ("col_0", "col_1")


EPSILON = 1e-05
NEGATIVE = -1000000000.0


MESH = pl.DeviceIdType.MESH
GROUP = 16
RING = 8
SIZES = {"b": 16, "c": 16, "z": 8}


def place():
    axes = [lax.axis_index(a) for a in ("branch", "row", *COL)]
    return (*axes, axes[0] * 8 + axes[1], axes[2] * 8 + axes[3])


def across(b, c):
    return (b // 8, lax.rem(b, 8), c // 8, lax.rem(c, 8))


def remote(src, dst, send, recv, to):
    return pltpu.make_async_remote_copy(
        src_ref=src, dst_ref=dst, send_sem=send, recv_sem=recv, device_id=to, device_id_type=MESH
    )


def call_exchange(kernel, out_shape, scratch, collective_id, sent, *args):
    return pl.pallas_call(
        kernel,
        out_shape=out_shape,
        in_specs=[pl.BlockSpec(memory_space=pltpu.VMEM)] * len(args),
        out_specs=jax.tree.map(lambda _: pl.BlockSpec(memory_space=pltpu.VMEM), out_shape),
        scratch_shapes=scratch,
        compiler_params=pltpu.CompilerParams(
            collective_id=collective_id, has_side_effects=True, vmem_limit_bytes=48 << 20
        ),
        cost_estimate=pl.CostEstimate(flops=0, bytes_accessed=2 * sent, transcendentals=0),
    )(*args)


class Pushes:
    def __init__(self, over, ins, outs, picks, puts, send, recv):
        br, ro, x, z, b, c = place()
        self.count = SIZES[over]
        self.me, self.device = {
            "b": (b, lambda k: across(k, c)),
            "c": (c, lambda k: across(b, k)),
            "z": (z, lambda k: (br, ro, x, k)),
        }[over]
        self.parts = list(zip(ins, outs, picks, puts))
        self.send, self.recv = send, recv

    def greet(self, barrier):
        def one(d, carry):
            to = self.device(lax.rem(self.me + d, self.count))
            pl.semaphore_signal(barrier, inc=1, device_id=to, device_id_type=MESH)
            return carry

        lax.fori_loop(1, self.count, one, 0)

    def sender(self, d):
        return lax.rem(self.me + (self.count - d), self.count)

    def copies(self, d, coming):
        peer = self.sender(d) if coming else lax.rem(self.me + d, self.count)
        for k, (src, dst, pick, put) in enumerate(self.parts):
            yield remote(
                pick(src, self.me if coming else peer),
                put(dst, peer if coming else self.me),
                self.send.at[k, d],
                self.recv.at[k, d],
                self.device(peer),
            )

    def start(self):
        def one(d, carry):
            for copy in self.copies(d, False):
                copy.start()
            return carry

        lax.fori_loop(1, self.count, one, 0)
        for src, dst, pick, put in self.parts:
            put(dst, self.me)[...] = pick(src, self.me)[...]

    def arrive(self, d):
        for copy in self.copies(d, True):
            copy.wait_recv()

    def sent(self, d):
        for copy in self.copies(d, False):
            copy.wait_send()

    def finish(self):
        def one(d, carry):
            self.arrive(d)
            self.sent(d)
            return carry

        lax.fori_loop(1, self.count, one, 0)


def exchange(over, arrays, shapes, picks, puts, collective_id):
    n = len(arrays)

    def kernel(*refs):
        pushes = Pushes(over, refs[:n], refs[n : 2 * n], picks, puts, refs[2 * n], refs[2 * n + 1])
        barrier = pltpu.get_barrier_semaphore()
        pushes.greet(barrier)
        pl.semaphore_wait(barrier, SIZES[over] - 1)
        pushes.start()
        pushes.finish()

    out_shape = [jax.ShapeDtypeStruct(s, jnp.bfloat16) for s in shapes]
    scratch = [pltpu.SemaphoreType.DMA((n, GROUP))] * 2
    return call_exchange(kernel, out_shape, scratch, collective_id, 1 << 18, *arrays)


def crosswise():
    br, ro, x, z = place()[:4]
    return (br, ro, 1 - x, z)


def gather_bias_and_rows(bias, rows):
    heads, some, all_ = bias.shape
    carried = heads // 2
    pair, _, tall, channels = rows.shape
    n_copies = 32

    def kernel(b_ref, r_ref, ob_ref, or_ref, psend, precv, xsend, xrecv, rsend, rrecv):
        br, ro, x, z, _, c = place()
        core = lax.rem(ro, 2)
        right = (br, ro, x, lax.rem(z + 1, RING))
        left = (br, ro, x, lax.rem(z + RING - 1, RING))
        twin = (br, ro + 1 - 2 * core, x, z)
        cross = crosswise()
        put = lambda ref, k: ref.at[:, x * RING + k]
        pushes = Pushes("z", (r_ref,), (or_ref,), [lambda ref, k: ref.at[:, k]], [put], psend, precv)
        barrier = pltpu.get_barrier_semaphore()
        pushes.greet(barrier)
        for device in (twin, cross):
            pl.semaphore_signal(barrier, inc=1, device_id=device, device_id_type=MESH)
        pl.semaphore_wait(barrier, RING - 1 + 2)

        def view(block, half, mine):
            first, count = mine * carried, carried
            if half is not None:
                count = carried // 2
                first = first + half * count
            rows_at = pl.multiple_of(lax.rem(block + RING, RING) * some, some)
            return ob_ref.at[pl.ds(first, count), pl.ds(rows_at, some)]

        copies, handed = [], []

        def push(src, block, half, to):
            k = len(copies)
            copies.append(remote(src, view(block, half, core), rsend.at[k], rrecv.at[k], to))
            copies[-1].start()
            return k

        def arrived(k, block, half):
            there = view(block, half, core)
            remote(there, there, rsend.at[k], rrecv.at[k], right).wait_recv()

        def hand(block, half):
            handed.append((push(view(block, half, core), block, half, twin), block, half))

        def over(d, coming):
            k = pushes.sender(d)
            place_at = (1 - x if coming else x) * RING + k
            there = or_ref.at[:, place_at]
            return remote(there, there, xsend.at[d], xrecv.at[d], cross)

        mine = b_ref.at[pl.ds(core * carried, carried)]
        pushes.start()
        going = {+1: push(mine, z, None, right), -1: push(mine, z, None, left)}
        first = remote(r_ref.at[:, z], or_ref.at[:, c], xsend.at[0], xrecv.at[0], cross)
        first.start()
        ob_ref[:, pl.ds(pl.multiple_of(z * some, some), some)] = b_ref[...]
        for step in (1, 2, 3):
            coming = {}
            for way, to in ((+1, right), (-1, left)):
                block = z - way * step
                arrived(going[way], block, None)
                half = None if step < 3 else (0 if way > 0 else 1)
                coming[way] = push(view(block, half, core), block, half, to)
                hand(block, None)
            going = coming
            for d in (step, RING - step):
                pushes.arrive(d)
                over(d, False).start()
        pushes.arrive(4)
        over(4, False).start()
        for way in (+1, -1):
            half = 0 if way > 0 else 1
            arrived(going[way], z - way * 4, half)
            hand(z - way * 4, half)
        for k, block, half in handed:
            there = view(block, half, 1 - core)
            remote(there, there, rsend.at[k], rrecv.at[k], twin).wait_recv()
        for d in range(RING):
            over(d, True).wait_recv()
        for copy in copies:
            copy.wait_send()
        first.wait_send()
        for d in range(1, RING):
            pushes.sent(d)
            over(d, False).wait_send()

    out_shape = [
        jax.ShapeDtypeStruct((heads, RING * some, all_), jnp.bfloat16),
        jax.ShapeDtypeStruct((pair, GROUP, tall, channels), jnp.bfloat16),
    ]
    scratch = [pltpu.SemaphoreType.DMA((1, RING))] * 2
    scratch += [pltpu.SemaphoreType.DMA((RING,))] * 2
    scratch += [pltpu.SemaphoreType.DMA((n_copies,))] * 2
    return call_exchange(kernel, out_shape, scratch, 1, 2 << 20, bias, rows)


def compute(kernel, out_shape, *args, scratch=(), limit=40):
    return pl.pallas_call(
        kernel,
        out_shape=out_shape,
        in_specs=[pl.BlockSpec(memory_space=pltpu.VMEM)] * len(args),
        out_specs=jax.tree.map(lambda _: pl.BlockSpec(memory_space=pltpu.VMEM), out_shape),
        scratch_shapes=list(scratch),
        compiler_params=pltpu.CompilerParams(vmem_limit_bytes=limit << 20),
    )(*args)


def heads_attend(queries, keys, values, present, bias_of):
    lanes = 128
    per = lanes // PER_HEAD_WIDTH
    lane = lax.broadcasted_iota(jnp.int32, (1, lanes), 1) // PER_HEAD_WIDTH
    blocks = []
    for block in range(HEADS // per):
        cols = slice(block * lanes, (block + 1) * lanes)
        total = jnp.zeros((queries.shape[0], lanes), jnp.float32)
        for h in range(per):
            here = (lane == h).astype(jnp.float32)
            query = queries[:, cols] * here.astype(jnp.bfloat16)
            scores = lax.dot_general(
                query, keys[:, cols], (((1,), (1,)), ((), ())), preferred_element_type=jnp.float32
            )
            if bias_of is not None:
                scores = scores + bias_of(block * per + h).astype(jnp.float32)
            scores = jnp.where(present, scores, NEGATIVE)
            powers = jnp.exp(scores - jnp.max(scores, axis=-1, keepdims=True))
            totals = jnp.sum(powers, axis=-1, keepdims=True)
            summed = jnp.dot(
                powers.astype(jnp.bfloat16), values[:, cols], preferred_element_type=jnp.float32
            )
            total = total + (summed / totals) * here
        blocks.append(total)
    return jnp.concatenate(blocks, axis=1)


def row_attention(rows, bias, weights):
    pair, blocks, tall, channels = rows.shape
    some = tall - 8
    residues = blocks * some
    step = 128

    def kernel(r_ref, b_ref, w_ref, o_ref, q_ref, g_ref):
        x = place()[2]
        for r in range(pair):
            whole = r_ref[r, :, :some].reshape(residues, channels)
            keys_values = jnp.dot(
                whole, w_ref[:, channels : 3 * channels], preferred_element_type=jnp.float32
            ).astype(jnp.bfloat16)
            keys, values = keys_values[:, :channels], keys_values[:, channels:]
            own = r_ref[r, pl.ds(x * RING, RING), :some].reshape(residues // 2, channels)
            q = jnp.dot(own, w_ref[:, :channels], preferred_element_type=jnp.float32)
            q_ref[...] = (q * PER_HEAD_WIDTH ** (-0.5)).astype(jnp.bfloat16)
            gate = jnp.dot(own, w_ref[:, 3 * channels :], preferred_element_type=jnp.float32)
            g_ref[...] = jax.nn.sigmoid(gate)
            present = []
            for half in range(2):
                total = jnp.zeros((8, channels), jnp.float32)
                for k in range(RING):
                    total = total + r_ref[r, half * RING + k, some:].astype(jnp.float32)
                present.append(total[:1])
            present = jnp.concatenate(present, axis=1) > 0

            def one(t, carry):
                at = pl.ds(pl.multiple_of(t * step, step), step)
                attended = heads_attend(
                    q_ref[at], keys, values, present, lambda h: b_ref[h, at, :]
                )
                gated = (attended * g_ref[at]).astype(jnp.bfloat16)
                o_ref[r, pl.ds(t * (step // some), step // some)] = gated.reshape(
                    step // some, some, channels
                )
                return carry

            lax.fori_loop(0, residues // 2 // step, one, 0)

    out_shape = jax.ShapeDtypeStruct((pair, RING, some, channels), jnp.bfloat16)
    scratch = [
        pltpu.VMEM((residues // 2, channels), jnp.bfloat16),
        pltpu.VMEM((residues // 2, channels), jnp.float32),
    ]
    return compute(kernel, out_shape, rows, bias, weights, scratch=scratch)


def column_attention(cols, presence, weights):
    few, rows, channels = cols.shape
    step = 128

    def kernel(c_ref, p_ref, w_ref, o_ref, q_ref, g_ref):
        halves = []
        for half in range(2):
            total = jnp.zeros((8, 128), jnp.float32)
            for k in range(RING):
                total = total + p_ref[half * RING + k].astype(jnp.float32)
            halves.append(total)
        there = jnp.concatenate(halves, axis=1)
        for r in range(few):
            whole = c_ref[r]
            projected = jnp.dot(whole, w_ref[...], preferred_element_type=jnp.float32)
            q_ref[...] = (projected[:, :channels] * PER_HEAD_WIDTH ** (-0.5)).astype(jnp.bfloat16)
            keys = projected[:, channels : 2 * channels].astype(jnp.bfloat16)
            values = projected[:, 2 * channels : 3 * channels].astype(jnp.bfloat16)
            g_ref[...] = jax.nn.sigmoid(projected[:, 3 * channels :])
            present = there[r : r + 1] > 0

            def one(t, carry):
                at = pl.ds(pl.multiple_of(t * step, step), step)
                attended = heads_attend(q_ref[at], keys, values, present, None)
                o_ref[r, at] = (attended * g_ref[at]).astype(jnp.bfloat16)
                return carry

            lax.fori_loop(0, rows // step, one, 0)

    out_shape = jax.ShapeDtypeStruct((few, rows, channels), jnp.bfloat16)
    scratch = [pltpu.VMEM((rows, channels), jnp.bfloat16), pltpu.VMEM((rows, channels), jnp.float32)]
    return compute(kernel, out_shape, cols, presence, weights, scratch=scratch)


def gather_factors(left, right):
    rows = left.shape[0]

    def kernel(l_ref, r_ref, ol_ref, or_ref, lsend, lrecv, rsend, rrecv):
        put = lambda ref, k: ref.at[pl.ds(pl.multiple_of(k * rows, rows), rows)]
        b, c = place()[4:]
        pushes = Pushes("b", (l_ref,), (ol_ref,), [lambda ref, k: ref], [put], lsend, lrecv)
        barrier = pltpu.get_barrier_semaphore()
        pushes.greet(barrier)

        def others(act):
            def one(d, carry):
                k = lax.rem(c + d, GROUP)

                @pl.when(jnp.logical_or(b != c, k != c))
                def _():
                    act(k)

                return carry

            lax.fori_loop(0, GROUP, one, 0)

        def senders(act):
            def one(d, carry):
                k = lax.rem(b + d, GROUP)

                @pl.when(jnp.logical_or(b != c, k != b))
                def _():
                    act(k)

                return carry

            lax.fori_loop(0, GROUP, one, 0)

        others(
            lambda k: pl.semaphore_signal(
                barrier, inc=1, device_id=across(c, k), device_id_type=MESH
            )
        )
        senders(
            lambda k: pl.semaphore_signal(
                barrier, inc=1, device_id=across(k, b), device_id_type=MESH
            )
        )
        pl.semaphore_wait(barrier, GROUP - 1 + 2 * jnp.where(b == c, GROUP - 1, GROUP))

        def copy(k):
            return remote(r_ref, put(or_ref, b), rsend.at[k], rrecv.at[b], across(c, k))

        def coming(k):
            there = put(or_ref, k)
            return remote(r_ref, there, rsend.at[k], rrecv.at[k], across(k, b))

        others(lambda k: copy(k).start())
        pushes.start()

        @pl.when(b == c)
        def _():
            put(or_ref, b)[...] = r_ref[...]

        pushes.finish()
        senders(lambda k: coming(k).wait_recv())
        others(lambda k: copy(k).wait_send())

    shape = jax.ShapeDtypeStruct((GROUP * rows, left.shape[1]), jnp.bfloat16)
    scratch = [pltpu.SemaphoreType.DMA((1, GROUP))] * 2 + [pltpu.SemaphoreType.DMA((GROUP,))] * 2
    return call_exchange(kernel, [shape, shape], scratch, 6, 1 << 20, left, right)


def norm_channels(x):
    centre = x - jnp.mean(x, axis=0, keepdims=True)
    spread = jnp.mean(centre * centre, axis=0, keepdims=True)
    return centre * lax.rsqrt(spread + EPSILON)


def pair_front(left, right, pair, mix, weights, keep):
    rows, wide = left.shape
    channels = pair.shape[0]
    lanes = 128
    per = lanes // PRODUCT_FEATURES
    some = 8
    chunk = some * PRODUCT_FEATURES
    count = wide // chunk
    groups = RING
    deep = channels // groups

    def kernel(l_ref, r_ref, p_ref, m_ref, w_ref, k_ref, opm_ref, tl_ref, tr_ref, gate_ref):
        lane = lax.broadcasted_iota(jnp.int32, (channels, lanes), 1) // PRODUCT_FEATURES

        def one(g, carry):
            cols = pl.ds(pl.multiple_of(g * chunk, chunk), chunk)
            outer = lax.dot_general(
                l_ref[:, cols], r_ref[...], (((0,), (0,)), ((), ())), preferred_element_type=jnp.float32
            )
            outer = (outer * (1.0 / rows)).astype(jnp.bfloat16)
            stacked = jnp.concatenate(
                [
                    jnp.concatenate(
                        [
                            outer[
                                i * PRODUCT_FEATURES : (i + 1) * PRODUCT_FEATURES,
                                q * lanes : (q + 1) * lanes,
                            ]
                            for q in range(wide // lanes)
                        ],
                        axis=0,
                    )
                    for i in range(some)
                ],
                axis=1,
            )
            mixed = lax.dot_general(
                m_ref[...], stacked, (((0,), (0,)), ((), ())), preferred_element_type=jnp.float32
            )
            pieces = []
            for h in range(some // per):
                piece = jnp.zeros((channels, lanes), jnp.float32)
                for i in range(per):
                    at = (h * per + i) * lanes
                    total = None
                    for y in range(per):
                        part = mixed[y * channels : (y + 1) * channels, at : at + lanes]
                        shift = (PRODUCT_FEATURES * (i - y)) % lanes
                        part = pltpu.roll(part, shift, 1) if shift else part
                        total = part if total is None else total + part
                    piece = jnp.where(lane == i, total, piece)
                pieces.append(piece)
            opm = p_ref[:, cols].astype(jnp.float32) + jnp.concatenate(pieces, axis=1)
            opm_ref[:, cols] = opm
            normed = norm_channels(opm).astype(jnp.bfloat16)
            projected = lax.dot_general(
                w_ref[...], normed, (((0,), (0,)), ((), ())), preferred_element_type=jnp.float32
            )
            block = lambda k: projected[k * channels : (k + 1) * channels]
            here = k_ref[:, cols]
            tri_left = (here * jax.nn.sigmoid(block(0)) * block(1)).astype(jnp.bfloat16)
            tri_right = (here * jax.nn.sigmoid(block(2)) * block(3)).astype(jnp.bfloat16)
            tl_ref[:, :, cols] = tri_left.reshape(groups, deep, chunk)
            tr_ref[:, :, cols] = tri_right.reshape(groups, deep, chunk)
            gate_ref[:, cols] = jax.nn.sigmoid(block(4))
            return carry

        lax.fori_loop(0, count, one, 0)

    tokens = pair.shape[1]
    return pl.pallas_call(
        kernel,
        out_shape=[
            jax.ShapeDtypeStruct((channels, tokens), jnp.float32),
            jax.ShapeDtypeStruct((groups, deep, tokens), jnp.bfloat16),
            jax.ShapeDtypeStruct((groups, deep, tokens), jnp.bfloat16),
            jax.ShapeDtypeStruct((channels, tokens), jnp.float32),
        ],
        in_specs=[pl.BlockSpec(memory_space=pltpu.VMEM)] * 6,
        out_specs=[pl.BlockSpec(memory_space=pltpu.VMEM)] * 4,
        compiler_params=pltpu.CompilerParams(vmem_limit_bytes=40 << 20),
    )(left, right, pair, mix, weights, keep)


def exchange_channels(left, right):
    channels, few, tokens = left.shape

    def kernel(l_ref, r_ref, ol_ref, or_ref, send, recv, xsend, xrecv):
        x = place()[2]
        cross = crosswise()
        at = lambda ref, k: ref.at[k]
        here = lambda ref, k: ref.at[x, k]
        pushes = Pushes("b", (l_ref, r_ref), (ol_ref, or_ref), [at] * 2, [at, here], send, recv)
        barrier = pltpu.get_barrier_semaphore()
        pushes.greet(barrier)
        pl.semaphore_signal(barrier, inc=1, device_id=cross, device_id_type=MESH)
        pl.semaphore_wait(barrier, GROUP)

        def over(d, coming):
            there = or_ref.at[1 - x if coming else x, pushes.sender(d)]
            return remote(there, there, xsend.at[d], xrecv.at[d], cross)

        pushes.start()
        me = pushes.me
        first = remote(r_ref.at[me], or_ref.at[x, me], xsend.at[0], xrecv.at[0], cross)
        first.start()

        def one(d, carry):
            pushes.arrive(d)
            over(d, False).start()
            return carry

        lax.fori_loop(1, GROUP, one, 0)

        def last(d, carry):
            pushes.sent(d)
            over(d, True).wait_recv()
            over(d, False).wait_send()
            return carry

        lax.fori_loop(1, GROUP, last, 0)
        over(0, True).wait_recv()
        first.wait_send()

    out_shape = [
        jax.ShapeDtypeStruct((GROUP, few, tokens), jnp.bfloat16),
        jax.ShapeDtypeStruct((2, GROUP, few, tokens), jnp.bfloat16),
    ]
    scratch = [pltpu.SemaphoreType.DMA((2, GROUP))] * 2 + [pltpu.SemaphoreType.DMA((GROUP,))] * 2
    return call_exchange(kernel, out_shape, scratch, 8, 1 << 20, left, right)


def multiply_channel(left, right):
    blocks, few, tokens = left.shape
    side = int(tokens**0.5)
    lanes = 128
    per = lanes // side
    wide = blocks * side
    tall = few * side

    def kernel(l_ref, r_ref, o_ref, a_ref, b_ref, y_ref):
        lane = lax.broadcasted_iota(jnp.int32, (few, lanes), 1) // side

        def unfold(block, put):
            def one(v, carry):
                x = block(pl.ds(pl.multiple_of(v * lanes, lanes), lanes)).astype(jnp.float32)
                x = x.reshape(blocks * few, lanes)
                turned = [x] + [pltpu.roll(x, side * s, 1) for s in range(1, per)]
                for n in range(per):
                    line = []
                    for q in range(blocks // per):
                        piece = jnp.zeros((few, lanes), jnp.float32)
                        for m in range(per):
                            k = (q * per + m) * few
                            piece = jnp.where(lane == m, turned[(m - n) % per][k : k + few], piece)
                        line.append(piece)
                    put(v * per + n, jnp.concatenate(line, axis=1))
                return carry

            lax.fori_loop(0, side // per, one, 0)

        def put_left(i, line):
            a_ref[pl.ds(pl.multiple_of(i * few, few), few)] = line

        unfold(lambda cols: l_ref[:, :, cols], put_left)
        for h in range(2):

            def put_right(j, line):
                b_ref[h, pl.ds(pl.multiple_of(j * few, few), few)] = line

            unfold(lambda cols: r_ref[h, :, :, cols], put_right)
        a = a_ref[...].astype(jnp.bfloat16)
        to = lax.broadcasted_iota(jnp.int32, (tall, tall), 0)
        of = lax.broadcasted_iota(jnp.int32, (tall, tall), 1)
        order = (of == lax.rem(to, side) * few + to // side).astype(jnp.float32).astype(jnp.bfloat16)
        for h in range(2):
            b = b_ref[h].astype(jnp.bfloat16)
            b = jnp.dot(order, b, preferred_element_type=jnp.float32).astype(jnp.bfloat16)
            y_ref[:, h * tall : (h + 1) * tall] = lax.dot_general(
                a, b, (((1,), (1,)), ((), ())), preferred_element_type=jnp.float32
            )

        def fold(v, carry):
            cols = pl.ds(pl.multiple_of(v * lanes, lanes), lanes)
            y = y_ref[pl.ds(pl.multiple_of(v * per * few, per * few), per * few)]
            for q in range(wide // lanes):
                x = y[:, q * lanes : (q + 1) * lanes]
                turned = [x] + [pltpu.roll(x, side * s, 1) for s in range(1, per)]
                for m in range(per):
                    piece = jnp.zeros((few, lanes), jnp.float32)
                    for n in range(per):
                        piece = jnp.where(
                            lane == n, turned[(n - m) % per][n * few : (n + 1) * few], piece
                        )
                    o_ref[q * per + m, :, cols] = piece.astype(jnp.bfloat16)
            return carry

        lax.fori_loop(0, side // per, fold, 0)

    out_shape = jax.ShapeDtypeStruct((blocks, few, tokens), jnp.bfloat16)
    scratch = [
        pltpu.VMEM((tall, wide), jnp.float32),
        pltpu.VMEM((2, tall, wide), jnp.float32),
        pltpu.VMEM((tall, wide), jnp.float32),
    ]
    return compute(kernel, out_shape, left, right, scratch=scratch)


def triangle(tri_left, tri_right):
    groups, deep, tokens = tri_left.shape
    at = lambda ref, k: ref.at[k]
    left, right = exchange("z", (tri_left, tri_right), (tri_left.shape,) * 2, [at] * 2, [at] * 2, 7)
    left, right = exchange_channels(jnp.transpose(left, (1, 0, 2)), jnp.transpose(right, (1, 0, 2)))
    mixed = multiply_channel(left, right)
    (mixed,) = exchange("b", (mixed,), ((deep, groups, tokens),), [at], [at], 9)
    mixed = jnp.transpose(mixed, (1, 0, 2))
    (mixed,) = exchange("z", (mixed,), ((groups, deep, tokens),), [at], [at], 10)
    return mixed.reshape(groups * deep, tokens)


def layer_normalize(tensor):
    tensor = tensor.astype(jnp.float32)
    centre = tensor - jnp.mean(tensor, axis=-1, keepdims=True)
    spread = jnp.mean(centre * centre, axis=-1, keepdims=True)
    return centre * lax.rsqrt(spread + EPSILON)


def on_device(
    homolog_embedding,
    pair_representation,
    alignment_entry_mask,
    residue_presence_mask,
    residue_chain_index,
    row_projection_weights,
    horizontal_attend_merge,
    pair_bias_matrix,
    same_chain_bias,
    column_projection_weights,
    vertical_attend_merge,
    homolog_mlp_expand,
    homolog_mlp_contract,
    tensor_product_linear,
    outer_output_matrix,
    triangle_input_weights,
    triangle_output_matrix,
    pair_up_weight,
    pair_down_weight,
):
    device_local_rows, residue_total, channel_count = homolog_embedding.shape
    pair_cols = pair_representation.shape[1]
    row_place = lax.axis_index(COL)
    col_place = lax.axis_index(("branch", "row"))
    chain_here = lax.dynamic_slice_in_dim(
        residue_chain_index, row_place * residue_total, residue_total
    )
    chain_there = lax.dynamic_slice_in_dim(residue_chain_index, col_place * pair_cols, pair_cols)
    residue_keep = residue_presence_mask.astype(jnp.float32)
    keep_here = lax.dynamic_slice_in_dim(residue_keep, row_place * residue_total, residue_total)
    keep_there = lax.dynamic_slice_in_dim(residue_keep, col_place * pair_cols, pair_cols)
    pair_normed = layer_normalize(pair_representation).astype(jnp.bfloat16)
    same_chain = (chain_here[:, None] == chain_there[None, :]).astype(jnp.float32)
    weights = lax.dot_general(
        pair_bias_matrix,
        pair_normed.reshape(residue_total * pair_cols, -1),
        (((0,), (1,)), ((), ())),
        preferred_element_type=jnp.float32,
    )
    bias_tile = (
        weights + same_chain_bias[:, None] * same_chain.reshape(1, residue_total * pair_cols)
    ).astype(jnp.bfloat16)
    group_count = GROUP
    residue_piece = residue_total // group_count
    key_presence_mask = alignment_entry_mask.astype(jnp.bfloat16)
    ring_place = lax.axis_index("col_1")
    row_presence = jnp.tile(key_presence_mask, (1, channel_count // residue_total))
    row_lane = lax.broadcasted_iota(jnp.int32, row_presence.shape, 1) // residue_total
    row_presence = jnp.where(row_lane == ring_place, row_presence, 0)
    row_presence = jnp.pad(row_presence[:, None, :], ((0, 0), (0, 7), (0, 0)))
    col_presence = jnp.transpose(
        key_presence_mask.reshape(device_local_rows, group_count, residue_piece), (1, 2, 0)
    )
    col_presence = jnp.tile(col_presence, (1, 1, 128 // device_local_rows))
    col_lane = lax.broadcasted_iota(jnp.int32, col_presence.shape, 2) // device_local_rows
    col_presence = jnp.where(col_lane == lax.rem(col_place, 8), col_presence, 0)
    col_presence = jnp.pad(col_presence, ((0, 0), (0, 8 - residue_piece), (0, 0)))
    bias_blocks, mask_cols = exchange(
        "b",
        (bias_tile, col_presence),
        ((GROUP, *bias_tile.shape), col_presence.shape),
        [lambda ref, k: ref, lambda ref, k: ref.at[k]],
        [lambda ref, k: ref.at[k]] * 2,
        0,
    )
    pair_bias = jnp.transpose(
        bias_blocks.reshape(GROUP, HEADS, residue_total, pair_cols), (1, 2, 0, 3)
    ).reshape(HEADS, residue_total, GROUP * pair_cols)
    row_normed_input = layer_normalize(homolog_embedding).astype(jnp.bfloat16)
    rows_sent = jnp.concatenate([row_normed_input, row_presence], axis=1)
    full_bias, rows_whole = gather_bias_and_rows(
        pair_bias, rows_sent.reshape(2, RING, *rows_sent.shape[1:])
    )
    gated_whole = row_attention(rows_whole, full_bias, row_projection_weights)
    along = lambda ref, k: ref.at[:, k]
    (row_gated,) = exchange("z", (gated_whole,), (gated_whole.shape,), [along], [along], 2)
    row_gated = row_gated.reshape(device_local_rows, residue_total, channel_count)
    alignment_row_state = homolog_embedding.astype(jnp.float32) + jnp.dot(
        row_gated, horizontal_attend_merge, preferred_element_type=jnp.float32
    )
    column_normed_input = layer_normalize(alignment_row_state).astype(jnp.bfloat16)
    split_input = jnp.transpose(column_normed_input, (1, 0, 2))
    rows_of = lambda ref, k: ref.at[
        :, pl.ds(pl.multiple_of(k * device_local_rows, device_local_rows), device_local_rows)
    ]
    residues_of = lambda ref, k: ref.at[pl.ds(k * residue_piece, residue_piece)]
    (normed_cols,) = exchange(
        "b",
        (split_input,),
        ((residue_piece, GROUP * device_local_rows, channel_count),),
        [residues_of],
        [rows_of],
        3,
    )
    gated = column_attention(normed_cols, mask_cols, column_projection_weights)
    (returned,) = exchange(
        "b",
        (gated,),
        ((residue_total, device_local_rows, channel_count),),
        [rows_of],
        [residues_of],
        4,
    )
    column_gated_output = jnp.transpose(returned, (1, 0, 2))
    alignment_column_state = alignment_row_state + jnp.dot(
        column_gated_output, vertical_attend_merge, preferred_element_type=jnp.float32
    )
    transition_normed_input = layer_normalize(alignment_column_state).astype(jnp.bfloat16)
    alignment_hidden_units = jax.nn.relu(
        jnp.dot(transition_normed_input, homolog_mlp_expand, preferred_element_type=jnp.float32)
    ).astype(jnp.bfloat16)
    alignment_final_state = alignment_column_state + jnp.dot(
        alignment_hidden_units, homolog_mlp_contract, preferred_element_type=jnp.float32
    )
    outer_normed_input = layer_normalize(alignment_final_state).astype(jnp.bfloat16)
    factors = (
        jnp.dot(outer_normed_input, tensor_product_linear, preferred_element_type=jnp.float32)
        * alignment_entry_mask.astype(jnp.float32)[:, :, None]
    )
    left_factor = (
        factors[..., :PRODUCT_FEATURES]
        .astype(jnp.bfloat16)
        .reshape(device_local_rows, residue_total * PRODUCT_FEATURES)
    )
    right_factor = jnp.transpose(
        factors[..., PRODUCT_FEATURES:].astype(jnp.bfloat16), (0, 2, 1)
    ).reshape(device_local_rows, residue_total * PRODUCT_FEATURES)
    left_all, right_rows = gather_factors(left_factor, right_factor)
    tokens = residue_total * pair_cols
    pair_first = jnp.transpose(pair_representation.reshape(tokens, CZ))
    mix = jnp.transpose(
        outer_output_matrix.reshape(PRODUCT_FEATURES, PRODUCT_FEATURES // 4, 4 * CZ), (1, 0, 2)
    ).reshape(PRODUCT_FEATURES * PRODUCT_FEATURES // 4, 4 * CZ)
    pair_keep = (keep_here[:, None] * keep_there[None, :]).reshape(1, tokens)
    pair_opm, tri_left, tri_right, tri_gate = pair_front(
        left_all, right_rows, pair_first, mix, triangle_input_weights, pair_keep
    )
    tri_mixed = triangle(tri_left, tri_right).astype(jnp.float32)
    contract = (((0,), (0,)), ((), ()))
    mixed_normed = norm_channels(tri_mixed).astype(jnp.bfloat16)
    pair_tri = pair_opm + tri_gate * lax.dot_general(
        triangle_output_matrix, mixed_normed, contract, preferred_element_type=jnp.float32
    )
    pair_trans_in = norm_channels(pair_tri).astype(jnp.bfloat16)
    pair_hidden = jax.nn.relu(
        lax.dot_general(pair_up_weight, pair_trans_in, contract, preferred_element_type=jnp.float32)
    ).astype(jnp.bfloat16)
    updated_pair_state = (
        jnp.transpose(pair_tri)
        + lax.dot_general(pair_hidden, pair_down_weight, contract, preferred_element_type=jnp.float32)
    ).astype(jnp.bfloat16)
    updated_pair_state = updated_pair_state.reshape(residue_total, pair_cols, CZ)
    return (alignment_final_state.astype(jnp.bfloat16), updated_pair_state)


def solution(mesh):
    split = Mesh(
        mesh.devices.reshape(mesh.shape["branch"], mesh.shape["row"], 2, 8),
        ("branch", "row", "col_0", "col_1"),
    )
    in_specs = (
        P(("branch", "row"), COL, None),
        P(COL, ("branch", "row"), None),
        P(("branch", "row"), COL),
        P(),
        P(),
        P(),
        P(),
        P(),
        P(),
        P(),
        P(),
        P(),
        P(),
        P(),
        P(),
        P(),
        P(),
        P(),
        P(),
    )
    out_specs = (P(("branch", "row"), COL, None), P(COL, ("branch", "row"), None))
    return jax.shard_map(
        on_device, mesh=split, in_specs=in_specs, out_specs=out_specs, check_vma=False
    )
```

```python
import jax
import jax.numpy as jnp
from jax import lax
from jax.experimental import pallas as pl
from jax.experimental.pallas import tpu as pltpu
from jax.sharding import Mesh
from jax.sharding import PartitionSpec as P

HEADS = 8
PER_HEAD_WIDTH = 32
CZ = 128
PRODUCT_FEATURES = 32
COL = ("col_0", "col_1")


EPSILON = 1e-05
NEGATIVE = -1000000000.0


MESH = pl.DeviceIdType.MESH
GROUP = 16
RING = 8
SIZES = {"b": 16, "c": 16, "z": 8}


def place():
    axes = [lax.axis_index(a) for a in ("branch", "row", *COL)]
    return (*axes, axes[0] * 8 + axes[1], axes[2] * 8 + axes[3])


def across(b, c):
    return (b // 8, lax.rem(b, 8), c // 8, lax.rem(c, 8))


def remote(src, dst, send, recv, to):
    return pltpu.make_async_remote_copy(
        src_ref=src, dst_ref=dst, send_sem=send, recv_sem=recv, device_id=to, device_id_type=MESH
    )


def call_exchange(kernel, out_shape, scratch, collective_id, sent, *args):
    return pl.pallas_call(
        kernel,
        out_shape=out_shape,
        in_specs=[pl.BlockSpec(memory_space=pltpu.VMEM)] * len(args),
        out_specs=jax.tree.map(lambda _: pl.BlockSpec(memory_space=pltpu.VMEM), out_shape),
        scratch_shapes=scratch,
        compiler_params=pltpu.CompilerParams(
            collective_id=collective_id, has_side_effects=True, vmem_limit_bytes=48 << 20
        ),
        cost_estimate=pl.CostEstimate(flops=0, bytes_accessed=2 * sent, transcendentals=0),
    )(*args)


class Pushes:
    def __init__(self, over, ins, outs, picks, puts, send, recv):
        br, ro, x, z, b, c = place()
        self.count = SIZES[over]
        self.me, self.device = {
            "b": (b, lambda k: across(k, c)),
            "c": (c, lambda k: across(b, k)),
            "z": (z, lambda k: (br, ro, x, k)),
        }[over]
        self.parts = list(zip(ins, outs, picks, puts))
        self.send, self.recv = send, recv

    def greet(self, barrier):
        def one(d, carry):
            to = self.device(lax.rem(self.me + d, self.count))
            pl.semaphore_signal(barrier, inc=1, device_id=to, device_id_type=MESH)
            return carry

        lax.fori_loop(1, self.count, one, 0)

    def sender(self, d):
        return lax.rem(self.me + (self.count - d), self.count)

    def copies(self, d, coming):
        peer = self.sender(d) if coming else lax.rem(self.me + d, self.count)
        for k, (src, dst, pick, put) in enumerate(self.parts):
            yield remote(
                pick(src, self.me if coming else peer),
                put(dst, peer if coming else self.me),
                self.send.at[k, d],
                self.recv.at[k, d],
                self.device(peer),
            )

    def start(self):
        def one(d, carry):
            for copy in self.copies(d, False):
                copy.start()
            return carry

        lax.fori_loop(1, self.count, one, 0)
        for src, dst, pick, put in self.parts:
            put(dst, self.me)[...] = pick(src, self.me)[...]

    def arrive(self, d):
        for copy in self.copies(d, True):
            copy.wait_recv()

    def sent(self, d):
        for copy in self.copies(d, False):
            copy.wait_send()

    def finish(self):
        def one(d, carry):
            self.arrive(d)
            self.sent(d)
            return carry

        lax.fori_loop(1, self.count, one, 0)


def exchange(over, arrays, shapes, picks, puts, collective_id):
    n = len(arrays)

    def kernel(*refs):
        pushes = Pushes(over, refs[:n], refs[n : 2 * n], picks, puts, refs[2 * n], refs[2 * n + 1])
        barrier = pltpu.get_barrier_semaphore()
        pushes.greet(barrier)
        pl.semaphore_wait(barrier, SIZES[over] - 1)
        pushes.start()
        pushes.finish()

    out_shape = [jax.ShapeDtypeStruct(s, jnp.bfloat16) for s in shapes]
    scratch = [pltpu.SemaphoreType.DMA((n, GROUP))] * 2
    return call_exchange(kernel, out_shape, scratch, collective_id, 1 << 18, *arrays)


def crosswise():
    br, ro, x, z = place()[:4]
    return (br, ro, 1 - x, z)


def normal(x):
    x = x.astype(jnp.float32)
    centre = x - jnp.mean(x, axis=-1, keepdims=True)
    spread = jnp.mean(centre * centre, axis=-1, keepdims=True)
    return (centre * lax.rsqrt(spread + EPSILON)).astype(jnp.bfloat16)


def gather_bias_and_rows(pair, weights, same, chain_bias, entries, presence, col_presence):
    some, others, pair_channels = pair.shape
    heads = weights.shape[1]
    msa_rows, _, channels = entries.shape
    carried = heads // 2
    tall = some + 8
    lanes = 128
    fold = lanes // others
    n_copies = 32

    def kernel(
        p_ref, w_ref, s_ref, h_ref, e_ref, k_ref, m_ref, ob_ref, or_ref, om_ref,
        turn, tile, tiles, rows, bsend, brecv, psend, precv, xsend, xrecv, rsend, rrecv,
    ):
        br, ro, x, z, _, c = place()
        core = lax.rem(ro, 2)
        right = (br, ro, x, lax.rem(z + 1, RING))
        left = (br, ro, x, lax.rem(z + RING - 1, RING))
        twin = (br, ro + 1 - 2 * core, x, z)
        cross = crosswise()
        at = lambda ref, k: ref.at[k]
        put = lambda ref, k: ref.at[:, x * RING + k]
        spread = Pushes("b", (tile, m_ref), (tiles, om_ref), [lambda ref, k: ref, at], [at] * 2, bsend, brecv)
        pushes = Pushes("z", (rows,), (or_ref,), [lambda ref, k: ref.at[:, k]], [put], psend, precv)
        barrier = pltpu.get_barrier_semaphore()
        spread.greet(barrier)
        pushes.greet(barrier)
        pl.semaphore_signal(barrier, inc=1, device_id=cross, device_id_type=MESH)

        normed = normal(p_ref[...].reshape(some * others, pair_channels))
        for low in range(8):
            tokens = jnp.concatenate(
                [normed[(high * 8 + low) * others :][:others] for high in range(fold)], axis=0
            )
            bias = lax.dot_general(
                w_ref[...], tokens, (((0,), (1,)), ((), ())), preferred_element_type=jnp.float32
            )
            turn[low * heads : (low + 1) * heads] = bias + h_ref[...] * s_ref[low : low + 1]
        for head in range(heads):
            tile[head] = turn[pl.ds(head, 8, stride=heads)].astype(jnp.bfloat16)
        pl.semaphore_wait(barrier, GROUP - 1 + RING - 1 + 1)
        spread.start()
        normed = normal(e_ref[...].reshape(msa_rows * some, channels))
        for half in range(2):
            for k in range(RING):
                row = half * RING + k
                rows[half, k, :some] = normed[row * some : (row + 1) * some]
                rows[half, k, some:] = k_ref[row]
        pushes.start()
        first = remote(rows.at[:, z], or_ref.at[:, c], xsend.at[0], xrecv.at[0], cross)
        first.start()
        spread.finish()
        lane = lax.broadcasted_iota(jnp.int32, (8, lanes), 1) // others

        def set_out(head, carry):
            t = tiles[:, head].astype(jnp.float32).reshape(GROUP * 8, lanes)
            turned = [t] + [pltpu.roll(t, others * s, 1) for s in range(1, fold)]
            lines = []
            for n in range(fold):
                line = []
                for q in range(GROUP // fold):
                    piece = jnp.zeros((8, lanes), jnp.float32)
                    for m in range(fold):
                        k = (q * fold + m) * 8
                        piece = jnp.where(lane == m, turned[(m - n) % fold][k : k + 8], piece)
                    line.append(piece)
                lines.append(jnp.concatenate(line, axis=1))
            whole = jnp.concatenate(lines, axis=0).astype(jnp.bfloat16)
            ob_ref[head, pl.ds(pl.multiple_of(z * some, some), some)] = whole
            return carry

        lax.fori_loop(0, heads, set_out, 0)

        def view(block, half, mine):
            at_head, count = mine * carried, carried
            if half is not None:
                count = carried // 2
                at_head = at_head + half * count
            rows_at = pl.multiple_of(lax.rem(block + RING, RING) * some, some)
            return ob_ref.at[pl.ds(at_head, count), pl.ds(rows_at, some)]

        copies, handed = [], []

        def push(block, half, to):
            k = len(copies)
            there = view(block, half, core)
            copies.append(remote(there, there, rsend.at[k], rrecv.at[k], to))
            copies[-1].start()
            return k

        def arrived(k, block, half):
            there = view(block, half, core)
            remote(there, there, rsend.at[k], rrecv.at[k], right).wait_recv()

        def hand(block, half):
            handed.append((push(block, half, twin), block, half))

        def over(d, coming):
            k = pushes.sender(d)
            there = or_ref.at[:, (1 - x if coming else x) * RING + k]
            return remote(there, there, xsend.at[d], xrecv.at[d], cross)

        for step in (1, 2, 3):
            for d in (step, RING - step):
                pushes.arrive(d)
                over(d, False).start()
            if step == 1:
                going = {+1: push(z, None, right), -1: push(z, None, left)}
            coming = {}
            for way, to in ((+1, right), (-1, left)):
                block = z - way * step
                arrived(going[way], block, None)
                half = None if step < 3 else (0 if way > 0 else 1)
                coming[way] = push(block, half, to)
                hand(block, None)
            going = coming
        pushes.arrive(4)
        over(4, False).start()
        for way in (+1, -1):
            half = 0 if way > 0 else 1
            arrived(going[way], z - way * 4, half)
            hand(z - way * 4, half)
        for k, block, half in handed:
            there = view(block, half, 1 - core)
            remote(there, there, rsend.at[k], rrecv.at[k], twin).wait_recv()
        for d in range(RING):
            over(d, True).wait_recv()
        for copy in copies:
            copy.wait_send()
        first.wait_send()
        for d in range(1, RING):
            pushes.sent(d)
            over(d, False).wait_send()

    wide = GROUP * others
    out_shape = [
        jax.ShapeDtypeStruct((heads, RING * some, wide), jnp.bfloat16),
        jax.ShapeDtypeStruct((2, GROUP, tall, channels), jnp.bfloat16),
        jax.ShapeDtypeStruct(col_presence.shape, jnp.bfloat16),
    ]
    scratch = [
        pltpu.VMEM((8 * heads, lanes), jnp.float32),
        pltpu.VMEM((heads, 8, lanes), jnp.bfloat16),
        pltpu.VMEM((GROUP, heads, 8, lanes), jnp.bfloat16),
        pltpu.VMEM((2, RING, tall, channels), jnp.bfloat16),
    ]
    scratch += [pltpu.SemaphoreType.DMA((2, GROUP))] * 2
    scratch += [pltpu.SemaphoreType.DMA((1, RING))] * 2
    scratch += [pltpu.SemaphoreType.DMA((RING,))] * 2
    scratch += [pltpu.SemaphoreType.DMA((n_copies,))] * 2
    return call_exchange(
        kernel, out_shape, scratch, 1, 2 << 20,
        pair, weights, same, chain_bias, entries, presence, col_presence,
    )


def compute(kernel, out_shape, *args, scratch=(), limit=40):
    return pl.pallas_call(
        kernel,
        out_shape=out_shape,
        in_specs=[pl.BlockSpec(memory_space=pltpu.VMEM)] * len(args),
        out_specs=jax.tree.map(lambda _: pl.BlockSpec(memory_space=pltpu.VMEM), out_shape),
        scratch_shapes=list(scratch),
        compiler_params=pltpu.CompilerParams(vmem_limit_bytes=limit << 20),
    )(*args)


def heads_attend(queries, keys, values, present, bias_of):
    lanes = 128
    per = lanes // PER_HEAD_WIDTH
    lane = lax.broadcasted_iota(jnp.int32, (1, lanes), 1) // PER_HEAD_WIDTH
    blocks = []
    for block in range(HEADS // per):
        cols = slice(block * lanes, (block + 1) * lanes)
        total = jnp.zeros((queries.shape[0], lanes), jnp.float32)
        for h in range(per):
            here = (lane == h).astype(jnp.float32)
            query = queries[:, cols] * here.astype(jnp.bfloat16)
            scores = lax.dot_general(
                query, keys[:, cols], (((1,), (1,)), ((), ())), preferred_element_type=jnp.float32
            )
            if bias_of is not None:
                scores = scores + bias_of(block * per + h).astype(jnp.float32)
            scores = jnp.where(present, scores, NEGATIVE)
            powers = jnp.exp(scores - jnp.max(scores, axis=-1, keepdims=True))
            totals = jnp.sum(powers, axis=-1, keepdims=True)
            summed = jnp.dot(
                powers.astype(jnp.bfloat16), values[:, cols], preferred_element_type=jnp.float32
            )
            total = total + (summed / totals) * here
        blocks.append(total)
    return jnp.concatenate(blocks, axis=1)


def row_attention(rows, bias, weights):
    pair, blocks, tall, channels = rows.shape
    some = tall - 8
    residues = blocks * some
    step = 128

    def kernel(r_ref, b_ref, w_ref, o_ref, q_ref, g_ref):
        x = place()[2]
        for r in range(pair):
            whole = r_ref[r, :, :some].reshape(residues, channels)
            keys_values = jnp.dot(
                whole, w_ref[:, channels : 3 * channels], preferred_element_type=jnp.float32
            ).astype(jnp.bfloat16)
            keys, values = keys_values[:, :channels], keys_values[:, channels:]
            own = r_ref[r, pl.ds(x * RING, RING), :some].reshape(residues // 2, channels)
            q = jnp.dot(own, w_ref[:, :channels], preferred_element_type=jnp.float32)
            q_ref[...] = (q * PER_HEAD_WIDTH ** (-0.5)).astype(jnp.bfloat16)
            gate = jnp.dot(own, w_ref[:, 3 * channels :], preferred_element_type=jnp.float32)
            g_ref[...] = jax.nn.sigmoid(gate)
            present = []
            for half in range(2):
                total = jnp.zeros((8, channels), jnp.float32)
                for k in range(RING):
                    total = total + r_ref[r, half * RING + k, some:].astype(jnp.float32)
                present.append(total[:1])
            present = jnp.concatenate(present, axis=1) > 0

            def one(t, carry):
                at = pl.ds(pl.multiple_of(t * step, step), step)
                attended = heads_attend(
                    q_ref[at], keys, values, present, lambda h: b_ref[h, at, :]
                )
                gated = (attended * g_ref[at]).astype(jnp.bfloat16)
                o_ref[r, pl.ds(t * (step // some), step // some)] = gated.reshape(
                    step // some, some, channels
                )
                return carry

            lax.fori_loop(0, residues // 2 // step, one, 0)

    out_shape = jax.ShapeDtypeStruct((pair, RING, some, channels), jnp.bfloat16)
    scratch = [
        pltpu.VMEM((residues // 2, channels), jnp.bfloat16),
        pltpu.VMEM((residues // 2, channels), jnp.float32),
    ]
    return compute(kernel, out_shape, rows, bias, weights, scratch=scratch)


def column_attention(cols, presence, weights):
    few, rows, channels = cols.shape
    step = 128

    def kernel(c_ref, p_ref, w_ref, o_ref, q_ref, g_ref):
        halves = []
        for half in range(2):
            total = jnp.zeros((8, 128), jnp.float32)
            for k in range(RING):
                total = total + p_ref[half * RING + k].astype(jnp.float32)
            halves.append(total)
        there = jnp.concatenate(halves, axis=1)
        for r in range(few):
            whole = c_ref[r]
            projected = jnp.dot(whole, w_ref[...], preferred_element_type=jnp.float32)
            q_ref[...] = (projected[:, :channels] * PER_HEAD_WIDTH ** (-0.5)).astype(jnp.bfloat16)
            keys = projected[:, channels : 2 * channels].astype(jnp.bfloat16)
            values = projected[:, 2 * channels : 3 * channels].astype(jnp.bfloat16)
            g_ref[...] = jax.nn.sigmoid(projected[:, 3 * channels :])
            present = there[r : r + 1] > 0

            def one(t, carry):
                at = pl.ds(pl.multiple_of(t * step, step), step)
                attended = heads_attend(q_ref[at], keys, values, present, None)
                o_ref[r, at] = (attended * g_ref[at]).astype(jnp.bfloat16)
                return carry

            lax.fori_loop(0, rows // step, one, 0)

    out_shape = jax.ShapeDtypeStruct((few, rows, channels), jnp.bfloat16)
    scratch = [pltpu.VMEM((rows, channels), jnp.bfloat16), pltpu.VMEM((rows, channels), jnp.float32)]
    return compute(kernel, out_shape, cols, presence, weights, scratch=scratch)


def gather_factors(left, right):
    rows, wide = left.shape
    chips = GROUP // 2

    def kernel(l_ref, r_ref, ol_ref, or_ref, stage, zsend, zrecv, lsend, lrecv, tsend, trecv, fsend, frecv):
        br, ro, x, z, b, _ = place()
        core = lax.rem(ro, 2)
        chip = b // 2
        twin = (br, ro + 1 - 2 * core, x, z)
        put = lambda ref, k: ref.at[pl.ds(pl.multiple_of(k * rows, rows), rows)]
        at = lambda ref, k: ref.at[k]
        pushes = Pushes("z", (r_ref,), (stage,), [lambda ref, k: ref], [at], zsend, zrecv)
        on_core = lambda k: across(k * 2 + core, x * RING + z)
        back = lambda d: lax.rem(chip + chips - d, chips)
        own = br == x
        barrier = pltpu.get_barrier_semaphore()
        pushes.greet(barrier)

        def signal(to):
            pl.semaphore_signal(barrier, inc=1, device_id=to, device_id_type=MESH)

        def greet(d, carry):
            signal(on_core(lax.rem(chip + d, chips)))
            return carry

        lax.fori_loop(1, chips, greet, 0)
        signal(twin)

        def each(act):
            def one(d, carry):
                for other in range(2):
                    act(lax.rem(ro + d, RING), other)
                return carry

            lax.fori_loop(0, RING, one, 0)

        def senders(act):
            def one(k, other):
                @pl.when(jnp.logical_not(jnp.logical_and(own, jnp.logical_and(k == ro, br == other))))
                def _():
                    act(k, other)

            each(one)

        senders(lambda k, other: signal((other, k, br, z)))
        pl.semaphore_wait(
            barrier, RING - 1 + chips - 1 + 1 + jnp.where(own, GROUP - 1, GROUP)
        )

        def to_chip(d, coming):
            block = back(d) * 2 + core if coming else b
            peer = back(d) if coming else lax.rem(chip + d, chips)
            return remote(l_ref, put(ol_ref, block), lsend.at[d], lrecv.at[d], on_core(peer))

        def to_twin(d, coming):
            block = put(ol_ref, back(d) * 2 + (1 - core if coming else core))
            return remote(block, block, tsend.at[d], trecv.at[d], twin)

        def forward(k, other, src):
            return remote(src, put(or_ref, b), fsend.at[k, other], frecv.at[b], (x, k, other, z))

        def forward_all(k, src):
            for other in range(2):
                mine = jnp.logical_and(own, jnp.logical_and(k == ro, x == other))

                @pl.when(jnp.logical_not(mine))
                def _():
                    forward(k, other, src).start()

                @pl.when(mine)
                def _():
                    put(or_ref, b)[...] = src[...]

        def start(d, carry):
            for copy in pushes.copies(d, False):
                copy.start()
            to_chip(d, False).start()
            return carry

        lax.fori_loop(1, RING, start, 0)
        first = remote(l_ref, put(ol_ref, b), tsend.at[0], trecv.at[0], twin)
        first.start()
        forward_all(z, r_ref)
        put(ol_ref, b)[...] = l_ref[...]

        def relay(d, carry):
            pushes.arrive(d)
            k = pushes.sender(d)
            forward_all(k, stage.at[k])
            to_chip(d, True).wait_recv()
            to_twin(d, False).start()
            return carry

        lax.fori_loop(1, RING, relay, 0)

        def last(d, carry):
            pushes.sent(d)
            to_chip(d, False).wait_send()
            to_twin(d, True).wait_recv()
            to_twin(d, False).wait_send()
            return carry

        lax.fori_loop(1, RING, last, 0)
        to_twin(0, True).wait_recv()
        first.wait_send()

        def sent(k, other):
            mine = jnp.logical_and(own, jnp.logical_and(k == ro, x == other))

            @pl.when(jnp.logical_not(mine))
            def _():
                forward(k, other, r_ref).wait_send()

        each(sent)

        def come(k, other):
            sender = other * RING + k
            there = put(or_ref, sender)
            remote(r_ref, there, fsend.at[k, other], frecv.at[sender], (other, k, br, z)).wait_recv()

        senders(come)

    shape = jax.ShapeDtypeStruct((GROUP * rows, wide), jnp.bfloat16)
    scratch = [pltpu.VMEM((RING, rows, wide), jnp.bfloat16)]
    scratch += [pltpu.SemaphoreType.DMA((1, RING))] * 2
    scratch += [pltpu.SemaphoreType.DMA((RING,))] * 4
    scratch += [pltpu.SemaphoreType.DMA((RING, 2)), pltpu.SemaphoreType.DMA((GROUP,))]
    return call_exchange(kernel, [shape, shape], scratch, 6, 1 << 20, left, right)


def norm_channels(x):
    centre = x - jnp.mean(x, axis=0, keepdims=True)
    spread = jnp.mean(centre * centre, axis=0, keepdims=True)
    return centre * lax.rsqrt(spread + EPSILON)


def pair_front(left, right, pair, mix, weights, keep):
    rows, wide = left.shape
    channels = pair.shape[0]
    lanes = 128
    per = lanes // PRODUCT_FEATURES
    some = 8
    chunk = some * PRODUCT_FEATURES
    count = wide // chunk
    groups = RING
    deep = channels // groups

    def kernel(l_ref, r_ref, p_ref, m_ref, w_ref, k_ref, opm_ref, tl_ref, tr_ref, gate_ref):
        lane = lax.broadcasted_iota(jnp.int32, (channels, lanes), 1) // PRODUCT_FEATURES

        def one(g, carry):
            cols = pl.ds(pl.multiple_of(g * chunk, chunk), chunk)
            outer = lax.dot_general(
                l_ref[:, cols], r_ref[...], (((0,), (0,)), ((), ())), preferred_element_type=jnp.float32
            )
            outer = (outer * (1.0 / rows)).astype(jnp.bfloat16)
            stacked = jnp.concatenate(
                [
                    jnp.concatenate(
                        [
                            outer[
                                i * PRODUCT_FEATURES : (i + 1) * PRODUCT_FEATURES,
                                q * lanes : (q + 1) * lanes,
                            ]
                            for q in range(wide // lanes)
                        ],
                        axis=0,
                    )
                    for i in range(some)
                ],
                axis=1,
            )
            mixed = lax.dot_general(
                m_ref[...], stacked, (((0,), (0,)), ((), ())), preferred_element_type=jnp.float32
            )
            pieces = []
            for h in range(some // per):
                piece = jnp.zeros((channels, lanes), jnp.float32)
                for i in range(per):
                    at = (h * per + i) * lanes
                    total = None
                    for y in range(per):
                        part = mixed[y * channels : (y + 1) * channels, at : at + lanes]
                        shift = (PRODUCT_FEATURES * (i - y)) % lanes
                        part = pltpu.roll(part, shift, 1) if shift else part
                        total = part if total is None else total + part
                    piece = jnp.where(lane == i, total, piece)
                pieces.append(piece)
            opm = p_ref[:, cols].astype(jnp.float32) + jnp.concatenate(pieces, axis=1)
            opm_ref[:, cols] = opm
            normed = norm_channels(opm).astype(jnp.bfloat16)
            projected = lax.dot_general(
                w_ref[...], normed, (((0,), (0,)), ((), ())), preferred_element_type=jnp.float32
            )
            block = lambda k: projected[k * channels : (k + 1) * channels]
            here = k_ref[:, cols]
            tri_left = (here * jax.nn.sigmoid(block(0)) * block(1)).astype(jnp.bfloat16)
            tri_right = (here * jax.nn.sigmoid(block(2)) * block(3)).astype(jnp.bfloat16)
            tl_ref[:, :, cols] = tri_left.reshape(groups, deep, chunk)
            tr_ref[:, :, cols] = tri_right.reshape(groups, deep, chunk)
            gate_ref[:, cols] = jax.nn.sigmoid(block(4))
            return carry

        lax.fori_loop(0, count, one, 0)

    tokens = pair.shape[1]
    return pl.pallas_call(
        kernel,
        out_shape=[
            jax.ShapeDtypeStruct((channels, tokens), jnp.float32),
            jax.ShapeDtypeStruct((groups, deep, tokens), jnp.bfloat16),
            jax.ShapeDtypeStruct((groups, deep, tokens), jnp.bfloat16),
            jax.ShapeDtypeStruct((channels, tokens), jnp.float32),
        ],
        in_specs=[pl.BlockSpec(memory_space=pltpu.VMEM)] * 6,
        out_specs=[pl.BlockSpec(memory_space=pltpu.VMEM)] * 4,
        compiler_params=pltpu.CompilerParams(vmem_limit_bytes=40 << 20),
    )(left, right, pair, mix, weights, keep)


def exchange_channels(left, right):
    channels, few, tokens = left.shape

    def kernel(l_ref, r_ref, ol_ref, or_ref, send, recv, xsend, xrecv):
        x = place()[2]
        cross = crosswise()
        at = lambda ref, k: ref.at[k]
        here = lambda ref, k: ref.at[x, k]
        pushes = Pushes("b", (l_ref, r_ref), (ol_ref, or_ref), [at] * 2, [at, here], send, recv)
        barrier = pltpu.get_barrier_semaphore()
        pushes.greet(barrier)
        pl.semaphore_signal(barrier, inc=1, device_id=cross, device_id_type=MESH)
        pl.semaphore_wait(barrier, GROUP)

        def over(d, coming):
            there = or_ref.at[1 - x if coming else x, pushes.sender(d)]
            return remote(there, there, xsend.at[d], xrecv.at[d], cross)

        pushes.start()
        me = pushes.me
        first = remote(r_ref.at[me], or_ref.at[x, me], xsend.at[0], xrecv.at[0], cross)
        first.start()

        def one(d, carry):
            pushes.arrive(d)
            over(d, False).start()
            return carry

        lax.fori_loop(1, GROUP, one, 0)

        def last(d, carry):
            pushes.sent(d)
            over(d, True).wait_recv()
            over(d, False).wait_send()
            return carry

        lax.fori_loop(1, GROUP, last, 0)
        over(0, True).wait_recv()
        first.wait_send()

    out_shape = [
        jax.ShapeDtypeStruct((GROUP, few, tokens), jnp.bfloat16),
        jax.ShapeDtypeStruct((2, GROUP, few, tokens), jnp.bfloat16),
    ]
    scratch = [pltpu.SemaphoreType.DMA((2, GROUP))] * 2 + [pltpu.SemaphoreType.DMA((GROUP,))] * 2
    return call_exchange(kernel, out_shape, scratch, 8, 1 << 20, left, right)


def multiply_channel(left, right):
    blocks, few, tokens = left.shape
    side = int(tokens**0.5)
    lanes = 128
    per = lanes // side
    wide = blocks * side
    tall = few * side

    def kernel(l_ref, r_ref, o_ref, a_ref, b_ref, y_ref):
        lane = lax.broadcasted_iota(jnp.int32, (few, lanes), 1) // side

        def unfold(block, put):
            def one(v, carry):
                x = block(pl.ds(pl.multiple_of(v * lanes, lanes), lanes)).astype(jnp.float32)
                x = x.reshape(blocks * few, lanes)
                turned = [x] + [pltpu.roll(x, side * s, 1) for s in range(1, per)]
                for n in range(per):
                    line = []
                    for q in range(blocks // per):
                        piece = jnp.zeros((few, lanes), jnp.float32)
                        for m in range(per):
                            k = (q * per + m) * few
                            piece = jnp.where(lane == m, turned[(m - n) % per][k : k + few], piece)
                        line.append(piece)
                    put(v * per + n, jnp.concatenate(line, axis=1))
                return carry

            lax.fori_loop(0, side // per, one, 0)

        def put_left(i, line):
            a_ref[pl.ds(pl.multiple_of(i * few, few), few)] = line

        unfold(lambda cols: l_ref[:, :, cols], put_left)
        for h in range(2):

            def put_right(j, line):
                b_ref[h, pl.ds(pl.multiple_of(j * few, few), few)] = line

            unfold(lambda cols: r_ref[h, :, :, cols], put_right)
        a = a_ref[...].astype(jnp.bfloat16)
        to = lax.broadcasted_iota(jnp.int32, (tall, tall), 0)
        of = lax.broadcasted_iota(jnp.int32, (tall, tall), 1)
        order = (of == lax.rem(to, side) * few + to // side).astype(jnp.float32).astype(jnp.bfloat16)
        for h in range(2):
            b = b_ref[h].astype(jnp.bfloat16)
            b = jnp.dot(order, b, preferred_element_type=jnp.float32).astype(jnp.bfloat16)
            y_ref[:, h * tall : (h + 1) * tall] = lax.dot_general(
                a, b, (((1,), (1,)), ((), ())), preferred_element_type=jnp.float32
            )

        def fold(v, carry):
            cols = pl.ds(pl.multiple_of(v * lanes, lanes), lanes)
            y = y_ref[pl.ds(pl.multiple_of(v * per * few, per * few), per * few)]
            for q in range(wide // lanes):
                x = y[:, q * lanes : (q + 1) * lanes]
                turned = [x] + [pltpu.roll(x, side * s, 1) for s in range(1, per)]
                for m in range(per):
                    piece = jnp.zeros((few, lanes), jnp.float32)
                    for n in range(per):
                        piece = jnp.where(
                            lane == n, turned[(n - m) % per][n * few : (n + 1) * few], piece
                        )
                    o_ref[q * per + m, :, cols] = piece.astype(jnp.bfloat16)
            return carry

        lax.fori_loop(0, side // per, fold, 0)

    out_shape = jax.ShapeDtypeStruct((blocks, few, tokens), jnp.bfloat16)
    scratch = [
        pltpu.VMEM((tall, wide), jnp.float32),
        pltpu.VMEM((2, tall, wide), jnp.float32),
        pltpu.VMEM((tall, wide), jnp.float32),
    ]
    return compute(kernel, out_shape, left, right, scratch=scratch)


def triangle(tri_left, tri_right):
    groups, deep, tokens = tri_left.shape
    at = lambda ref, k: ref.at[k]
    left, right = exchange("z", (tri_left, tri_right), (tri_left.shape,) * 2, [at] * 2, [at] * 2, 7)
    left, right = exchange_channels(jnp.transpose(left, (1, 0, 2)), jnp.transpose(right, (1, 0, 2)))
    mixed = multiply_channel(left, right)
    (mixed,) = exchange("b", (mixed,), ((deep, groups, tokens),), [at], [at], 9)
    mixed = jnp.transpose(mixed, (1, 0, 2))
    (mixed,) = exchange("z", (mixed,), ((groups, deep, tokens),), [at], [at], 10)
    return mixed.reshape(groups * deep, tokens)


def layer_normalize(tensor):
    tensor = tensor.astype(jnp.float32)
    centre = tensor - jnp.mean(tensor, axis=-1, keepdims=True)
    spread = jnp.mean(centre * centre, axis=-1, keepdims=True)
    return centre * lax.rsqrt(spread + EPSILON)


def on_device(
    homolog_embedding,
    pair_representation,
    alignment_entry_mask,
    residue_presence_mask,
    residue_chain_index,
    row_projection_weights,
    horizontal_attend_merge,
    pair_bias_matrix,
    same_chain_bias,
    column_projection_weights,
    vertical_attend_merge,
    homolog_mlp_expand,
    homolog_mlp_contract,
    tensor_product_linear,
    outer_output_matrix,
    triangle_input_weights,
    triangle_output_matrix,
    pair_up_weight,
    pair_down_weight,
):
    device_local_rows, residue_total, channel_count = homolog_embedding.shape
    pair_cols = pair_representation.shape[1]
    row_place = lax.axis_index(COL)
    col_place = lax.axis_index(("branch", "row"))
    chain_here = lax.dynamic_slice_in_dim(
        residue_chain_index, row_place * residue_total, residue_total
    )
    chain_there = lax.dynamic_slice_in_dim(residue_chain_index, col_place * pair_cols, pair_cols)
    residue_keep = residue_presence_mask.astype(jnp.float32)
    keep_here = lax.dynamic_slice_in_dim(residue_keep, row_place * residue_total, residue_total)
    keep_there = lax.dynamic_slice_in_dim(residue_keep, col_place * pair_cols, pair_cols)
    group_count = GROUP
    residue_piece = residue_total // group_count
    key_presence_mask = alignment_entry_mask.astype(jnp.bfloat16)
    ring_place = lax.axis_index("col_1")
    row_presence = jnp.tile(key_presence_mask, (1, channel_count // residue_total))
    row_lane = lax.broadcasted_iota(jnp.int32, row_presence.shape, 1) // residue_total
    row_presence = jnp.where(row_lane == ring_place, row_presence, 0)
    row_presence = jnp.pad(row_presence[:, None, :], ((0, 0), (0, 7), (0, 0)))
    col_presence = jnp.transpose(
        key_presence_mask.reshape(device_local_rows, group_count, residue_piece), (1, 2, 0)
    )
    col_presence = jnp.tile(col_presence, (1, 1, 128 // device_local_rows))
    col_lane = lax.broadcasted_iota(jnp.int32, col_presence.shape, 2) // device_local_rows
    col_presence = jnp.where(col_lane == lax.rem(col_place, 8), col_presence, 0)
    col_presence = jnp.pad(col_presence, ((0, 0), (0, 8 - residue_piece), (0, 0)))
    low_first = jnp.transpose(chain_here.reshape(residue_total // 8, 8))
    same_chain = (low_first[:, :, None] == chain_there[None, None, :]).astype(jnp.float32)
    full_bias, rows_whole, mask_cols = gather_bias_and_rows(
        pair_representation,
        pair_bias_matrix,
        same_chain.reshape(8, residue_total // 8 * pair_cols),
        same_chain_bias[:, None],
        homolog_embedding,
        row_presence,
        col_presence,
    )
    gated_whole = row_attention(rows_whole, full_bias, row_projection_weights)
    along = lambda ref, k: ref.at[:, k]
    (row_gated,) = exchange("z", (gated_whole,), (gated_whole.shape,), [along], [along], 2)
    row_gated = row_gated.reshape(device_local_rows, residue_total, channel_count)
    alignment_row_state = homolog_embedding.astype(jnp.float32) + jnp.dot(
        row_gated, horizontal_attend_merge, preferred_element_type=jnp.float32
    )
    column_normed_input = layer_normalize(alignment_row_state).astype(jnp.bfloat16)
    split_input = jnp.transpose(column_normed_input, (1, 0, 2))
    rows_of = lambda ref, k: ref.at[
        :, pl.ds(pl.multiple_of(k * device_local_rows, device_local_rows), device_local_rows)
    ]
    residues_of = lambda ref, k: ref.at[pl.ds(k * residue_piece, residue_piece)]
    (normed_cols,) = exchange(
        "b",
        (split_input,),
        ((residue_piece, GROUP * device_local_rows, channel_count),),
        [residues_of],
        [rows_of],
        3,
    )
    gated = column_attention(normed_cols, mask_cols, column_projection_weights)
    (returned,) = exchange(
        "b",
        (gated,),
        ((residue_total, device_local_rows, channel_count),),
        [rows_of],
        [residues_of],
        4,
    )
    column_gated_output = jnp.transpose(returned, (1, 0, 2))
    alignment_column_state = alignment_row_state + jnp.dot(
        column_gated_output, vertical_attend_merge, preferred_element_type=jnp.float32
    )
    transition_normed_input = layer_normalize(alignment_column_state).astype(jnp.bfloat16)
    alignment_hidden_units = jax.nn.relu(
        jnp.dot(transition_normed_input, homolog_mlp_expand, preferred_element_type=jnp.float32)
    ).astype(jnp.bfloat16)
    alignment_final_state = alignment_column_state + jnp.dot(
        alignment_hidden_units, homolog_mlp_contract, preferred_element_type=jnp.float32
    )
    outer_normed_input = layer_normalize(alignment_final_state).astype(jnp.bfloat16)
    factors = (
        jnp.dot(outer_normed_input, tensor_product_linear, preferred_element_type=jnp.float32)
        * alignment_entry_mask.astype(jnp.float32)[:, :, None]
    )
    left_factor = (
        factors[..., :PRODUCT_FEATURES]
        .astype(jnp.bfloat16)
        .reshape(device_local_rows, residue_total * PRODUCT_FEATURES)
    )
    right_factor = jnp.transpose(
        factors[..., PRODUCT_FEATURES:].astype(jnp.bfloat16), (0, 2, 1)
    ).reshape(device_local_rows, residue_total * PRODUCT_FEATURES)
    left_all, right_rows = gather_factors(left_factor, right_factor)
    tokens = residue_total * pair_cols
    pair_first = jnp.transpose(pair_representation.reshape(tokens, CZ))
    mix = jnp.transpose(
        outer_output_matrix.reshape(PRODUCT_FEATURES, PRODUCT_FEATURES // 4, 4 * CZ), (1, 0, 2)
    ).reshape(PRODUCT_FEATURES * PRODUCT_FEATURES // 4, 4 * CZ)
    pair_keep = (keep_here[:, None] * keep_there[None, :]).reshape(1, tokens)
    pair_opm, tri_left, tri_right, tri_gate = pair_front(
        left_all, right_rows, pair_first, mix, triangle_input_weights, pair_keep
    )
    tri_mixed = triangle(tri_left, tri_right).astype(jnp.float32)
    contract = (((0,), (0,)), ((), ()))
    mixed_normed = norm_channels(tri_mixed).astype(jnp.bfloat16)
    pair_tri = pair_opm + tri_gate * lax.dot_general(
        triangle_output_matrix, mixed_normed, contract, preferred_element_type=jnp.float32
    )
    pair_trans_in = norm_channels(pair_tri).astype(jnp.bfloat16)
    pair_hidden = jax.nn.relu(
        lax.dot_general(pair_up_weight, pair_trans_in, contract, preferred_element_type=jnp.float32)
    ).astype(jnp.bfloat16)
    updated_pair_state = (
        jnp.transpose(pair_tri)
        + lax.dot_general(pair_hidden, pair_down_weight, contract, preferred_element_type=jnp.float32)
    ).astype(jnp.bfloat16)
    updated_pair_state = updated_pair_state.reshape(residue_total, pair_cols, CZ)
    return (alignment_final_state.astype(jnp.bfloat16), updated_pair_state)


def solution(mesh):
    split = Mesh(
        mesh.devices.reshape(mesh.shape["branch"], mesh.shape["row"], 2, 8),
        ("branch", "row", "col_0", "col_1"),
    )
    in_specs = (
        P(("branch", "row"), COL, None),
        P(COL, ("branch", "row"), None),
        P(("branch", "row"), COL),
        P(),
        P(),
        P(),
        P(),
        P(),
        P(),
        P(),
        P(),
        P(),
        P(),
        P(),
        P(),
        P(),
        P(),
        P(),
        P(),
    )
    out_specs = (P(("branch", "row"), COL, None), P(COL, ("branch", "row"), None))
    return jax.shard_map(
        on_device, mesh=split, in_specs=in_specs, out_specs=out_specs, check_vma=False
    )
```

```python
import jax
import jax.numpy as jnp
from jax import lax
from jax.experimental import pallas as pl
from jax.experimental.pallas import tpu as pltpu
from jax.sharding import Mesh
from jax.sharding import PartitionSpec as P

HEADS = 8
PER_HEAD_WIDTH = 32
CZ = 128
PRODUCT_FEATURES = 32
COL = ("col_0", "col_1")


EPSILON = 1e-05
NEGATIVE = -1000000000.0


MESH = pl.DeviceIdType.MESH
GROUP = 16
RING = 8
SIZES = {"b": 16, "c": 16, "z": 8}


def place():
    axes = [lax.axis_index(a) for a in ("branch", "row", *COL)]
    return (*axes, axes[0] * 8 + axes[1], axes[2] * 8 + axes[3])


def across(b, c):
    return (b // 8, lax.rem(b, 8), c // 8, lax.rem(c, 8))


def remote(src, dst, send, recv, to):
    return pltpu.make_async_remote_copy(
        src_ref=src, dst_ref=dst, send_sem=send, recv_sem=recv, device_id=to, device_id_type=MESH
    )


def call_exchange(kernel, out_shape, scratch, collective_id, sent, *args):
    return pl.pallas_call(
        kernel,
        out_shape=out_shape,
        in_specs=[pl.BlockSpec(memory_space=pltpu.VMEM)] * len(args),
        out_specs=jax.tree.map(lambda _: pl.BlockSpec(memory_space=pltpu.VMEM), out_shape),
        scratch_shapes=scratch,
        compiler_params=pltpu.CompilerParams(
            collective_id=collective_id, has_side_effects=True, vmem_limit_bytes=48 << 20
        ),
        cost_estimate=pl.CostEstimate(flops=0, bytes_accessed=2 * sent, transcendentals=0),
    )(*args)


class Pushes:
    def __init__(self, over, ins, outs, picks, puts, send, recv):
        br, ro, x, z, b, c = place()
        self.count = SIZES[over]
        self.me, self.device = {
            "b": (b, lambda k: across(k, c)),
            "c": (c, lambda k: across(b, k)),
            "z": (z, lambda k: (br, ro, x, k)),
        }[over]
        self.parts = list(zip(ins, outs, picks, puts))
        self.send, self.recv = send, recv

    def greet(self, barrier):
        def one(d, carry):
            to = self.device(lax.rem(self.me + d, self.count))
            pl.semaphore_signal(barrier, inc=1, device_id=to, device_id_type=MESH)
            return carry

        lax.fori_loop(1, self.count, one, 0)

    def sender(self, d):
        return lax.rem(self.me + (self.count - d), self.count)

    def copies(self, d, coming):
        peer = self.sender(d) if coming else lax.rem(self.me + d, self.count)
        for k, (src, dst, pick, put) in enumerate(self.parts):
            yield remote(
                pick(src, self.me if coming else peer),
                put(dst, peer if coming else self.me),
                self.send.at[k, d],
                self.recv.at[k, d],
                self.device(peer),
            )

    def start(self):
        def one(d, carry):
            for copy in self.copies(d, False):
                copy.start()
            return carry

        lax.fori_loop(1, self.count, one, 0)
        for src, dst, pick, put in self.parts:
            put(dst, self.me)[...] = pick(src, self.me)[...]

    def arrive(self, d):
        for copy in self.copies(d, True):
            copy.wait_recv()

    def sent(self, d):
        for copy in self.copies(d, False):
            copy.wait_send()

    def finish(self):
        def one(d, carry):
            self.arrive(d)
            self.sent(d)
            return carry

        lax.fori_loop(1, self.count, one, 0)


def exchange(over, arrays, shapes, picks, puts, collective_id):
    n = len(arrays)

    def kernel(*refs):
        pushes = Pushes(over, refs[:n], refs[n : 2 * n], picks, puts, refs[2 * n], refs[2 * n + 1])
        barrier = pltpu.get_barrier_semaphore()
        pushes.greet(barrier)
        pl.semaphore_wait(barrier, SIZES[over] - 1)
        pushes.start()
        pushes.finish()

    out_shape = [jax.ShapeDtypeStruct(s, jnp.bfloat16) for s in shapes]
    scratch = [pltpu.SemaphoreType.DMA((n, GROUP))] * 2
    return call_exchange(kernel, out_shape, scratch, collective_id, 1 << 18, *arrays)


def crosswise():
    br, ro, x, z = place()[:4]
    return (br, ro, 1 - x, z)


def normal(x):
    x = x.astype(jnp.float32)
    centre = x - jnp.mean(x, axis=-1, keepdims=True)
    spread = jnp.mean(centre * centre, axis=-1, keepdims=True)
    return (centre * lax.rsqrt(spread + EPSILON)).astype(jnp.bfloat16)


def gather_bias_and_rows(pair, weights, same, chain_bias, entries, presence, col_presence):
    some, others, pair_channels = pair.shape
    heads = weights.shape[1]
    msa_rows, _, channels = entries.shape
    carried = heads // 2
    tall = some + 8
    lanes = 128
    fold = lanes // others
    n_copies = 32

    def kernel(
        p_ref, w_ref, s_ref, h_ref, e_ref, k_ref, m_ref, ob_ref, or_ref, om_ref,
        turn, tile, tiles, rows, bsend, brecv, psend, precv, xsend, xrecv, rsend, rrecv,
    ):
        br, ro, x, z, _, c = place()
        core = lax.rem(ro, 2)
        right = (br, ro, x, lax.rem(z + 1, RING))
        left = (br, ro, x, lax.rem(z + RING - 1, RING))
        twin = (br, ro + 1 - 2 * core, x, z)
        cross = crosswise()
        at = lambda ref, k: ref.at[k]
        put = lambda ref, k: ref.at[:, x * RING + k]
        spread = Pushes("b", (tile, m_ref), (tiles, om_ref), [lambda ref, k: ref, at], [at] * 2, bsend, brecv)
        pushes = Pushes("z", (rows,), (or_ref,), [lambda ref, k: ref.at[:, k]], [put], psend, precv)
        barrier = pltpu.get_barrier_semaphore()
        spread.greet(barrier)
        pushes.greet(barrier)
        pl.semaphore_signal(barrier, inc=1, device_id=cross, device_id_type=MESH)

        normed = normal(p_ref[...].reshape(some * others, pair_channels))
        for low in range(8):
            tokens = jnp.concatenate(
                [normed[(high * 8 + low) * others :][:others] for high in range(fold)], axis=0
            )
            bias = lax.dot_general(
                w_ref[...], tokens, (((0,), (1,)), ((), ())), preferred_element_type=jnp.float32
            )
            turn[low * heads : (low + 1) * heads] = bias + h_ref[...] * s_ref[low : low + 1]
        for head in range(heads):
            tile[head] = turn[pl.ds(head, 8, stride=heads)].astype(jnp.bfloat16)
        pl.semaphore_wait(barrier, GROUP - 1 + RING - 1 + 1)
        spread.start()
        normed = normal(e_ref[...].reshape(msa_rows * some, channels))
        for half in range(2):
            for k in range(RING):
                row = half * RING + k
                rows[half, k, :some] = normed[row * some : (row + 1) * some]
                rows[half, k, some:] = k_ref[row]
        pushes.start()
        first = remote(rows.at[:, z], or_ref.at[:, c], xsend.at[0], xrecv.at[0], cross)
        first.start()
        spread.finish()
        lane = lax.broadcasted_iota(jnp.int32, (8, lanes), 1) // others

        def set_out(head, carry):
            t = tiles[:, head].astype(jnp.float32).reshape(GROUP * 8, lanes)
            turned = [t] + [pltpu.roll(t, others * s, 1) for s in range(1, fold)]
            lines = []
            for n in range(fold):
                line = []
                for q in range(GROUP // fold):
                    piece = jnp.zeros((8, lanes), jnp.float32)
                    for m in range(fold):
                        k = (q * fold + m) * 8
                        piece = jnp.where(lane == m, turned[(m - n) % fold][k : k + 8], piece)
                    line.append(piece)
                lines.append(jnp.concatenate(line, axis=1))
            whole = jnp.concatenate(lines, axis=0).astype(jnp.bfloat16)
            ob_ref[head, pl.ds(pl.multiple_of(z * some, some), some)] = whole
            return carry

        lax.fori_loop(0, heads, set_out, 0)

        def view(block, half, mine):
            at_head, count = mine * carried, carried
            if half is not None:
                count = carried // 2
                at_head = at_head + half * count
            rows_at = pl.multiple_of(lax.rem(block + RING, RING) * some, some)
            return ob_ref.at[pl.ds(at_head, count), pl.ds(rows_at, some)]

        copies, handed = [], []

        def push(block, half, to):
            k = len(copies)
            there = view(block, half, core)
            copies.append(remote(there, there, rsend.at[k], rrecv.at[k], to))
            copies[-1].start()
            return k

        def arrived(k, block, half):
            there = view(block, half, core)
            remote(there, there, rsend.at[k], rrecv.at[k], right).wait_recv()

        def hand(block, half):
            handed.append((push(block, half, twin), block, half))

        def over(d, coming):
            k = pushes.sender(d)
            there = or_ref.at[:, (1 - x if coming else x) * RING + k]
            return remote(there, there, xsend.at[d], xrecv.at[d], cross)

        for step in (1, 2, 3):
            for d in (step, RING - step):
                pushes.arrive(d)
                over(d, False).start()
            if step == 1:
                going = {+1: push(z, None, right), -1: push(z, None, left)}
            coming = {}
            for way, to in ((+1, right), (-1, left)):
                block = z - way * step
                arrived(going[way], block, None)
                half = None if step < 3 else (0 if way > 0 else 1)
                coming[way] = push(block, half, to)
                hand(block, None)
            going = coming
        pushes.arrive(4)
        over(4, False).start()
        for way in (+1, -1):
            half = 0 if way > 0 else 1
            arrived(going[way], z - way * 4, half)
            hand(z - way * 4, half)
        for k, block, half in handed:
            there = view(block, half, 1 - core)
            remote(there, there, rsend.at[k], rrecv.at[k], twin).wait_recv()
        for d in range(RING):
            over(d, True).wait_recv()
        for copy in copies:
            copy.wait_send()
        first.wait_send()
        for d in range(1, RING):
            pushes.sent(d)
            over(d, False).wait_send()

    wide = GROUP * others
    out_shape = [
        jax.ShapeDtypeStruct((heads, RING * some, wide), jnp.bfloat16),
        jax.ShapeDtypeStruct((2, GROUP, tall, channels), jnp.bfloat16),
        jax.ShapeDtypeStruct(col_presence.shape, jnp.bfloat16),
    ]
    scratch = [
        pltpu.VMEM((8 * heads, lanes), jnp.float32),
        pltpu.VMEM((heads, 8, lanes), jnp.bfloat16),
        pltpu.VMEM((GROUP, heads, 8, lanes), jnp.bfloat16),
        pltpu.VMEM((2, RING, tall, channels), jnp.bfloat16),
    ]
    scratch += [pltpu.SemaphoreType.DMA((2, GROUP))] * 2
    scratch += [pltpu.SemaphoreType.DMA((1, RING))] * 2
    scratch += [pltpu.SemaphoreType.DMA((RING,))] * 2
    scratch += [pltpu.SemaphoreType.DMA((n_copies,))] * 2
    return call_exchange(
        kernel, out_shape, scratch, 1, 2 << 20,
        pair, weights, same, chain_bias, entries, presence, col_presence,
    )


def compute(kernel, out_shape, *args, scratch=(), limit=40):
    return pl.pallas_call(
        kernel,
        out_shape=out_shape,
        in_specs=[pl.BlockSpec(memory_space=pltpu.VMEM)] * len(args),
        out_specs=jax.tree.map(lambda _: pl.BlockSpec(memory_space=pltpu.VMEM), out_shape),
        scratch_shapes=list(scratch),
        compiler_params=pltpu.CompilerParams(vmem_limit_bytes=limit << 20),
    )(*args)


def heads_attend(queries, keys, values, present, bias_of):
    lanes = 128
    per = lanes // PER_HEAD_WIDTH
    lane = lax.broadcasted_iota(jnp.int32, (1, lanes), 1) // PER_HEAD_WIDTH
    blocks = []
    for block in range(HEADS // per):
        cols = slice(block * lanes, (block + 1) * lanes)
        total = jnp.zeros((queries.shape[0], lanes), jnp.float32)
        for h in range(per):
            here = (lane == h).astype(jnp.float32)
            query = queries[:, cols] * here.astype(jnp.bfloat16)
            scores = lax.dot_general(
                query, keys[:, cols], (((1,), (1,)), ((), ())), preferred_element_type=jnp.float32
            )
            if bias_of is not None:
                scores = scores + bias_of(block * per + h).astype(jnp.float32)
            scores = jnp.where(present, scores, NEGATIVE)
            powers = jnp.exp(scores - jnp.max(scores, axis=-1, keepdims=True))
            totals = jnp.sum(powers, axis=-1, keepdims=True)
            summed = jnp.dot(
                powers.astype(jnp.bfloat16), values[:, cols], preferred_element_type=jnp.float32
            )
            total = total + (summed / totals) * here
        blocks.append(total)
    return jnp.concatenate(blocks, axis=1)


def row_attention(rows, bias, weights):
    pair, blocks, tall, channels = rows.shape
    some = tall - 8
    residues = blocks * some
    step = 128

    def kernel(r_ref, b_ref, w_ref, o_ref, q_ref, g_ref):
        x = place()[2]
        for r in range(pair):
            whole = r_ref[r, :, :some].reshape(residues, channels)
            keys_values = jnp.dot(
                whole, w_ref[:, channels : 3 * channels], preferred_element_type=jnp.float32
            ).astype(jnp.bfloat16)
            keys, values = keys_values[:, :channels], keys_values[:, channels:]
            own = r_ref[r, pl.ds(x * RING, RING), :some].reshape(residues // 2, channels)
            q = jnp.dot(own, w_ref[:, :channels], preferred_element_type=jnp.float32)
            q_ref[...] = (q * PER_HEAD_WIDTH ** (-0.5)).astype(jnp.bfloat16)
            gate = jnp.dot(own, w_ref[:, 3 * channels :], preferred_element_type=jnp.float32)
            g_ref[...] = jax.nn.sigmoid(gate)
            present = []
            for half in range(2):
                total = jnp.zeros((8, channels), jnp.float32)
                for k in range(RING):
                    total = total + r_ref[r, half * RING + k, some:].astype(jnp.float32)
                present.append(total[:1])
            present = jnp.concatenate(present, axis=1) > 0

            def one(t, carry):
                at = pl.ds(pl.multiple_of(t * step, step), step)
                attended = heads_attend(
                    q_ref[at], keys, values, present, lambda h: b_ref[h, at, :]
                )
                gated = (attended * g_ref[at]).astype(jnp.bfloat16)
                o_ref[r, pl.ds(t * (step // some), step // some)] = gated.reshape(
                    step // some, some, channels
                )
                return carry

            lax.fori_loop(0, residues // 2 // step, one, 0)

    out_shape = jax.ShapeDtypeStruct((pair, RING, some, channels), jnp.bfloat16)
    scratch = [
        pltpu.VMEM((residues // 2, channels), jnp.bfloat16),
        pltpu.VMEM((residues // 2, channels), jnp.float32),
    ]
    return compute(kernel, out_shape, rows, bias, weights, scratch=scratch)


def column_attention(cols, presence, weights):
    few, rows, channels = cols.shape
    step = 128

    def kernel(c_ref, p_ref, w_ref, o_ref, q_ref, g_ref):
        halves = []
        for half in range(2):
            total = jnp.zeros((8, 128), jnp.float32)
            for k in range(RING):
                total = total + p_ref[half * RING + k].astype(jnp.float32)
            halves.append(total)
        there = jnp.concatenate(halves, axis=1)
        for r in range(few):
            whole = c_ref[r]
            projected = jnp.dot(whole, w_ref[...], preferred_element_type=jnp.float32)
            q_ref[...] = (projected[:, :channels] * PER_HEAD_WIDTH ** (-0.5)).astype(jnp.bfloat16)
            keys = projected[:, channels : 2 * channels].astype(jnp.bfloat16)
            values = projected[:, 2 * channels : 3 * channels].astype(jnp.bfloat16)
            g_ref[...] = jax.nn.sigmoid(projected[:, 3 * channels :])
            present = there[r : r + 1] > 0

            def one(t, carry):
                at = pl.ds(pl.multiple_of(t * step, step), step)
                attended = heads_attend(q_ref[at], keys, values, present, None)
                o_ref[r, at] = (attended * g_ref[at]).astype(jnp.bfloat16)
                return carry

            lax.fori_loop(0, rows // step, one, 0)

    out_shape = jax.ShapeDtypeStruct((few, rows, channels), jnp.bfloat16)
    scratch = [pltpu.VMEM((rows, channels), jnp.bfloat16), pltpu.VMEM((rows, channels), jnp.float32)]
    return compute(kernel, out_shape, cols, presence, weights, scratch=scratch)


def norm_channels(x):
    centre = x - jnp.mean(x, axis=0, keepdims=True)
    spread = jnp.mean(centre * centre, axis=0, keepdims=True)
    return centre * lax.rsqrt(spread + EPSILON)


def pair_stack(left, right, pair, mix, tri_in, keep, tri_out, up, down):
    rows, wide = left.shape
    channels, tokens = pair.shape
    lanes = 128
    side = PRODUCT_FEATURES
    per = lanes // side
    chips = GROUP // 2
    few = RING
    deep = channels // RING
    chunk = 8 * side
    chunks = wide // chunk
    tall = few * side
    across_k = GROUP * side
    bf16, f32 = jnp.bfloat16, jnp.float32
    buffers = {
        "stage": ((RING, rows, wide), bf16),
        "all_left": ((GROUP * rows, wide), bf16),
        "all_right": ((GROUP * rows, wide), bf16),
        "opm": ((channels, tokens), f32),
        "gate": ((channels, tokens), f32),
        "tl": ((RING, deep, tokens), bf16),
        "tr": ((RING, deep, tokens), bf16),
        "l1": ((RING, deep, tokens), bf16),
        "r1": ((RING, deep, tokens), bf16),
        "turn": ((tokens // lanes, channels, lanes), f32),
        "l2": ((GROUP, few, tokens), bf16),
        "r2": ((GROUP, few, tokens), bf16),
        "l3": ((GROUP, few, tokens), bf16),
        "r3": ((2, GROUP, few, tokens), bf16),
        "a": ((tall, across_k), f32),
        "b": ((2, tall, across_k), f32),
        "y": ((tall, across_k), f32),
        "m0": ((GROUP, few, tokens), bf16),
        "m1": ((GROUP, few, tokens), bf16),
        "m2": ((RING, deep, tokens), bf16),
        "m3": ((RING, deep, tokens), bf16),
    }
    sems = {
        "zs": (1, RING), "zr": (1, RING), "ls": (RING,), "lr": (RING,), "ts": (RING,), "tr_": (RING,),
        "fs": (RING, 2), "fr": (GROUP,), "p1s": (2, chunks, RING), "p1r": (2, chunks, RING),
        "p2s": (2, GROUP), "p2r": (2, GROUP), "xs": (GROUP,), "xr": (GROUP,),
        "p3s": (1, GROUP), "p3r": (1, GROUP), "p4s": (1, RING), "p4r": (1, RING),
    }
    names = [*buffers, *sems]

    def kernel(l_ref, r_ref, p_ref, mix_ref, in_ref, k_ref, out_ref, up_ref, down_ref, o_ref, *scratch):
        s = dict(zip(names, scratch))
        br, ro, x, z, b, _ = place()
        core = lax.rem(ro, 2)
        chip = b // 2
        twin = (br, ro + 1 - 2 * core, x, z)
        cross = crosswise()
        put = lambda ref, k: ref.at[pl.ds(pl.multiple_of(k * rows, rows), rows)]
        at = lambda ref, k: ref.at[k]
        whole = lambda ref, k: ref
        ol, orr = s["all_left"], s["all_right"]
        along = Pushes("z", (r_ref,), (s["stage"],), [whole], [at], s["zs"], s["zr"])
        on_core = lambda k: across(k * 2 + core, x * RING + z)
        back = lambda d: lax.rem(chip + chips - d, chips)
        own = br == x

        def each(act):
            def one(d, carry):
                for other in range(2):
                    act(lax.rem(ro + d, RING), other)
                return carry

            lax.fori_loop(0, RING, one, 0)

        def senders(act):
            def one(k, other):
                @pl.when(jnp.logical_not(jnp.logical_and(own, jnp.logical_and(k == ro, br == other))))
                def _():
                    act(k, other)

            each(one)

        to_channel = Pushes(
            "b", (s["l2"], s["r2"]), (s["l3"], s["r3"]), [at] * 2, [at, lambda ref, k: ref.at[x, k]],
            s["p2s"], s["p2r"],
        )
        from_channel = Pushes("b", (s["m0"],), (s["m1"],), [at], [at], s["p3s"], s["p3r"])
        from_ring = Pushes("z", (s["m2"],), (s["m3"],), [at], [at], s["p4s"], s["p4r"])

        barrier = pltpu.get_barrier_semaphore()
        along.greet(barrier)
        to_channel.greet(barrier)

        def signal(to):
            pl.semaphore_signal(barrier, inc=1, device_id=to, device_id_type=MESH)

        signal(cross)
        senders(lambda k, other: signal((other, k, br, z)))
        pl.semaphore_wait(barrier, RING - 1 + GROUP - 1 + 1 + jnp.where(own, GROUP - 1, GROUP))

        def to_chip(d, coming):
            block = back(d) * 2 + core if coming else b
            peer = back(d) if coming else lax.rem(chip + d, chips)
            return remote(l_ref, put(ol, block), s["ls"].at[d], s["lr"].at[d], on_core(peer))

        def to_twin(d, coming):
            block = put(ol, back(d) * 2 + (1 - core if coming else core))
            return remote(block, block, s["ts"].at[d], s["tr_"].at[d], twin)

        def forward(k, other, src):
            return remote(src, put(orr, b), s["fs"].at[k, other], s["fr"].at[b], (x, k, other, z))

        def forward_all(k, src):
            for other in range(2):
                mine = jnp.logical_and(own, jnp.logical_and(k == ro, x == other))

                @pl.when(jnp.logical_not(mine))
                def _():
                    forward(k, other, src).start()

                @pl.when(mine)
                def _():
                    put(orr, b)[...] = src[...]

        def start(d, carry):
            for copy in along.copies(d, False):
                copy.start()
            to_chip(d, False).start()
            return carry

        lax.fori_loop(1, RING, start, 0)
        first = remote(l_ref, put(ol, b), s["ts"].at[0], s["tr_"].at[0], twin)
        first.start()
        forward_all(z, r_ref)
        put(ol, b)[...] = l_ref[...]

        def relay(d, carry):
            along.arrive(d)
            k = along.sender(d)
            forward_all(k, s["stage"].at[k])
            to_chip(d, True).wait_recv()
            to_twin(d, False).start()
            return carry

        lax.fori_loop(1, RING, relay, 0)

        def left_in(d, carry):
            to_twin(d, True).wait_recv()
            return carry

        lax.fori_loop(0, RING, left_in, 0)

        def come(k, other):
            sender = other * RING + k
            there = put(orr, sender)
            remote(r_ref, there, s["fs"].at[k, other], s["fr"].at[sender], (other, k, br, z)).wait_recv()

        senders(come)

        lane_of = lax.broadcasted_iota(jnp.int32, (channels, lanes), 1) // side
        contract = (((0,), (0,)), ((), ()))

        def channel_push(k, g, d, coming):
            src, dst = (s["tl"], s["l1"]) if k == 0 else (s["tr"], s["r1"])
            cols = pl.ds(pl.multiple_of(g * chunk, chunk), chunk)
            peer = along.sender(d) if coming else lax.rem(z + d, RING)
            return remote(
                src.at[z if coming else peer, :, cols],
                dst.at[peer if coming else z, :, cols],
                s["p1s"].at[k, g, d],
                s["p1r"].at[k, g, d],
                (br, ro, x, peer),
            )

        def front(g, carry):
            cols = pl.ds(pl.multiple_of(g * chunk, chunk), chunk)
            outer = lax.dot_general(ol[:, cols], orr[...], contract, preferred_element_type=f32)
            outer = (outer * (1.0 / (GROUP * rows))).astype(bf16)
            stacked = jnp.concatenate(
                [
                    jnp.concatenate(
                        [
                            outer[i * side : (i + 1) * side, q * lanes : (q + 1) * lanes]
                            for q in range(wide // lanes)
                        ],
                        axis=0,
                    )
                    for i in range(chunk // side)
                ],
                axis=1,
            )
            mixed = lax.dot_general(mix_ref[...], stacked, contract, preferred_element_type=f32)
            pieces = []
            for h in range(chunk // lanes):
                piece = jnp.zeros((channels, lanes), f32)
                for i in range(per):
                    at_lane = (h * per + i) * lanes
                    total = None
                    for y in range(per):
                        part = mixed[y * channels : (y + 1) * channels, at_lane : at_lane + lanes]
                        shift = (side * (i - y)) % lanes
                        part = pltpu.roll(part, shift, 1) if shift else part
                        total = part if total is None else total + part
                    piece = jnp.where(lane_of == i, total, piece)
                pieces.append(piece)
            opm = p_ref[:, cols].astype(f32) + jnp.concatenate(pieces, axis=1)
            s["opm"][:, cols] = opm
            normed = norm_channels(opm).astype(bf16)
            projected = lax.dot_general(in_ref[...], normed, contract, preferred_element_type=f32)
            block = lambda k: projected[k * channels : (k + 1) * channels]
            here = k_ref[:, cols]
            tri_left = (here * jax.nn.sigmoid(block(0)) * block(1)).astype(bf16)
            tri_right = (here * jax.nn.sigmoid(block(2)) * block(3)).astype(bf16)
            s["tl"][:, :, cols] = tri_left.reshape(RING, deep, chunk)
            s["tr"][:, :, cols] = tri_right.reshape(RING, deep, chunk)
            s["gate"][:, cols] = jax.nn.sigmoid(block(4))

            def push(d, carry):
                for k in range(2):
                    channel_push(k, g, d, False).start()
                return carry

            lax.fori_loop(1, RING, push, 0)
            return carry

        lax.fori_loop(0, chunks, front, 0)
        turn = s["turn"]

        def regroup(src, dst):
            outer, inner, _ = src.shape

            def one(v, carry):
                cols = pl.ds(pl.multiple_of(v * lanes, lanes), lanes)
                for g in range(outer):
                    turn[v, g * inner : (g + 1) * inner] = src[g, :, cols].astype(f32)
                for g in range(inner):
                    dst[g, :, cols] = turn[v, pl.ds(g, outer, stride=inner)].astype(bf16)
                return carry

            lax.fori_loop(0, tokens // lanes, one, 0)

        s["l1"][z] = s["tl"][z]
        s["r1"][z] = s["tr"][z]
        for k, ref in ((0, "l1"), (1, "r1")):

            def arrive(d, carry):
                for g in range(chunks):
                    channel_push(k, g, d, True).wait_recv()
                return carry

            lax.fori_loop(1, RING, arrive, 0)
            to = s["l2"] if k == 0 else s["r2"]
            regroup(s[ref], to)

        def over(d, coming):
            there = s["r3"].at[1 - x if coming else x, to_channel.sender(d)]
            return remote(there, there, s["xs"].at[d], s["xr"].at[d], cross)

        to_channel.start()
        first_over = remote(s["r2"].at[b], s["r3"].at[x, b], s["xs"].at[0], s["xr"].at[0], cross)
        first_over.start()

        def hand(d, carry):
            to_channel.arrive(d)
            over(d, False).start()
            return carry

        lax.fori_loop(1, GROUP, hand, 0)
        lane = lax.broadcasted_iota(jnp.int32, (few, lanes), 1) // side

        def unfold(block, put_line):
            def one(v, carry):
                t = block(pl.ds(pl.multiple_of(v * lanes, lanes), lanes)).astype(f32)
                t = t.reshape(GROUP * few, lanes)
                turned = [t] + [pltpu.roll(t, side * n, 1) for n in range(1, per)]
                for n in range(per):
                    line = []
                    for q in range(GROUP // per):
                        piece = jnp.zeros((few, lanes), f32)
                        for m in range(per):
                            k = (q * per + m) * few
                            piece = jnp.where(lane == m, turned[(m - n) % per][k : k + few], piece)
                        line.append(piece)
                    put_line(v * per + n, jnp.concatenate(line, axis=1))
                return carry

            lax.fori_loop(0, side // per, one, 0)

        lines = lambda i: pl.ds(pl.multiple_of(i * few, few), few)

        def put_left(i, line):
            s["a"][lines(i)] = line

        unfold(lambda cols: s["l3"][:, :, cols], put_left)
        a = s["a"][...].astype(bf16)
        to = lax.broadcasted_iota(jnp.int32, (tall, tall), 0)
        of = lax.broadcasted_iota(jnp.int32, (tall, tall), 1)
        order = (of == lax.rem(to, side) * few + to // side).astype(f32).astype(bf16)

        def multiply(h, carry):
            def put_right(j, line):
                s["b"][h, lines(j)] = line

            unfold(lambda cols: s["r3"][h, :, :, cols], put_right)
            t = jnp.dot(order, s["b"][h].astype(bf16), preferred_element_type=f32).astype(bf16)
            s["y"][:, pl.ds(pl.multiple_of(h * tall, tall), tall)] = lax.dot_general(
                a, t, (((1,), (1,)), ((), ())), preferred_element_type=f32
            )
            return carry

        multiply(x, 0)

        def over_in(d, carry):
            over(d, True).wait_recv()
            return carry

        lax.fori_loop(0, GROUP, over_in, 0)
        multiply(1 - x, 0)

        def fold(v, carry):
            cols = pl.ds(pl.multiple_of(v * lanes, lanes), lanes)
            y = s["y"][pl.ds(pl.multiple_of(v * per * few, per * few), per * few)]
            for q in range(across_k // lanes):
                t = y[:, q * lanes : (q + 1) * lanes]
                turned = [t] + [pltpu.roll(t, side * n, 1) for n in range(1, per)]
                for m in range(per):
                    piece = jnp.zeros((few, lanes), f32)
                    for n in range(per):
                        piece = jnp.where(
                            lane == n, turned[(n - m) % per][n * few : (n + 1) * few], piece
                        )
                    s["m0"][q * per + m, :, cols] = piece.astype(bf16)
            return carry

        lax.fori_loop(0, side // per, fold, 0)
        from_channel.start()
        from_channel.finish()
        regroup(s["m1"], s["m2"])
        from_ring.start()
        from_ring.finish()

        def end(g, carry):
            cols = pl.ds(pl.multiple_of(g * chunk, chunk), chunk)
            mixed = s["m3"][:, :, cols].astype(f32).reshape(channels, chunk)
            mixed = norm_channels(mixed).astype(bf16)
            mixed = lax.dot_general(out_ref[...], mixed, contract, preferred_element_type=f32)
            state = s["opm"][:, cols] + s["gate"][:, cols] * mixed
            normed = norm_channels(state).astype(bf16)
            hidden = lax.dot_general(up_ref[...], normed, contract, preferred_element_type=f32)
            hidden = jnp.maximum(hidden, 0.0).astype(bf16)
            update = lax.dot_general(hidden, down_ref[...], contract, preferred_element_type=f32)
            o_ref[cols] = (jnp.transpose(state) + update).astype(bf16)
            return carry

        lax.fori_loop(0, chunks, end, 0)

        def sent(d, carry):
            along.sent(d)
            to_chip(d, False).wait_send()
            to_twin(d, False).wait_send()
            for k in range(2):
                for g in range(chunks):
                    channel_push(k, g, d, False).wait_send()
            return carry

        lax.fori_loop(1, RING, sent, 0)
        first.wait_send()

        def forwarded(k, other):
            mine = jnp.logical_and(own, jnp.logical_and(k == ro, x == other))

            @pl.when(jnp.logical_not(mine))
            def _():
                forward(k, other, r_ref).wait_send()

        each(forwarded)

        def handed(d, carry):
            to_channel.sent(d)
            over(d, False).wait_send()
            return carry

        lax.fori_loop(1, GROUP, handed, 0)
        first_over.wait_send()

    scratch = [pltpu.VMEM(*v) for v in buffers.values()]
    scratch += [pltpu.SemaphoreType.DMA(v) for v in sems.values()]
    return call_exchange(
        kernel, jax.ShapeDtypeStruct((tokens, channels), bf16), scratch, 6, 4 << 20,
        left, right, pair, mix, tri_in, keep, tri_out, up, down,
    )


def layer_normalize(tensor):
    tensor = tensor.astype(jnp.float32)
    centre = tensor - jnp.mean(tensor, axis=-1, keepdims=True)
    spread = jnp.mean(centre * centre, axis=-1, keepdims=True)
    return centre * lax.rsqrt(spread + EPSILON)


def on_device(
    homolog_embedding,
    pair_representation,
    alignment_entry_mask,
    residue_presence_mask,
    residue_chain_index,
    row_projection_weights,
    horizontal_attend_merge,
    pair_bias_matrix,
    same_chain_bias,
    column_projection_weights,
    vertical_attend_merge,
    homolog_mlp_expand,
    homolog_mlp_contract,
    tensor_product_linear,
    outer_output_matrix,
    triangle_input_weights,
    triangle_output_matrix,
    pair_up_weight,
    pair_down_weight,
):
    device_local_rows, residue_total, channel_count = homolog_embedding.shape
    pair_cols = pair_representation.shape[1]
    row_place = lax.axis_index(COL)
    col_place = lax.axis_index(("branch", "row"))
    chain_here = lax.dynamic_slice_in_dim(
        residue_chain_index, row_place * residue_total, residue_total
    )
    chain_there = lax.dynamic_slice_in_dim(residue_chain_index, col_place * pair_cols, pair_cols)
    residue_keep = residue_presence_mask.astype(jnp.float32)
    keep_here = lax.dynamic_slice_in_dim(residue_keep, row_place * residue_total, residue_total)
    keep_there = lax.dynamic_slice_in_dim(residue_keep, col_place * pair_cols, pair_cols)
    group_count = GROUP
    residue_piece = residue_total // group_count
    key_presence_mask = alignment_entry_mask.astype(jnp.bfloat16)
    ring_place = lax.axis_index("col_1")
    row_presence = jnp.tile(key_presence_mask, (1, channel_count // residue_total))
    row_lane = lax.broadcasted_iota(jnp.int32, row_presence.shape, 1) // residue_total
    row_presence = jnp.where(row_lane == ring_place, row_presence, 0)
    row_presence = jnp.pad(row_presence[:, None, :], ((0, 0), (0, 7), (0, 0)))
    col_presence = jnp.transpose(
        key_presence_mask.reshape(device_local_rows, group_count, residue_piece), (1, 2, 0)
    )
    col_presence = jnp.tile(col_presence, (1, 1, 128 // device_local_rows))
    col_lane = lax.broadcasted_iota(jnp.int32, col_presence.shape, 2) // device_local_rows
    col_presence = jnp.where(col_lane == lax.rem(col_place, 8), col_presence, 0)
    col_presence = jnp.pad(col_presence, ((0, 0), (0, 8 - residue_piece), (0, 0)))
    low_first = jnp.transpose(chain_here.reshape(residue_total // 8, 8))
    same_chain = (low_first[:, :, None] == chain_there[None, None, :]).astype(jnp.float32)
    full_bias, rows_whole, mask_cols = gather_bias_and_rows(
        pair_representation,
        pair_bias_matrix,
        same_chain.reshape(8, residue_total // 8 * pair_cols),
        same_chain_bias[:, None],
        homolog_embedding,
        row_presence,
        col_presence,
    )
    gated_whole = row_attention(rows_whole, full_bias, row_projection_weights)
    along = lambda ref, k: ref.at[:, k]
    (row_gated,) = exchange("z", (gated_whole,), (gated_whole.shape,), [along], [along], 2)
    row_gated = row_gated.reshape(device_local_rows, residue_total, channel_count)
    alignment_row_state = homolog_embedding.astype(jnp.float32) + jnp.dot(
        row_gated, horizontal_attend_merge, preferred_element_type=jnp.float32
    )
    column_normed_input = layer_normalize(alignment_row_state).astype(jnp.bfloat16)
    split_input = jnp.transpose(column_normed_input, (1, 0, 2))
    rows_of = lambda ref, k: ref.at[
        :, pl.ds(pl.multiple_of(k * device_local_rows, device_local_rows), device_local_rows)
    ]
    residues_of = lambda ref, k: ref.at[pl.ds(k * residue_piece, residue_piece)]
    (normed_cols,) = exchange(
        "b",
        (split_input,),
        ((residue_piece, GROUP * device_local_rows, channel_count),),
        [residues_of],
        [rows_of],
        3,
    )
    gated = column_attention(normed_cols, mask_cols, column_projection_weights)
    (returned,) = exchange(
        "b",
        (gated,),
        ((residue_total, device_local_rows, channel_count),),
        [rows_of],
        [residues_of],
        4,
    )
    column_gated_output = jnp.transpose(returned, (1, 0, 2))
    alignment_column_state = alignment_row_state + jnp.dot(
        column_gated_output, vertical_attend_merge, preferred_element_type=jnp.float32
    )
    transition_normed_input = layer_normalize(alignment_column_state).astype(jnp.bfloat16)
    alignment_hidden_units = jax.nn.relu(
        jnp.dot(transition_normed_input, homolog_mlp_expand, preferred_element_type=jnp.float32)
    ).astype(jnp.bfloat16)
    alignment_final_state = alignment_column_state + jnp.dot(
        alignment_hidden_units, homolog_mlp_contract, preferred_element_type=jnp.float32
    )
    outer_normed_input = layer_normalize(alignment_final_state).astype(jnp.bfloat16)
    factors = (
        jnp.dot(outer_normed_input, tensor_product_linear, preferred_element_type=jnp.float32)
        * alignment_entry_mask.astype(jnp.float32)[:, :, None]
    )
    left_factor = (
        factors[..., :PRODUCT_FEATURES]
        .astype(jnp.bfloat16)
        .reshape(device_local_rows, residue_total * PRODUCT_FEATURES)
    )
    right_factor = jnp.transpose(
        factors[..., PRODUCT_FEATURES:].astype(jnp.bfloat16), (0, 2, 1)
    ).reshape(device_local_rows, residue_total * PRODUCT_FEATURES)
    tokens = residue_total * pair_cols
    pair_first = jnp.transpose(pair_representation.reshape(tokens, CZ))
    mix = jnp.transpose(
        outer_output_matrix.reshape(PRODUCT_FEATURES, PRODUCT_FEATURES // 4, 4 * CZ), (1, 0, 2)
    ).reshape(PRODUCT_FEATURES * PRODUCT_FEATURES // 4, 4 * CZ)
    pair_keep = (keep_here[:, None] * keep_there[None, :]).reshape(1, tokens)
    updated_pair_state = pair_stack(
        left_factor,
        right_factor,
        pair_first,
        mix,
        triangle_input_weights,
        pair_keep,
        triangle_output_matrix,
        pair_up_weight,
        pair_down_weight,
    )
    updated_pair_state = updated_pair_state.reshape(residue_total, pair_cols, CZ)
    return (alignment_final_state.astype(jnp.bfloat16), updated_pair_state)


def solution(mesh):
    split = Mesh(
        mesh.devices.reshape(mesh.shape["branch"], mesh.shape["row"], 2, 8),
        ("branch", "row", "col_0", "col_1"),
    )
    in_specs = (
        P(("branch", "row"), COL, None),
        P(COL, ("branch", "row"), None),
        P(("branch", "row"), COL),
        P(),
        P(),
        P(),
        P(),
        P(),
        P(),
        P(),
        P(),
        P(),
        P(),
        P(),
        P(),
        P(),
        P(),
        P(),
        P(),
    )
    out_specs = (P(("branch", "row"), COL, None), P(COL, ("branch", "row"), None))
    return jax.shard_map(
        on_device, mesh=split, in_specs=in_specs, out_specs=out_specs, check_vma=False
    )
```

```python
import jax
import jax.numpy as jnp
from jax import lax
from jax.experimental import pallas as pl
from jax.experimental.pallas import tpu as pltpu
from jax.sharding import Mesh
from jax.sharding import PartitionSpec as P

HEADS = 8
PER_HEAD_WIDTH = 32
CZ = 128
PRODUCT_FEATURES = 32
COL = ("col_0", "col_1")


EPSILON = 1e-05
NEGATIVE = -1000000000.0


MESH = pl.DeviceIdType.MESH
GROUP = 16
RING = 8
SIZES = {"b": 16, "c": 16, "z": 8}


def place():
    axes = [lax.axis_index(a) for a in ("branch", "row", *COL)]
    return (*axes, axes[0] * 8 + axes[1], axes[2] * 8 + axes[3])


def across(b, c):
    return (b // 8, lax.rem(b, 8), c // 8, lax.rem(c, 8))


def remote(src, dst, send, recv, to):
    return pltpu.make_async_remote_copy(
        src_ref=src, dst_ref=dst, send_sem=send, recv_sem=recv, device_id=to, device_id_type=MESH
    )


IN_VMEM = pl.BlockSpec(memory_space=pltpu.VMEM)
IN_SMEM = pl.BlockSpec(memory_space=pltpu.SMEM)
IN_PLACE = pl.BlockSpec(memory_space=pl.ANY)


def call_exchange(kernel, out_shape, scratch, collective_id, sent, specs, *args):
    return pl.pallas_call(
        kernel,
        out_shape=out_shape,
        in_specs=specs,
        out_specs=jax.tree.map(lambda _: IN_VMEM, out_shape),
        scratch_shapes=scratch,
        compiler_params=pltpu.CompilerParams(
            collective_id=collective_id, has_side_effects=True, vmem_limit_bytes=62 << 20
        ),
        cost_estimate=pl.CostEstimate(flops=0, bytes_accessed=2 * sent, transcendentals=0),
    )(*args)


class Pushes:
    def __init__(self, over, ins, outs, picks, puts, send, recv):
        br, ro, x, z, b, c = place()
        self.count = SIZES[over]
        self.me, self.device = {
            "b": (b, lambda k: across(k, c)),
            "c": (c, lambda k: across(b, k)),
            "z": (z, lambda k: (br, ro, x, k)),
        }[over]
        self.parts = list(zip(ins, outs, picks, puts))
        self.send, self.recv = send, recv

    def greet(self, barrier):
        def one(d, carry):
            to = self.device(lax.rem(self.me + d, self.count))
            pl.semaphore_signal(barrier, inc=1, device_id=to, device_id_type=MESH)
            return carry

        lax.fori_loop(1, self.count, one, 0)

    def sender(self, d):
        return lax.rem(self.me + (self.count - d), self.count)

    def copies(self, d, coming):
        peer = self.sender(d) if coming else lax.rem(self.me + d, self.count)
        for k, (src, dst, pick, put) in enumerate(self.parts):
            yield remote(
                pick(src, self.me if coming else peer),
                put(dst, peer if coming else self.me),
                self.send.at[k, d],
                self.recv.at[k, d],
                self.device(peer),
            )

    def start(self):
        def one(d, carry):
            for copy in self.copies(d, False):
                copy.start()
            return carry

        lax.fori_loop(1, self.count, one, 0)
        for src, dst, pick, put in self.parts:
            put(dst, self.me)[...] = pick(src, self.me)[...]

    def arrive(self, d):
        for copy in self.copies(d, True):
            copy.wait_recv()

    def sent(self, d):
        for copy in self.copies(d, False):
            copy.wait_send()

    def finish(self):
        def one(d, carry):
            self.arrive(d)
            self.sent(d)
            return carry

        lax.fori_loop(1, self.count, one, 0)


def crosswise():
    br, ro, x, z = place()[:4]
    return (br, ro, 1 - x, z)


def normal(x):
    x = x.astype(jnp.float32)
    centre = x - jnp.mean(x, axis=-1, keepdims=True)
    spread = jnp.mean(centre * centre, axis=-1, keepdims=True)
    return (centre * lax.rsqrt(spread + EPSILON)).astype(jnp.bfloat16)


def gather_bias_and_rows(pair, weights, same, chain_bias, entries, presence):
    some, others, pair_channels = pair.shape
    heads = weights.shape[0]
    msa_rows, _, channels = entries.shape
    carried = heads // 2
    tall = some + 8
    lanes = 128
    fold = lanes // others
    n_copies = 32

    def kernel(
        p_in, w_ref, s_ref, h_ref, e_in, k_ref, ob_ref, or_ref, om_ref,
        p_ref, e_ref, m_ref, load, turn, tile, tiles, rows, bsend, brecv, psend, precv, xsend, xrecv, rsend, rrecv,
    ):
        br, ro, x, z, _, c = place()
        core = lax.rem(ro, 2)
        right = (br, ro, x, lax.rem(z + 1, RING))
        left = (br, ro, x, lax.rem(z + RING - 1, RING))
        twin = (br, ro + 1 - 2 * core, x, z)
        cross = crosswise()
        at = lambda ref, k: ref.at[k]
        put = lambda ref, k: ref.at[:, x * RING + k]
        spread = Pushes(
            "b", (tile, m_ref), (tiles, om_ref), [lambda ref, k: ref, lambda ref, k: ref.at[k // 4]], [at] * 2, bsend, brecv
        )
        pair_load = pltpu.make_async_copy(p_in, p_ref, load.at[0])
        entry_load = pltpu.make_async_copy(e_in, e_ref, load.at[1])
        pair_load.start()
        entry_load.start()
        pushes = Pushes("z", (rows,), (or_ref,), [lambda ref, k: ref.at[:, k]], [put], psend, precv)
        barrier = pltpu.get_barrier_semaphore()
        spread.greet(barrier)
        pushes.greet(barrier)
        pl.semaphore_signal(barrier, inc=1, device_id=cross, device_id_type=MESH)

        present = k_ref[...].astype(jnp.float32)
        spot = lax.broadcasted_iota(jnp.int32, (msa_rows, lanes), 0)
        wide_lane = lax.broadcasted_iota(jnp.int32, (msa_rows, lanes), 1)
        copies_of = (lax.rem(wide_lane, msa_rows) == spot).astype(jnp.float32)
        by_residue = lax.dot_general(
            present, copies_of, (((0,), (0,)), ((), ())), preferred_element_type=jnp.float32
        )
        mine = lax.broadcasted_iota(jnp.int32, (some, lanes), 1) // msa_rows == lax.rem(br * 8 + ro, 8)
        by_residue = jnp.where(mine, by_residue, 0.0).astype(jnp.bfloat16)
        for k in range(some // 8):
            m_ref[k] = by_residue[k * 8 : (k + 1) * 8]
        spot = lax.broadcasted_iota(jnp.int32, (some, channels), 0)
        wide_lane = lax.broadcasted_iota(jnp.int32, (some, channels), 1)
        here = jnp.logical_and(lax.rem(wide_lane, some) == spot, wide_lane // some == z)
        by_row = jnp.dot(present, here.astype(jnp.float32), preferred_element_type=jnp.float32)
        head_of = lax.broadcasted_iota(jnp.int32, (heads, lanes), 0)
        chain = jnp.zeros((heads, lanes), jnp.float32)
        for head in range(heads):
            chain = jnp.where(head_of == head, h_ref[head], chain)
        pair_load.wait()
        normed = normal(p_ref[...].reshape(some * others, pair_channels))
        for low in range(8):
            tokens = jnp.concatenate(
                [normed[(high * 8 + low) * others :][:others] for high in range(fold)], axis=0
            )
            bias = lax.dot_general(
                w_ref[...], tokens, (((1,), (1,)), ((), ())), preferred_element_type=jnp.float32
            )
            turn[low * heads : (low + 1) * heads] = bias + chain * s_ref[low : low + 1]
        for head in range(heads):
            tile[head] = turn[pl.ds(head, 8, stride=heads)].astype(jnp.bfloat16)
        pl.semaphore_wait(barrier, GROUP - 1 + RING - 1 + 1)
        spread.start()
        entry_load.wait()
        normed = normal(e_ref[...].reshape(msa_rows * some, channels))
        for half in range(2):
            for k in range(RING):
                row = half * RING + k
                rows[half, k, :some] = normed[row * some : (row + 1) * some]
                rows[half, k, some:] = jnp.broadcast_to(by_row[row : row + 1], (8, channels)).astype(jnp.bfloat16)
        pushes.start()
        first = remote(rows.at[:, z], or_ref.at[:, c], xsend.at[0], xrecv.at[0], cross)
        first.start()
        spread.finish()
        lane = lax.broadcasted_iota(jnp.int32, (8, lanes), 1) // others

        def set_out(head, carry):
            t = tiles[:, head].astype(jnp.float32).reshape(GROUP * 8, lanes)
            turned = [t] + [pltpu.roll(t, others * s, 1) for s in range(1, fold)]
            lines = []
            for n in range(fold):
                line = []
                for q in range(GROUP // fold):
                    piece = jnp.zeros((8, lanes), jnp.float32)
                    for m in range(fold):
                        k = (q * fold + m) * 8
                        piece = jnp.where(lane == m, turned[(m - n) % fold][k : k + 8], piece)
                    line.append(piece)
                lines.append(jnp.concatenate(line, axis=1))
            whole = jnp.concatenate(lines, axis=0).astype(jnp.bfloat16)
            ob_ref[head, pl.ds(pl.multiple_of(z * some, some), some)] = whole
            return carry

        lax.fori_loop(0, heads, set_out, 0)

        def view(block, half, mine):
            at_head, count = mine * carried, carried
            if half is not None:
                count = carried // 2
                at_head = at_head + half * count
            rows_at = pl.multiple_of(lax.rem(block + RING, RING) * some, some)
            return ob_ref.at[pl.ds(at_head, count), pl.ds(rows_at, some)]

        copies, handed = [], []

        def push(block, half, to):
            k = len(copies)
            there = view(block, half, core)
            copies.append(remote(there, there, rsend.at[k], rrecv.at[k], to))
            copies[-1].start()
            return k

        def arrived(k, block, half):
            there = view(block, half, core)
            remote(there, there, rsend.at[k], rrecv.at[k], right).wait_recv()

        def hand(block, half):
            handed.append((push(block, half, twin), block, half))

        def over(d, coming):
            k = pushes.sender(d)
            there = or_ref.at[:, (1 - x if coming else x) * RING + k]
            return remote(there, there, xsend.at[d], xrecv.at[d], cross)

        for step in (1, 2, 3):
            for d in (step, RING - step):
                pushes.arrive(d)
                over(d, False).start()
            if step == 1:
                going = {+1: push(z, None, right), -1: push(z, None, left)}
            coming = {}
            for way, to in ((+1, right), (-1, left)):
                block = z - way * step
                arrived(going[way], block, None)
                half = None if step < 3 else (0 if way > 0 else 1)
                coming[way] = push(block, half, to)
                hand(block, None)
            going = coming
        pushes.arrive(4)
        over(4, False).start()
        for way in (+1, -1):
            half = 0 if way > 0 else 1
            arrived(going[way], z - way * 4, half)
            hand(z - way * 4, half)
        for k, block, half in handed:
            there = view(block, half, 1 - core)
            remote(there, there, rsend.at[k], rrecv.at[k], twin).wait_recv()
        for d in range(RING):
            over(d, True).wait_recv()
        for copy in copies:
            copy.wait_send()
        first.wait_send()
        for d in range(1, RING):
            pushes.sent(d)
            over(d, False).wait_send()

    wide = GROUP * others
    out_shape = [
        jax.ShapeDtypeStruct((heads, RING * some, wide), jnp.bfloat16),
        jax.ShapeDtypeStruct((2, GROUP, tall, channels), jnp.bfloat16),
        jax.ShapeDtypeStruct((GROUP, 8, lanes), jnp.bfloat16),
    ]
    scratch = [
        pltpu.VMEM(pair.shape, jnp.bfloat16),
        pltpu.VMEM(entries.shape, jnp.bfloat16),
        pltpu.VMEM((some // 8, 8, lanes), jnp.bfloat16),
        pltpu.SemaphoreType.DMA((2,)),
        pltpu.VMEM((8 * heads, lanes), jnp.float32),
        pltpu.VMEM((heads, 8, lanes), jnp.bfloat16),
        pltpu.VMEM((GROUP, heads, 8, lanes), jnp.bfloat16),
        pltpu.VMEM((2, RING, tall, channels), jnp.bfloat16),
    ]
    scratch += [pltpu.SemaphoreType.DMA((2, GROUP))] * 2
    scratch += [pltpu.SemaphoreType.DMA((1, RING))] * 2
    scratch += [pltpu.SemaphoreType.DMA((RING,))] * 2
    scratch += [pltpu.SemaphoreType.DMA((n_copies,))] * 2
    return call_exchange(
        kernel, out_shape, scratch, 1, 2 << 20,
        [IN_PLACE, IN_VMEM, IN_VMEM, IN_SMEM, IN_PLACE, IN_VMEM],
        pair, weights, same, chain_bias, entries, presence,
    )


def heads_attend(queries, keys, values, present, bias_of):
    lanes = 128
    per = lanes // PER_HEAD_WIDTH
    lane = lax.broadcasted_iota(jnp.int32, (1, lanes), 1) // PER_HEAD_WIDTH
    blocks = []
    for block in range(HEADS // per):
        cols = slice(block * lanes, (block + 1) * lanes)
        total = jnp.zeros((queries.shape[0], lanes), jnp.float32)
        for h in range(per):
            here = (lane == h).astype(jnp.float32)
            query = queries[:, cols] * here.astype(jnp.bfloat16)
            scores = lax.dot_general(
                query, keys[:, cols], (((1,), (1,)), ((), ())), preferred_element_type=jnp.float32
            )
            if bias_of is not None:
                scores = scores + bias_of(block * per + h).astype(jnp.float32)
            scores = jnp.where(present, scores, NEGATIVE)
            powers = jnp.exp(scores - jnp.max(scores, axis=-1, keepdims=True))
            totals = jnp.sum(powers, axis=-1, keepdims=True)
            summed = jnp.dot(
                powers.astype(jnp.bfloat16), values[:, cols], preferred_element_type=jnp.float32
            )
            total = total + (summed / totals) * here
        blocks.append(total)
    return jnp.concatenate(blocks, axis=1)


def norm_channels(x):
    centre = x - jnp.mean(x, axis=0, keepdims=True)
    spread = jnp.mean(centre * centre, axis=0, keepdims=True)
    return centre * lax.rsqrt(spread + EPSILON)


def both_stacks(
    whole_rows, bias, row_weights, row_merge, entries, col_presence, col_weights, col_merge, expand,
    contract_weights, factor_weights, presence, pair, outer_weights, tri_in, keep, tri_out, up, down,
):
    rows, residues, features = entries.shape
    wide = residues * PRODUCT_FEATURES
    entry_count = rows * residues
    columns = residues // GROUP
    queries = RING * residues
    keys_count = GROUP * residues
    step = 128
    tokens, channels = pair.shape
    lanes = 128
    side = PRODUCT_FEATURES
    per = lanes // side
    chips = GROUP // 2
    few = RING
    deep = channels // RING
    chunk = 8 * side
    chunks = wide // chunk
    tall = few * side
    across_k = GROUP * side
    bf16, f32 = jnp.bfloat16, jnp.float32
    inputs = dict(
        w=whole_rows, wr=row_weights, bias=bias, ow=outer_weights, e=entries, rm=row_merge, cp=col_presence, wc=col_weights,
        cm=col_merge, ex=expand, co=contract_weights, fw=factor_weights, p=pair, tri_in=tri_in, tri_out=tri_out, up=up,
        down=down,
    )
    buffers = {
        **{"in_" + name: (value.shape, value.dtype) for name, value in inputs.items()},
        "mix": ((PRODUCT_FEATURES * PRODUCT_FEATURES // 4, 4 * channels), bf16),
        "outer_f32": (outer_weights.shape, f32),
        "there": ((8, 2 * lanes), f32),
        "q": ((queries, features), bf16),
        "g": ((queries, features), f32),
        "row_out": ((2, RING, residues, features), bf16),
        "row_in": ((2, RING, residues, features), bf16),
        "by_lane": ((features // 128, entry_count, 128), f32),
        "state": ((entry_count, features), f32),
        "again": ((entry_count, features), f32),
        "col_sent": ((residues, rows, features), bf16),
        "cols": ((columns, GROUP * rows, features), bf16),
        "col_out": ((columns, GROUP * rows, features), bf16),
        "col_in": ((residues, rows, features), bf16),
        "apart": ((rows // 4, PRODUCT_FEATURES, 128), f32),
        "joined": ((rows * 8, 128), f32),
        "left": ((rows, wide), bf16),
        "right": ((rows, wide), bf16),
        "stage": ((RING, rows, wide), bf16),
        "all_left": ((GROUP * rows, wide), bf16),
        "all_right": ((GROUP * rows, wide), bf16),
        "opm": ((channels, tokens), f32),
        "gate": ((channels, tokens), f32),
        "tl": ((RING, deep, tokens), bf16),
        "tr": ((RING, deep, tokens), bf16),
        "l1": ((RING, deep, tokens), bf16),
        "r1": ((RING, deep, tokens), bf16),
        "turn": ((tokens // lanes, channels, lanes), f32),
        "l2": ((GROUP, few, tokens), bf16),
        "r2": ((GROUP, few, tokens), bf16),
        "l3": ((GROUP, few, tokens), bf16),
        "r3": ((2, GROUP, few, tokens), bf16),
        "a": ((tall, across_k), f32),
        "b": ((2, tall, across_k), f32),
        "y": ((tall, across_k), f32),
        "m0": ((GROUP, few, tokens), bf16),
        "m1": ((GROUP, few, tokens), bf16),
        "m2": ((RING, deep, tokens), bf16),
        "m3": ((RING, deep, tokens), bf16),
    }
    sems = {
        "load": (len(inputs),),
        "rs": (2, RING), "rr": (2, RING), "c1s": (1, GROUP), "c1r": (1, GROUP),
        "c2s": (1, GROUP), "c2r": (1, GROUP), "c3s": (1, GROUP), "c3r": (1, GROUP),
        "zs": (1, RING), "zr": (1, RING), "ls": (RING,), "lr": (RING,), "ts": (RING,), "tr_": (RING,),
        "fs": (RING, 2), "fr": (GROUP,), "p1s": (2, chunks, RING), "p1r": (2, chunks, RING),
        "p2s": (2, GROUP), "p2r": (2, GROUP), "xs": (GROUP,), "xr": (GROUP,),
        "p3s": (1, GROUP), "p3r": (1, GROUP), "p4s": (1, RING), "p4r": (1, RING),
    }
    names = [*buffers, *sems]

    def kernel(
        w_in, b_in, wr_in, rm_in, e_in, cp_in, wc_in, cm_in, ex_in, co_in, fw_in, pr_ref,
        p_in, ow_in, in_in, k_ref, out_in, up_in, down_in, om_ref, o_ref, *scratch,
    ):
        s = dict(zip(names, scratch))
        loads = {}
        for n, (name, ref) in enumerate(
            dict(
                w=w_in, wr=wr_in, bias=b_in, ow=ow_in, e=e_in, rm=rm_in, cp=cp_in, wc=wc_in, cm=cm_in, ex=ex_in,
                co=co_in, fw=fw_in, p=p_in, tri_in=in_in, tri_out=out_in, up=up_in, down=down_in,
            ).items()
        ):
            loads[name] = pltpu.make_async_copy(ref, s["in_" + name], s["load"].at[n])
            loads[name].start()
        w_ref, wr_ref, b_ref, ow_ref, e_ref, rm_ref, cp_ref, wc_ref, cm_ref, ex_ref, co_ref, fw_ref, p_ref = (
            s["in_" + n] for n in ("w", "wr", "bias", "ow", "e", "rm", "cp", "wc", "cm", "ex", "co", "fw", "p")
        )
        in_ref, out_ref, up_ref, down_ref = (s["in_" + n] for n in ("tri_in", "tri_out", "up", "down"))
        mix_ref = s["mix"]

        def ready(*wanted):
            for name in wanted:
                loads[name].wait()

        l_ref, r_ref = s["left"], s["right"]
        br, ro, x, z, b, _ = place()
        core = lax.rem(ro, 2)
        chip = b // 2
        twin = (br, ro + 1 - 2 * core, x, z)
        cross = crosswise()
        put = lambda ref, k: ref.at[pl.ds(pl.multiple_of(k * rows, rows), rows)]
        at = lambda ref, k: ref.at[k]
        whole = lambda ref, k: ref
        ol, orr = s["all_left"], s["all_right"]
        along = Pushes("z", (r_ref,), (s["stage"],), [whole], [at], s["zs"], s["zr"])
        on_core = lambda k: across(k * 2 + core, x * RING + z)
        back = lambda d: lax.rem(chip + chips - d, chips)
        own = br == x

        def each(act):
            def one(d, carry):
                for other in range(2):
                    act(lax.rem(ro + d, RING), other)
                return carry

            lax.fori_loop(0, RING, one, 0)

        def senders(act):
            def one(k, other):
                @pl.when(jnp.logical_not(jnp.logical_and(own, jnp.logical_and(k == ro, br == other))))
                def _():
                    act(k, other)

            each(one)

        to_channel = Pushes(
            "b", (s["l2"], s["r2"]), (s["l3"], s["r3"]), [at] * 2, [at, lambda ref, k: ref.at[x, k]],
            s["p2s"], s["p2r"],
        )
        from_channel = Pushes("b", (s["m0"],), (s["m1"],), [at], [at], s["p3s"], s["p3r"])
        from_ring = Pushes("z", (s["m2"],), (s["m3"],), [at], [at], s["p4s"], s["p4r"])

        barrier = pltpu.get_barrier_semaphore()
        along.greet(barrier)
        to_channel.greet(barrier)

        def signal(to):
            pl.semaphore_signal(barrier, inc=1, device_id=to, device_id_type=MESH)

        signal(cross)
        senders(lambda k, other: signal((other, k, br, z)))
        lane_at = lax.broadcasted_iota(jnp.int32, (1, lanes), 1) // side

        def row_push(r, d, coming):
            peer = along.sender(d) if coming else lax.rem(z + d, RING)
            return remote(
                s["row_out"].at[r, z if coming else peer],
                s["row_in"].at[r, peer if coming else z],
                s["rs"].at[r, d],
                s["rr"].at[r, d],
                (br, ro, x, peer),
            )

        ready("w", "wr")
        for r in range(2):
            whole_row = w_ref[r, :, :residues].reshape(keys_count, features)
            keys_values = jnp.dot(
                whole_row, wr_ref[:, features : 3 * features], preferred_element_type=f32
            ).astype(bf16)
            keys, values = keys_values[:, :features], keys_values[:, features:]
            half_row = w_ref[r, pl.ds(x * RING, RING), :residues].reshape(queries, features)
            q = jnp.dot(half_row, wr_ref[:, :features], preferred_element_type=f32)
            s["q"][...] = (q * PER_HEAD_WIDTH ** (-0.5)).astype(bf16)
            gate = jnp.dot(half_row, wr_ref[:, 3 * features :], preferred_element_type=f32)
            s["g"][...] = jax.nn.sigmoid(gate)
            present = []
            for half in range(2):
                total = jnp.zeros((8, features), f32)
                for k in range(RING):
                    total = total + w_ref[r, half * RING + k, residues:].astype(f32)
                present.append(total[:1])
            present = jnp.concatenate(present, axis=1) > 0
            if r == 0:
                ready("bias")
                pl.semaphore_wait(
                    barrier, RING - 1 + GROUP - 1 + 1 + jnp.where(own, GROUP - 1, GROUP)
                )

            def row_block(t, carry):
                t = lax.rem(t + 1 - z // 4, 2)
                rows_at = pl.ds(pl.multiple_of(t * step, step), step)
                attended = heads_attend(
                    s["q"][rows_at], keys, values, present, lambda h: b_ref[h, rows_at, :]
                )
                gated = (attended * s["g"][rows_at]).astype(bf16)
                some = step // residues
                s["row_out"][r, pl.ds(t * some, some)] = gated.reshape(some, residues, features)

                def push(k, carry):
                    d = lax.rem(t * some + k - z + RING, RING)

                    @pl.when(d != 0)
                    def _():
                        row_push(r, d, False).start()

                    return carry

                lax.fori_loop(0, some, push, 0)
                return carry

            lax.fori_loop(0, queries // step, row_block, 0)
            s["row_in"][r, z] = s["row_out"][r, z]

        ready("ow", "e", "rm", "cp", "wc", "fw")
        s["outer_f32"][...] = ow_ref[...].astype(f32)
        for q in range(PRODUCT_FEATURES // 4):
            for y in range(4):
                mix_ref[q * side : (q + 1) * side, y * channels : (y + 1) * channels] = s["outer_f32"][
                    pl.ds(q * 4 + y, side, stride=PRODUCT_FEATURES)
                ].astype(bf16)
        copied = lax.broadcasted_iota(jnp.int32, (2 * side, lanes), 0)
        copied_to = lax.rem(lax.broadcasted_iota(jnp.int32, (2 * side, lanes), 1), side)
        copied = (copied == copied_to).astype(f32).astype(bf16)
        left_weights = jnp.dot(fw_ref[...], copied, preferred_element_type=f32).astype(bf16)
        present = pr_ref[...].astype(f32)
        spot = lax.broadcasted_iota(jnp.int32, (residues, lanes), 0)
        wide_lane = lax.broadcasted_iota(jnp.int32, (residues, lanes), 1)
        beside = (lax.rem(wide_lane, residues) == spot).astype(f32)
        right_presence = jnp.dot(present, beside, preferred_element_type=f32)

        def left_presence(q):
            spread = jnp.logical_and(spot // per == q, wide_lane // side == lax.rem(spot, per))
            return jnp.dot(present, spread.astype(f32), preferred_element_type=f32)

        def row_arrive(d, carry):
            for r in range(2):
                row_push(r, d, True).wait_recv()
            return carry

        lax.fori_loop(1, RING, row_arrive, 0)

        part = entry_count // 4

        def merge_rows(g, carry):
            at_rows = pl.ds(pl.multiple_of(g * part, part), part)
            few_rows = part // residues
            half = few_rows * g // RING
            first_at = lax.rem(few_rows * g, RING)
            gated = s["row_in"][half, pl.ds(first_at, few_rows)].reshape(part, features)
            here = e_ref[pl.ds(g * few_rows, few_rows)].reshape(part, features).astype(f32)
            here = here + jnp.dot(gated, rm_ref[...], preferred_element_type=f32)
            for k in range(features // lanes):
                s["by_lane"][k, at_rows] = here[:, k * lanes : (k + 1) * lanes]
            return carry

        lax.fori_loop(0, 4, merge_rows, 0)

        def turn_rows(g, carry):
            some = part // rows
            for i in range(some):
                at_rows = pl.ds(pl.multiple_of(g * part + i * rows, rows), rows)
                for k in range(features // lanes):
                    s["state"][at_rows, k * lanes : (k + 1) * lanes] = s["by_lane"][
                        k, pl.ds(g * some + i, rows, stride=residues)
                    ]
            here = normal(s["state"][pl.ds(pl.multiple_of(g * part, part), part)])
            s["col_sent"][pl.ds(g * some, some)] = here.reshape(some, rows, features)
            return carry

        lax.fori_loop(0, 4, turn_rows, 0)
        pair_of = lambda ref, k: ref.at[pl.ds(k * columns, columns)]
        rows_of = lambda ref, k: ref.at[:, pl.ds(pl.multiple_of(k * rows, rows), rows)]
        to_cols = Pushes("b", (s["col_sent"],), (s["cols"],), [pair_of], [rows_of], s["c1s"], s["c1r"])
        to_cols.start()
        halves = []
        for half in range(2):
            total = jnp.zeros((8, lanes), f32)
            for k in range(RING):
                total = total + cp_ref[half * RING + k].astype(f32)
            halves.append(total)
        s["there"][...] = jnp.concatenate(halves, axis=1)
        to_cols.finish()
        returns = []
        for r in range(columns):
            projected = jnp.dot(s["cols"][r], wc_ref[...], preferred_element_type=f32)
            s["q"][...] = (projected[:, :features] * PER_HEAD_WIDTH ** (-0.5)).astype(bf16)
            col_keys = projected[:, features : 2 * features].astype(bf16)
            col_values = projected[:, 2 * features : 3 * features].astype(bf16)
            s["g"][...] = jax.nn.sigmoid(projected[:, 3 * features :])
            col_present = s["there"][pl.ds(lax.rem(b, 4) * columns + r, 1)] > 0

            def col_block(t, carry):
                rows_at = pl.ds(pl.multiple_of(t * step, step), step)
                attended = heads_attend(s["q"][rows_at], col_keys, col_values, col_present, None)
                s["col_out"][r, rows_at] = (attended * s["g"][rows_at]).astype(bf16)
                return carry

            lax.fori_loop(0, GROUP * rows // step, col_block, 0)
            returns.append(
                Pushes(
                    "b",
                    (s["col_out"],),
                    (s["col_in"],),
                    [lambda ref, k, r=r: ref.at[r, pl.ds(pl.multiple_of(k * rows, rows), rows)]],
                    [lambda ref, k, r=r: ref.at[k * columns + r]],
                    s["c2s" if r == 0 else "c3s"],
                    s["c2r" if r == 0 else "c3r"],
                )
            )
            returns[-1].start()
        for back_again in returns:
            back_again.finish()

        ready("cm", "ex", "co", "p", "tri_in", "tri_out", "up", "down")

        def transition(g, carry):
            at_rows = pl.ds(pl.multiple_of(g * part, part), part)
            some = part // rows
            gated = s["col_in"][pl.ds(g * some, some)].reshape(part, features)
            here = s["state"][at_rows] + jnp.dot(gated, cm_ref[...], preferred_element_type=f32)
            hidden = jnp.dot(normal(here), ex_ref[...], preferred_element_type=f32)
            hidden = jnp.maximum(hidden, 0.0).astype(bf16)
            here = here + jnp.dot(hidden, co_ref[...], preferred_element_type=f32)
            for k in range(features // lanes):
                s["by_lane"][k, at_rows] = here[:, k * lanes : (k + 1) * lanes]
            factor = jnp.dot(normal(here), left_weights, preferred_element_type=f32)
            for q in range(some // per):
                piece = jnp.zeros((rows, lanes), f32)
                for m in range(per):
                    k = (q * per + m) * rows
                    piece = jnp.where(lane_at == m, factor[k : k + rows], piece)
                at_q = g * (some // per) + q
                cols = pl.ds(pl.multiple_of(at_q * lanes, lanes), lanes)
                l_ref[:, cols] = (piece * left_presence(at_q)).astype(bf16)
            return carry

        lax.fori_loop(0, 4, transition, 0)

        def turn_back(i, carry):
            at_rows = pl.ds(pl.multiple_of(i * residues, residues), residues)
            for k in range(features // lanes):
                here = s["by_lane"][k, pl.ds(i, residues, stride=rows)]
                s["again"][at_rows, k * lanes : (k + 1) * lanes] = here
                om_ref[i, :, k * lanes : (k + 1) * lanes] = here.astype(bf16)
            return carry

        lax.fori_loop(0, rows, turn_back, 0)
        for v in range(rows // per):
            some_rows = s["again"][v * lanes : (v + 1) * lanes]
            s["apart"][v] = lax.dot_general(
                fw_ref[...], normal(some_rows), (((0,), (1,)), ((), ())), preferred_element_type=f32
            )[side:]
            pieces = [s["apart"][v, pl.ds(m, 8, stride=per)] for m in range(per)]
            for n in range(per):
                piece = jnp.zeros((8, lanes), f32)
                for m in range(per):
                    shift = (side * (m - n)) % lanes
                    turned = pltpu.roll(pieces[m], shift, 1) if shift else pieces[m]
                    piece = jnp.where(lane_at == m, turned, piece)
                s["joined"][(v * per + n) * 8 : (v * per + n + 1) * 8] = piece
        for q in range(wide // lanes):
            cols = slice(q * lanes, (q + 1) * lanes)
            right = s["joined"][pl.ds(q, rows, stride=8)] * right_presence
            r_ref[:, cols] = right.astype(bf16)

        def to_chip(d, coming):
            block = back(d) * 2 + core if coming else b
            peer = back(d) if coming else lax.rem(chip + d, chips)
            return remote(l_ref, put(ol, block), s["ls"].at[d], s["lr"].at[d], on_core(peer))

        def to_twin(d, coming):
            block = put(ol, back(d) * 2 + (1 - core if coming else core))
            return remote(block, block, s["ts"].at[d], s["tr_"].at[d], twin)

        def forward(k, other, src):
            return remote(src, put(orr, b), s["fs"].at[k, other], s["fr"].at[b], (x, k, other, z))

        def forward_all(k, src):
            for other in range(2):
                mine = jnp.logical_and(own, jnp.logical_and(k == ro, x == other))

                @pl.when(jnp.logical_not(mine))
                def _():
                    forward(k, other, src).start()

                @pl.when(mine)
                def _():
                    put(orr, b)[...] = src[...]

        def start(d, carry):
            for copy in along.copies(d, False):
                copy.start()
            to_chip(d, False).start()
            return carry

        lax.fori_loop(1, RING, start, 0)
        first = remote(l_ref, put(ol, b), s["ts"].at[0], s["tr_"].at[0], twin)
        first.start()
        forward_all(z, r_ref)
        put(ol, b)[...] = l_ref[...]

        def relay(d, carry):
            along.arrive(d)
            k = along.sender(d)
            forward_all(k, s["stage"].at[k])
            to_chip(d, True).wait_recv()
            to_twin(d, False).start()
            return carry

        lax.fori_loop(1, RING, relay, 0)

        def left_in(d, carry):
            to_twin(d, True).wait_recv()
            return carry

        lax.fori_loop(0, RING, left_in, 0)

        def come(k, other):
            sender = other * RING + k
            there = put(orr, sender)
            remote(r_ref, there, s["fs"].at[k, other], s["fr"].at[sender], (other, k, br, z)).wait_recv()

        senders(come)

        lane_of = lax.broadcasted_iota(jnp.int32, (channels, lanes), 1) // side
        contract = (((0,), (0,)), ((), ()))

        def channel_push(k, g, d, coming):
            src, dst = (s["tl"], s["l1"]) if k == 0 else (s["tr"], s["r1"])
            cols = pl.ds(pl.multiple_of(g * chunk, chunk), chunk)
            peer = along.sender(d) if coming else lax.rem(z + d, RING)
            return remote(
                src.at[z if coming else peer, :, cols],
                dst.at[peer if coming else z, :, cols],
                s["p1s"].at[k, g, d],
                s["p1r"].at[k, g, d],
                (br, ro, x, peer),
            )

        def front(g, carry):
            cols = pl.ds(pl.multiple_of(g * chunk, chunk), chunk)
            outer = lax.dot_general(ol[:, cols], orr[...], contract, preferred_element_type=f32)
            outer = (outer * (1.0 / (GROUP * rows))).astype(bf16)
            stacked = jnp.concatenate(
                [
                    jnp.concatenate(
                        [
                            outer[i * side : (i + 1) * side, q * lanes : (q + 1) * lanes]
                            for q in range(wide // lanes)
                        ],
                        axis=0,
                    )
                    for i in range(chunk // side)
                ],
                axis=1,
            )
            mixed = lax.dot_general(mix_ref[...], stacked, contract, preferred_element_type=f32)
            pieces = []
            for h in range(chunk // lanes):
                piece = jnp.zeros((channels, lanes), f32)
                for i in range(per):
                    at_lane = (h * per + i) * lanes
                    total = None
                    for y in range(per):
                        part = mixed[y * channels : (y + 1) * channels, at_lane : at_lane + lanes]
                        shift = (side * (i - y)) % lanes
                        part = pltpu.roll(part, shift, 1) if shift else part
                        total = part if total is None else total + part
                    piece = jnp.where(lane_of == i, total, piece)
                pieces.append(piece)
            opm = jnp.transpose(p_ref[cols].astype(f32)) + jnp.concatenate(pieces, axis=1)
            s["opm"][:, cols] = opm
            normed = norm_channels(opm).astype(bf16)
            projected = lax.dot_general(in_ref[...], normed, contract, preferred_element_type=f32)
            block = lambda k: projected[k * channels : (k + 1) * channels]
            here = k_ref[:, cols]
            tri_left = (here * jax.nn.sigmoid(block(0)) * block(1)).astype(bf16)
            tri_right = (here * jax.nn.sigmoid(block(2)) * block(3)).astype(bf16)
            s["tl"][:, :, cols] = tri_left.reshape(RING, deep, chunk)
            s["tr"][:, :, cols] = tri_right.reshape(RING, deep, chunk)
            s["gate"][:, cols] = jax.nn.sigmoid(block(4))

            def push(d, carry):
                for k in range(2):
                    channel_push(k, g, d, False).start()
                return carry

            lax.fori_loop(1, RING, push, 0)
            return carry

        lax.fori_loop(0, chunks, front, 0)
        turn = s["turn"]

        def regroup(src, dst):
            outer, inner, _ = src.shape

            def one(v, carry):
                cols = pl.ds(pl.multiple_of(v * lanes, lanes), lanes)
                for g in range(outer):
                    turn[v, g * inner : (g + 1) * inner] = src[g, :, cols].astype(f32)
                for g in range(inner):
                    dst[g, :, cols] = turn[v, pl.ds(g, outer, stride=inner)].astype(bf16)
                return carry

            lax.fori_loop(0, tokens // lanes, one, 0)

        s["l1"][z] = s["tl"][z]
        s["r1"][z] = s["tr"][z]
        for k, ref in ((0, "l1"), (1, "r1")):

            def arrive(d, carry):
                for g in range(chunks):
                    channel_push(k, g, d, True).wait_recv()
                return carry

            lax.fori_loop(1, RING, arrive, 0)
            to = s["l2"] if k == 0 else s["r2"]
            regroup(s[ref], to)

        def over(d, coming):
            there = s["r3"].at[1 - x if coming else x, to_channel.sender(d)]
            return remote(there, there, s["xs"].at[d], s["xr"].at[d], cross)

        to_channel.start()
        first_over = remote(s["r2"].at[b], s["r3"].at[x, b], s["xs"].at[0], s["xr"].at[0], cross)
        first_over.start()

        def hand(d, carry):
            to_channel.arrive(d)
            over(d, False).start()
            return carry

        lax.fori_loop(1, GROUP, hand, 0)
        lane = lax.broadcasted_iota(jnp.int32, (few, lanes), 1) // side

        def unfold(block, put_line):
            def one(v, carry):
                t = block(pl.ds(pl.multiple_of(v * lanes, lanes), lanes)).astype(f32)
                t = t.reshape(GROUP * few, lanes)
                turned = [t] + [pltpu.roll(t, side * n, 1) for n in range(1, per)]
                for n in range(per):
                    line = []
                    for q in range(GROUP // per):
                        piece = jnp.zeros((few, lanes), f32)
                        for m in range(per):
                            k = (q * per + m) * few
                            piece = jnp.where(lane == m, turned[(m - n) % per][k : k + few], piece)
                        line.append(piece)
                    put_line(v * per + n, jnp.concatenate(line, axis=1))
                return carry

            lax.fori_loop(0, side // per, one, 0)

        lines = lambda i: pl.ds(pl.multiple_of(i * few, few), few)

        def put_left(i, line):
            s["a"][lines(i)] = line

        unfold(lambda cols: s["l3"][:, :, cols], put_left)
        a = s["a"][...].astype(bf16)
        to = lax.broadcasted_iota(jnp.int32, (tall, tall), 0)
        of = lax.broadcasted_iota(jnp.int32, (tall, tall), 1)
        order = (of == lax.rem(to, side) * few + to // side).astype(f32).astype(bf16)

        def multiply(h, carry):
            def put_right(j, line):
                s["b"][h, lines(j)] = line

            unfold(lambda cols: s["r3"][h, :, :, cols], put_right)
            t = jnp.dot(order, s["b"][h].astype(bf16), preferred_element_type=f32).astype(bf16)
            s["y"][:, pl.ds(pl.multiple_of(h * tall, tall), tall)] = lax.dot_general(
                a, t, (((1,), (1,)), ((), ())), preferred_element_type=f32
            )
            return carry

        multiply(x, 0)

        def over_in(d, carry):
            over(d, True).wait_recv()
            return carry

        lax.fori_loop(0, GROUP, over_in, 0)
        multiply(1 - x, 0)

        def fold(v, carry):
            cols = pl.ds(pl.multiple_of(v * lanes, lanes), lanes)
            y = s["y"][pl.ds(pl.multiple_of(v * per * few, per * few), per * few)]
            for q in range(across_k // lanes):
                t = y[:, q * lanes : (q + 1) * lanes]
                turned = [t] + [pltpu.roll(t, side * n, 1) for n in range(1, per)]
                for m in range(per):
                    piece = jnp.zeros((few, lanes), f32)
                    for n in range(per):
                        piece = jnp.where(
                            lane == n, turned[(n - m) % per][n * few : (n + 1) * few], piece
                        )
                    s["m0"][q * per + m, :, cols] = piece.astype(bf16)
            return carry

        lax.fori_loop(0, side // per, fold, 0)
        from_channel.start()
        from_channel.finish()
        regroup(s["m1"], s["m2"])
        from_ring.start()
        from_ring.finish()

        def end(g, carry):
            cols = pl.ds(pl.multiple_of(g * chunk, chunk), chunk)
            mixed = s["m3"][:, :, cols].astype(f32).reshape(channels, chunk)
            mixed = norm_channels(mixed).astype(bf16)
            mixed = lax.dot_general(out_ref[...], mixed, contract, preferred_element_type=f32)
            state = s["opm"][:, cols] + s["gate"][:, cols] * mixed
            normed = norm_channels(state).astype(bf16)
            hidden = lax.dot_general(up_ref[...], normed, contract, preferred_element_type=f32)
            hidden = jnp.maximum(hidden, 0.0).astype(bf16)
            update = lax.dot_general(hidden, down_ref[...], contract, preferred_element_type=f32)
            o_ref[cols] = (jnp.transpose(state) + update).astype(bf16)
            return carry

        lax.fori_loop(0, chunks, end, 0)

        def sent(d, carry):
            along.sent(d)
            for r in range(2):
                row_push(r, d, False).wait_send()
            to_chip(d, False).wait_send()
            to_twin(d, False).wait_send()
            for k in range(2):
                for g in range(chunks):
                    channel_push(k, g, d, False).wait_send()
            return carry

        lax.fori_loop(1, RING, sent, 0)
        first.wait_send()

        def forwarded(k, other):
            mine = jnp.logical_and(own, jnp.logical_and(k == ro, x == other))

            @pl.when(jnp.logical_not(mine))
            def _():
                forward(k, other, r_ref).wait_send()

        each(forwarded)

        def handed(d, carry):
            to_channel.sent(d)
            over(d, False).wait_send()
            return carry

        lax.fori_loop(1, GROUP, handed, 0)
        first_over.wait_send()

    scratch = [pltpu.VMEM(*v) for v in buffers.values()]
    scratch += [pltpu.SemaphoreType.DMA(v) for v in sems.values()]
    return call_exchange(
        kernel,
        [jax.ShapeDtypeStruct(entries.shape, bf16), jax.ShapeDtypeStruct((tokens, channels), bf16)],
        scratch, 6, 4 << 20,
        [IN_PLACE] * 11 + [IN_VMEM] + [IN_PLACE] * 3 + [IN_VMEM] + [IN_PLACE] * 3,
        whole_rows, bias, row_weights, row_merge, entries, col_presence, col_weights, col_merge, expand,
        contract_weights, factor_weights, presence, pair, outer_weights, tri_in, keep, tri_out, up, down,
    )


def on_device(
    homolog_embedding,
    pair_representation,
    alignment_entry_mask,
    residue_presence_mask,
    residue_chain_index,
    row_projection_weights,
    horizontal_attend_merge,
    pair_bias_matrix,
    same_chain_bias,
    column_projection_weights,
    vertical_attend_merge,
    homolog_mlp_expand,
    homolog_mlp_contract,
    tensor_product_linear,
    outer_output_matrix,
    triangle_input_weights,
    triangle_output_matrix,
    pair_up_weight,
    pair_down_weight,
):
    device_local_rows, residue_total, channel_count = homolog_embedding.shape
    pair_cols = pair_representation.shape[1]
    row_place = lax.axis_index(COL)
    col_place = lax.axis_index(("branch", "row"))
    chain_here = lax.dynamic_slice_in_dim(
        residue_chain_index, row_place * residue_total, residue_total
    )
    chain_there = lax.dynamic_slice_in_dim(residue_chain_index, col_place * pair_cols, pair_cols)
    residue_keep = residue_presence_mask.astype(jnp.float32)
    keep_here = lax.dynamic_slice_in_dim(residue_keep, row_place * residue_total, residue_total)
    keep_there = lax.dynamic_slice_in_dim(residue_keep, col_place * pair_cols, pair_cols)
    low_first = jnp.transpose(chain_here.reshape(residue_total // 8, 8))
    same_chain = (low_first[:, :, None] == chain_there[None, None, :]).astype(jnp.float32)
    full_bias, rows_whole, mask_cols = gather_bias_and_rows(
        pair_representation,
        jnp.transpose(pair_bias_matrix),
        same_chain.reshape(8, residue_total // 8 * pair_cols),
        same_chain_bias,
        homolog_embedding,
        alignment_entry_mask,
    )
    tokens = residue_total * pair_cols
    pair_keep = (keep_here[:, None] * keep_there[None, :]).reshape(1, tokens)
    msa_out, updated_pair_state = both_stacks(
        rows_whole,
        full_bias,
        row_projection_weights,
        horizontal_attend_merge,
        homolog_embedding,
        mask_cols,
        column_projection_weights,
        vertical_attend_merge,
        homolog_mlp_expand,
        homolog_mlp_contract,
        tensor_product_linear,
        alignment_entry_mask,
        pair_representation.reshape(tokens, CZ),
        outer_output_matrix,
        triangle_input_weights,
        pair_keep,
        triangle_output_matrix,
        pair_up_weight,
        pair_down_weight,
    )
    updated_pair_state = updated_pair_state.reshape(residue_total, pair_cols, CZ)
    return (msa_out, updated_pair_state)


def solution(mesh):
    split = Mesh(
        mesh.devices.reshape(mesh.shape["branch"], mesh.shape["row"], 2, 8),
        ("branch", "row", "col_0", "col_1"),
    )
    in_specs = (
        P(("branch", "row"), COL, None),
        P(COL, ("branch", "row"), None),
        P(("branch", "row"), COL),
        P(),
        P(),
        P(),
        P(),
        P(),
        P(),
        P(),
        P(),
        P(),
        P(),
        P(),
        P(),
        P(),
        P(),
        P(),
        P(),
    )
    out_specs = (P(("branch", "row"), COL, None), P(COL, ("branch", "row"), None))
    return jax.shard_map(
        on_device, mesh=split, in_specs=in_specs, out_specs=out_specs, check_vma=False
    )
```

```python
import jax
import jax.numpy as jnp
from jax import lax
from jax.experimental import pallas as pl
from jax.experimental.pallas import tpu as pltpu
from jax.sharding import Mesh
from jax.sharding import PartitionSpec as P

HEADS = 8
PER_HEAD_WIDTH = 32
CZ = 128
PRODUCT_FEATURES = 32
COL = ("col_0", "col_1")


EPSILON = 1e-05
NEGATIVE = -1000000000.0


MESH = pl.DeviceIdType.MESH
GROUP = 16
RING = 8
SIZES = {"b": 16, "c": 16, "z": 8}


def place():
    axes = [lax.axis_index(a) for a in ("branch", "row", *COL)]
    return (*axes, axes[0] * 8 + axes[1], axes[2] * 8 + axes[3])


def across(b, c):
    return (b // 8, lax.rem(b, 8), c // 8, lax.rem(c, 8))


def remote(src, dst, send, recv, to):
    return pltpu.make_async_remote_copy(
        src_ref=src, dst_ref=dst, send_sem=send, recv_sem=recv, device_id=to, device_id_type=MESH
    )


IN_VMEM = pl.BlockSpec(memory_space=pltpu.VMEM)
IN_SMEM = pl.BlockSpec(memory_space=pltpu.SMEM)
IN_PLACE = pl.BlockSpec(memory_space=pl.ANY)


def call_exchange(kernel, out_shape, scratch, collective_id, sent, specs, *args):
    return pl.pallas_call(
        kernel,
        out_shape=out_shape,
        in_specs=specs,
        out_specs=jax.tree.map(lambda _: IN_VMEM, out_shape),
        scratch_shapes=scratch,
        compiler_params=pltpu.CompilerParams(
            collective_id=collective_id, has_side_effects=True, vmem_limit_bytes=62 << 20
        ),
        cost_estimate=pl.CostEstimate(flops=0, bytes_accessed=2 * sent, transcendentals=0),
    )(*args)


class Pushes:
    def __init__(self, over, ins, outs, picks, puts, send, recv):
        br, ro, x, z, b, c = place()
        self.count = SIZES[over]
        self.me, self.device = {
            "b": (b, lambda k: across(k, c)),
            "c": (c, lambda k: across(b, k)),
            "z": (z, lambda k: (br, ro, x, k)),
        }[over]
        self.parts = list(zip(ins, outs, picks, puts))
        self.send, self.recv = send, recv

    def greet(self, barrier):
        def one(d, carry):
            to = self.device(lax.rem(self.me + d, self.count))
            pl.semaphore_signal(barrier, inc=1, device_id=to, device_id_type=MESH)
            return carry

        lax.fori_loop(1, self.count, one, 0)

    def sender(self, d):
        return lax.rem(self.me + (self.count - d), self.count)

    def copies(self, d, coming):
        peer = self.sender(d) if coming else lax.rem(self.me + d, self.count)
        for k, (src, dst, pick, put) in enumerate(self.parts):
            yield remote(
                pick(src, self.me if coming else peer),
                put(dst, peer if coming else self.me),
                self.send.at[k, d],
                self.recv.at[k, d],
                self.device(peer),
            )

    def start(self):
        def one(d, carry):
            for copy in self.copies(d, False):
                copy.start()
            return carry

        lax.fori_loop(1, self.count, one, 0)
        for src, dst, pick, put in self.parts:
            put(dst, self.me)[...] = pick(src, self.me)[...]

    def arrive(self, d):
        for copy in self.copies(d, True):
            copy.wait_recv()

    def sent(self, d):
        for copy in self.copies(d, False):
            copy.wait_send()

    def finish(self):
        def one(d, carry):
            self.arrive(d)
            self.sent(d)
            return carry

        lax.fori_loop(1, self.count, one, 0)


def crosswise():
    br, ro, x, z = place()[:4]
    return (br, ro, 1 - x, z)


def normal(x):
    x = x.astype(jnp.float32)
    centre = x - jnp.mean(x, axis=-1, keepdims=True)
    spread = jnp.mean(centre * centre, axis=-1, keepdims=True)
    return (centre * lax.rsqrt(spread + EPSILON)).astype(jnp.bfloat16)


def bias_and_rows(pair, weights, entries, residues):
    some, others = residues, residues
    pair_channels = pair.shape[1]
    heads = weights.shape[0]
    msa_rows, _, channels = entries.shape
    carried = heads // 2
    tall = some + 8
    lanes = 128
    fold = lanes // others
    n_copies = 32

    def kernel(
        p_ref, w_ref, s_ref, h_ref, e_ref, k_ref, pair_ready, entries_ready, entered,
        ob_ref, or_ref, om_ref, m_ref, turn, tile, tiles, rows, bsend, brecv, psend, precv, xsend, xrecv, rsend, rrecv,
    ):
        br, ro, x, z, _, c = place()
        core = lax.rem(ro, 2)
        right = (br, ro, x, lax.rem(z + 1, RING))
        left = (br, ro, x, lax.rem(z + RING - 1, RING))
        twin = (br, ro + 1 - 2 * core, x, z)
        cross = crosswise()
        at = lambda ref, k: ref.at[k]
        put = lambda ref, k: ref.at[:, x * RING + k]
        spread = Pushes(
            "b", (tile, m_ref), (tiles, om_ref), [lambda ref, k: ref, lambda ref, k: ref.at[k // 4]], [at] * 2, bsend, brecv
        )
        pushes = Pushes("z", (rows,), (or_ref,), [lambda ref, k: ref.at[:, k]], [put], psend, precv)
        barrier = pltpu.get_barrier_semaphore()
        spread.greet(barrier)
        pushes.greet(barrier)
        pl.semaphore_signal(barrier, inc=1, device_id=cross, device_id_type=MESH)

        present = k_ref[...].astype(jnp.float32)
        spot = lax.broadcasted_iota(jnp.int32, (msa_rows, lanes), 0)
        wide_lane = lax.broadcasted_iota(jnp.int32, (msa_rows, lanes), 1)
        copies_of = (lax.rem(wide_lane, msa_rows) == spot).astype(jnp.float32)
        by_residue = lax.dot_general(
            present, copies_of, (((0,), (0,)), ((), ())), preferred_element_type=jnp.float32
        )
        mine = lax.broadcasted_iota(jnp.int32, (some, lanes), 1) // msa_rows == lax.rem(br * 8 + ro, 8)
        by_residue = jnp.where(mine, by_residue, 0.0).astype(jnp.bfloat16)
        for k in range(some // 8):
            m_ref[k] = by_residue[k * 8 : (k + 1) * 8]
        spot = lax.broadcasted_iota(jnp.int32, (some, channels), 0)
        wide_lane = lax.broadcasted_iota(jnp.int32, (some, channels), 1)
        here = jnp.logical_and(lax.rem(wide_lane, some) == spot, wide_lane // some == z)
        by_row = jnp.dot(present, here.astype(jnp.float32), preferred_element_type=jnp.float32)
        head_of = lax.broadcasted_iota(jnp.int32, (heads, lanes), 0)
        chain = jnp.zeros((heads, lanes), jnp.float32)
        for head in range(heads):
            chain = jnp.where(head_of == head, h_ref[head], chain)
        pair_ready()
        normed = normal(p_ref[...].reshape(some * others, pair_channels))
        for low in range(8):
            tokens = jnp.concatenate(
                [normed[(high * 8 + low) * others :][:others] for high in range(fold)], axis=0
            )
            bias = lax.dot_general(
                w_ref[...], tokens, (((1,), (1,)), ((), ())), preferred_element_type=jnp.float32
            )
            turn[low * heads : (low + 1) * heads] = bias + chain * s_ref[low : low + 1]
        for head in range(heads):
            tile[head] = turn[pl.ds(head, 8, stride=heads)].astype(jnp.bfloat16)
        entered()
        spread.start()
        entries_ready()
        normed = normal(e_ref[...].reshape(msa_rows * some, channels))
        for half in range(2):
            for k in range(RING):
                row = half * RING + k
                rows[half, k, :some] = normed[row * some : (row + 1) * some]
                rows[half, k, some:] = jnp.broadcast_to(by_row[row : row + 1], (8, channels)).astype(jnp.bfloat16)
        pushes.start()
        first = remote(rows.at[:, z], or_ref.at[:, c], xsend.at[0], xrecv.at[0], cross)
        first.start()
        spread.finish()
        lane = lax.broadcasted_iota(jnp.int32, (8, lanes), 1) // others

        def set_out(head, carry):
            t = tiles[:, head].astype(jnp.float32).reshape(GROUP * 8, lanes)
            turned = [t] + [pltpu.roll(t, others * s, 1) for s in range(1, fold)]
            lines = []
            for n in range(fold):
                line = []
                for q in range(GROUP // fold):
                    piece = jnp.zeros((8, lanes), jnp.float32)
                    for m in range(fold):
                        k = (q * fold + m) * 8
                        piece = jnp.where(lane == m, turned[(m - n) % fold][k : k + 8], piece)
                    line.append(piece)
                lines.append(jnp.concatenate(line, axis=1))
            whole = jnp.concatenate(lines, axis=0).astype(jnp.bfloat16)
            ob_ref[head, pl.ds(pl.multiple_of(z * some, some), some)] = whole
            return carry

        lax.fori_loop(0, heads, set_out, 0)

        def view(block, half, mine):
            at_head, count = mine * carried, carried
            if half is not None:
                count = carried // 2
                at_head = at_head + half * count
            rows_at = pl.multiple_of(lax.rem(block + RING, RING) * some, some)
            return ob_ref.at[pl.ds(at_head, count), pl.ds(rows_at, some)]

        copies, handed = [], []

        def push(block, half, to):
            k = len(copies)
            there = view(block, half, core)
            copies.append(remote(there, there, rsend.at[k], rrecv.at[k], to))
            copies[-1].start()
            return k

        def arrived(k, block, half):
            there = view(block, half, core)
            remote(there, there, rsend.at[k], rrecv.at[k], right).wait_recv()

        def hand(block, half):
            handed.append((push(block, half, twin), block, half))

        def over(d, coming):
            k = pushes.sender(d)
            there = or_ref.at[:, (1 - x if coming else x) * RING + k]
            return remote(there, there, xsend.at[d], xrecv.at[d], cross)

        for step in (1, 2, 3):
            for d in (step, RING - step):
                pushes.arrive(d)
                over(d, False).start()
            if step == 1:
                going = {+1: push(z, None, right), -1: push(z, None, left)}
            coming = {}
            for way, to in ((+1, right), (-1, left)):
                block = z - way * step
                arrived(going[way], block, None)
                half = None if step < 3 else (0 if way > 0 else 1)
                coming[way] = push(block, half, to)
                hand(block, None)
            going = coming
        pushes.arrive(4)
        over(4, False).start()
        for way in (+1, -1):
            half = 0 if way > 0 else 1
            arrived(going[way], z - way * 4, half)
            hand(z - way * 4, half)
        for k, block, half in handed:
            there = view(block, half, 1 - core)
            remote(there, there, rsend.at[k], rrecv.at[k], twin).wait_recv()
        for d in range(RING):
            over(d, True).wait_recv()
        for copy in copies:
            copy.wait_send()
        first.wait_send()
        for d in range(1, RING):
            pushes.sent(d)
            over(d, False).wait_send()

    wide = GROUP * others
    bf16 = jnp.bfloat16
    arrays = [
        ((heads, RING * some, wide), bf16),
        ((2, GROUP, tall, channels), bf16),
        ((GROUP, 8, lanes), bf16),
        ((some // 8, 8, lanes), bf16),
        ((8 * heads, lanes), jnp.float32),
        ((heads, 8, lanes), bf16),
        ((GROUP, heads, 8, lanes), bf16),
        ((2, RING, tall, channels), bf16),
    ]
    scratch = [pltpu.VMEM(*v) for v in arrays]
    scratch += [pltpu.SemaphoreType.DMA((2, GROUP))] * 2
    scratch += [pltpu.SemaphoreType.DMA((1, RING))] * 2
    scratch += [pltpu.SemaphoreType.DMA((RING,))] * 2
    scratch += [pltpu.SemaphoreType.DMA((n_copies,))] * 2
    return kernel, scratch


def heads_attend(queries, keys, values, present, bias_of):
    lanes = 128
    per = lanes // PER_HEAD_WIDTH
    lane = lax.broadcasted_iota(jnp.int32, (1, lanes), 1) // PER_HEAD_WIDTH
    blocks = []
    for block in range(HEADS // per):
        cols = slice(block * lanes, (block + 1) * lanes)
        total = jnp.zeros((queries.shape[0], lanes), jnp.float32)
        for h in range(per):
            here = (lane == h).astype(jnp.float32)
            query = queries[:, cols] * here.astype(jnp.bfloat16)
            scores = lax.dot_general(
                query, keys[:, cols], (((1,), (1,)), ((), ())), preferred_element_type=jnp.float32
            )
            if bias_of is not None:
                scores = scores + bias_of(block * per + h).astype(jnp.float32)
            scores = jnp.where(present, scores, NEGATIVE)
            powers = jnp.exp(scores - jnp.max(scores, axis=-1, keepdims=True))
            totals = jnp.sum(powers, axis=-1, keepdims=True)
            summed = jnp.dot(
                powers.astype(jnp.bfloat16), values[:, cols], preferred_element_type=jnp.float32
            )
            total = total + (summed / totals) * here
        blocks.append(total)
    return jnp.concatenate(blocks, axis=1)


def norm_channels(x):
    centre = x - jnp.mean(x, axis=0, keepdims=True)
    spread = jnp.mean(centre * centre, axis=0, keepdims=True)
    return centre * lax.rsqrt(spread + EPSILON)


def whole_block(
    bias_weights, same, chain_bias, row_weights, row_merge, entries, col_weights, col_merge, expand,
    contract_weights, factor_weights, presence, pair, outer_weights, tri_in, keep, tri_out, up, down,
):
    rows, residues, features = entries.shape
    wide = residues * PRODUCT_FEATURES
    entry_count = rows * residues
    columns = residues // GROUP
    queries = RING * residues
    keys_count = GROUP * residues
    step = 128
    tokens, channels = pair.shape
    lanes = 128
    side = PRODUCT_FEATURES
    per = lanes // side
    chips = GROUP // 2
    few = RING
    deep = channels // RING
    chunk = 8 * side
    chunks = wide // chunk
    tall = few * side
    across_k = GROUP * side
    bf16, f32 = jnp.bfloat16, jnp.float32
    inputs = dict(
        p=pair, e=entries, wr=row_weights, ow=outer_weights, rm=row_merge, wc=col_weights,
        cm=col_merge, ex=expand, co=contract_weights, fw=factor_weights, tri_in=tri_in, tri_out=tri_out, up=up,
        down=down,
    )
    buffers = {
        **{"in_" + name: (value.shape, value.dtype) for name, value in inputs.items()},
        "mix": ((PRODUCT_FEATURES * PRODUCT_FEATURES // 4, 4 * channels), bf16),
        "outer_f32": (outer_weights.shape, f32),
        "there": ((8, 2 * lanes), f32),
        "q": ((queries, features), bf16),
        "g": ((queries, features), f32),
        "row_out": ((2, RING, residues, features), bf16),
        "row_in": ((2, RING, residues, features), bf16),
        "by_lane": ((features // 128, entry_count, 128), f32),
        "state": ((entry_count, features), f32),
        "again": ((entry_count, features), f32),
        "col_sent": ((residues, rows, features), bf16),
        "cols": ((columns, GROUP * rows, features), bf16),
        "col_out": ((columns, GROUP * rows, features), bf16),
        "col_in": ((residues, rows, features), bf16),
        "apart": ((rows // 4, PRODUCT_FEATURES, 128), f32),
        "joined": ((rows * 8, 128), f32),
        "left": ((rows, wide), bf16),
        "right": ((rows, wide), bf16),
        "stage": ((RING, rows, wide), bf16),
        "all_left": ((GROUP * rows, wide), bf16),
        "all_right": ((GROUP * rows, wide), bf16),
        "opm": ((channels, tokens), f32),
        "gate": ((channels, tokens), f32),
        "tl": ((RING, deep, tokens), bf16),
        "tr": ((RING, deep, tokens), bf16),
        "l1": ((RING, deep, tokens), bf16),
        "r1": ((RING, deep, tokens), bf16),
        "turn": ((tokens // lanes, channels, lanes), f32),
        "l2": ((GROUP, few, tokens), bf16),
        "r2": ((GROUP, few, tokens), bf16),
        "l3": ((GROUP, few, tokens), bf16),
        "r3": ((2, GROUP, few, tokens), bf16),
        "a": ((tall, across_k), f32),
        "b": ((2, tall, across_k), f32),
        "y": ((tall, across_k), f32),
        "m0": ((GROUP, few, tokens), bf16),
        "m1": ((GROUP, few, tokens), bf16),
        "m2": ((RING, deep, tokens), bf16),
        "m3": ((RING, deep, tokens), bf16),
    }
    sems = {
        "load": (len(inputs),),
        "rs": (2, RING), "rr": (2, RING), "c1s": (1, GROUP), "c1r": (1, GROUP),
        "c2s": (1, GROUP), "c2r": (1, GROUP), "c3s": (1, GROUP), "c3r": (1, GROUP),
        "zs": (1, RING), "zr": (1, RING), "ls": (RING,), "lr": (RING,), "ts": (RING,), "tr_": (RING,),
        "fs": (RING, 2), "fr": (GROUP,), "p1s": (2, chunks, RING), "p1r": (2, chunks, RING),
        "p2s": (2, GROUP), "p2r": (2, GROUP), "xs": (GROUP,), "xr": (GROUP,),
        "p3s": (1, GROUP), "p3r": (1, GROUP), "p4s": (1, RING), "p4r": (1, RING),
    }
    names = [*buffers, *sems]
    first_part, first_scratch = bias_and_rows(pair, bias_weights, entries, residues)

    def kernel(
        bw_ref, same_ref, chain_ref, wr_in, rm_in, e_in, wc_in, cm_in, ex_in, co_in, fw_in, pr_ref,
        p_in, ow_in, in_in, k_ref, out_in, up_in, down_in, om_ref, o_ref, *scratch,
    ):
        s = dict(zip(names, scratch))
        loads = {}
        for n, (name, ref) in enumerate(
            dict(
                p=p_in, e=e_in, wr=wr_in, ow=ow_in, rm=rm_in, wc=wc_in, cm=cm_in, ex=ex_in,
                co=co_in, fw=fw_in, tri_in=in_in, tri_out=out_in, up=up_in, down=down_in,
            ).items()
        ):
            loads[name] = pltpu.make_async_copy(ref, s["in_" + name], s["load"].at[n])
            loads[name].start()
        wr_ref, ow_ref, e_ref, rm_ref, wc_ref, cm_ref, ex_ref, co_ref, fw_ref, p_ref = (
            s["in_" + n] for n in ("wr", "ow", "e", "rm", "wc", "cm", "ex", "co", "fw", "p")
        )
        of_first = scratch[len(names) :]
        b_ref, w_ref, cp_ref = of_first[:3]
        in_ref, out_ref, up_ref, down_ref = (s["in_" + n] for n in ("tri_in", "tri_out", "up", "down"))
        mix_ref = s["mix"]

        def ready(*wanted):
            for name in wanted:
                loads[name].wait()

        l_ref, r_ref = s["left"], s["right"]
        br, ro, x, z, b, _ = place()
        core = lax.rem(ro, 2)
        chip = b // 2
        twin = (br, ro + 1 - 2 * core, x, z)
        cross = crosswise()
        put = lambda ref, k: ref.at[pl.ds(pl.multiple_of(k * rows, rows), rows)]
        at = lambda ref, k: ref.at[k]
        whole = lambda ref, k: ref
        ol, orr = s["all_left"], s["all_right"]
        along = Pushes("z", (r_ref,), (s["stage"],), [whole], [at], s["zs"], s["zr"])
        on_core = lambda k: across(k * 2 + core, x * RING + z)
        back = lambda d: lax.rem(chip + chips - d, chips)
        own = br == x

        def each(act):
            def one(d, carry):
                for other in range(2):
                    act(lax.rem(ro + d, RING), other)
                return carry

            lax.fori_loop(0, RING, one, 0)

        def senders(act):
            def one(k, other):
                @pl.when(jnp.logical_not(jnp.logical_and(own, jnp.logical_and(k == ro, br == other))))
                def _():
                    act(k, other)

            each(one)

        to_channel = Pushes(
            "b", (s["l2"], s["r2"]), (s["l3"], s["r3"]), [at] * 2, [at, lambda ref, k: ref.at[x, k]],
            s["p2s"], s["p2r"],
        )
        from_channel = Pushes("b", (s["m0"],), (s["m1"],), [at], [at], s["p3s"], s["p3r"])
        from_ring = Pushes("z", (s["m2"],), (s["m3"],), [at], [at], s["p4s"], s["p4r"])

        barrier = pltpu.get_barrier_semaphore()
        along.greet(barrier)
        to_channel.greet(barrier)

        def signal(to):
            pl.semaphore_signal(barrier, inc=1, device_id=to, device_id_type=MESH)

        signal(cross)
        senders(lambda k, other: signal((other, k, br, z)))
        lane_at = lax.broadcasted_iota(jnp.int32, (1, lanes), 1) // side

        def entered():
            others = jnp.where(own, GROUP - 1, GROUP)
            pl.semaphore_wait(barrier, 2 * (RING - 1 + GROUP - 1 + 1) + others)

        first_part(
            p_ref, bw_ref, same_ref, chain_ref, e_ref, pr_ref,
            lambda: ready("p"), lambda: ready("e"), entered, *of_first,
        )

        def row_push(r, d, coming):
            peer = along.sender(d) if coming else lax.rem(z + d, RING)
            return remote(
                s["row_out"].at[r, z if coming else peer],
                s["row_in"].at[r, peer if coming else z],
                s["rs"].at[r, d],
                s["rr"].at[r, d],
                (br, ro, x, peer),
            )

        ready("wr")
        for r in range(2):
            whole_row = w_ref[r, :, :residues].reshape(keys_count, features)
            keys_values = jnp.dot(
                whole_row, wr_ref[:, features : 3 * features], preferred_element_type=f32
            ).astype(bf16)
            keys, values = keys_values[:, :features], keys_values[:, features:]
            half_row = w_ref[r, pl.ds(x * RING, RING), :residues].reshape(queries, features)
            q = jnp.dot(half_row, wr_ref[:, :features], preferred_element_type=f32)
            s["q"][...] = (q * PER_HEAD_WIDTH ** (-0.5)).astype(bf16)
            gate = jnp.dot(half_row, wr_ref[:, 3 * features :], preferred_element_type=f32)
            s["g"][...] = jax.nn.sigmoid(gate)
            present = []
            for half in range(2):
                total = jnp.zeros((8, features), f32)
                for k in range(RING):
                    total = total + w_ref[r, half * RING + k, residues:].astype(f32)
                present.append(total[:1])
            present = jnp.concatenate(present, axis=1) > 0

            def row_block(t, carry):
                t = lax.rem(t + 1 - z // 4, 2)
                rows_at = pl.ds(pl.multiple_of(t * step, step), step)
                attended = heads_attend(
                    s["q"][rows_at], keys, values, present, lambda h: b_ref[h, rows_at, :]
                )
                gated = (attended * s["g"][rows_at]).astype(bf16)
                some = step // residues
                s["row_out"][r, pl.ds(t * some, some)] = gated.reshape(some, residues, features)

                def push(k, carry):
                    d = lax.rem(t * some + k - z + RING, RING)

                    @pl.when(d != 0)
                    def _():
                        row_push(r, d, False).start()

                    return carry

                lax.fori_loop(0, some, push, 0)
                return carry

            lax.fori_loop(0, queries // step, row_block, 0)
            s["row_in"][r, z] = s["row_out"][r, z]

        ready("ow", "rm", "wc", "fw")
        s["outer_f32"][...] = ow_ref[...].astype(f32)
        for q in range(PRODUCT_FEATURES // 4):
            for y in range(4):
                mix_ref[q * side : (q + 1) * side, y * channels : (y + 1) * channels] = s["outer_f32"][
                    pl.ds(q * 4 + y, side, stride=PRODUCT_FEATURES)
                ].astype(bf16)
        copied = lax.broadcasted_iota(jnp.int32, (2 * side, lanes), 0)
        copied_to = lax.rem(lax.broadcasted_iota(jnp.int32, (2 * side, lanes), 1), side)
        copied = (copied == copied_to).astype(f32).astype(bf16)
        left_weights = lax.dot_general(
            copied, fw_ref[...], (((0,), (0,)), ((), ())), preferred_element_type=f32
        ).astype(bf16)
        present = pr_ref[...].astype(f32)
        spot = lax.broadcasted_iota(jnp.int32, (residues, lanes), 0)
        wide_lane = lax.broadcasted_iota(jnp.int32, (residues, lanes), 1)
        beside = (lax.rem(wide_lane, residues) == spot).astype(f32)
        right_presence = jnp.dot(present, beside, preferred_element_type=f32)

        def left_presence(q):
            spread = jnp.logical_and(spot // per == q, wide_lane // side == lax.rem(spot, per))
            return jnp.dot(present, spread.astype(f32), preferred_element_type=f32)

        def row_arrive(d, carry):
            for r in range(2):
                row_push(r, d, True).wait_recv()
            return carry

        lax.fori_loop(1, RING, row_arrive, 0)

        part = entry_count // 4

        def merge_rows(g, carry):
            at_rows = pl.ds(pl.multiple_of(g * part, part), part)
            few_rows = part // residues
            half = few_rows * g // RING
            first_at = lax.rem(few_rows * g, RING)
            gated = s["row_in"][half, pl.ds(first_at, few_rows)].reshape(part, features)
            here = e_ref[pl.ds(g * few_rows, few_rows)].reshape(part, features).astype(f32)
            here = here + jnp.dot(gated, rm_ref[...], preferred_element_type=f32)
            for k in range(features // lanes):
                s["by_lane"][k, at_rows] = here[:, k * lanes : (k + 1) * lanes]
            return carry

        lax.fori_loop(0, 4, merge_rows, 0)

        def turn_rows(g, carry):
            some = part // rows
            for i in range(some):
                at_rows = pl.ds(pl.multiple_of(g * part + i * rows, rows), rows)
                for k in range(features // lanes):
                    s["state"][at_rows, k * lanes : (k + 1) * lanes] = s["by_lane"][
                        k, pl.ds(g * some + i, rows, stride=residues)
                    ]
            here = normal(s["state"][pl.ds(pl.multiple_of(g * part, part), part)])
            s["col_sent"][pl.ds(g * some, some)] = here.reshape(some, rows, features)
            return carry

        lax.fori_loop(0, 4, turn_rows, 0)
        pair_of = lambda ref, k: ref.at[pl.ds(k * columns, columns)]
        rows_of = lambda ref, k: ref.at[:, pl.ds(pl.multiple_of(k * rows, rows), rows)]
        to_cols = Pushes("b", (s["col_sent"],), (s["cols"],), [pair_of], [rows_of], s["c1s"], s["c1r"])
        to_cols.start()
        halves = []
        for half in range(2):
            total = jnp.zeros((8, lanes), f32)
            for k in range(RING):
                total = total + cp_ref[half * RING + k].astype(f32)
            halves.append(total)
        s["there"][...] = jnp.concatenate(halves, axis=1)
        to_cols.finish()
        returns = []
        for r in range(columns):
            projected = jnp.dot(s["cols"][r], wc_ref[...], preferred_element_type=f32)
            s["q"][...] = (projected[:, :features] * PER_HEAD_WIDTH ** (-0.5)).astype(bf16)
            col_keys = projected[:, features : 2 * features].astype(bf16)
            col_values = projected[:, 2 * features : 3 * features].astype(bf16)
            s["g"][...] = jax.nn.sigmoid(projected[:, 3 * features :])
            col_present = s["there"][pl.ds(lax.rem(b, 4) * columns + r, 1)] > 0

            def col_block(t, carry):
                rows_at = pl.ds(pl.multiple_of(t * step, step), step)
                attended = heads_attend(s["q"][rows_at], col_keys, col_values, col_present, None)
                s["col_out"][r, rows_at] = (attended * s["g"][rows_at]).astype(bf16)
                return carry

            lax.fori_loop(0, GROUP * rows // step, col_block, 0)
            returns.append(
                Pushes(
                    "b",
                    (s["col_out"],),
                    (s["col_in"],),
                    [lambda ref, k, r=r: ref.at[r, pl.ds(pl.multiple_of(k * rows, rows), rows)]],
                    [lambda ref, k, r=r: ref.at[k * columns + r]],
                    s["c2s" if r == 0 else "c3s"],
                    s["c2r" if r == 0 else "c3r"],
                )
            )
            returns[-1].start()
        for back_again in returns:
            back_again.finish()

        ready("cm", "ex", "co", "tri_in", "tri_out", "up", "down")

        def transition(g, carry):
            at_rows = pl.ds(pl.multiple_of(g * part, part), part)
            some = part // rows
            gated = s["col_in"][pl.ds(g * some, some)].reshape(part, features)
            here = s["state"][at_rows] + jnp.dot(gated, cm_ref[...], preferred_element_type=f32)
            hidden = jnp.dot(normal(here), ex_ref[...], preferred_element_type=f32)
            hidden = jnp.maximum(hidden, 0.0).astype(bf16)
            here = here + jnp.dot(hidden, co_ref[...], preferred_element_type=f32)
            for k in range(features // lanes):
                s["by_lane"][k, at_rows] = here[:, k * lanes : (k + 1) * lanes]
            factor = lax.dot_general(
                normal(here), left_weights, (((1,), (1,)), ((), ())), preferred_element_type=f32
            )
            for q in range(some // per):
                piece = jnp.zeros((rows, lanes), f32)
                for m in range(per):
                    k = (q * per + m) * rows
                    piece = jnp.where(lane_at == m, factor[k : k + rows], piece)
                at_q = g * (some // per) + q
                cols = pl.ds(pl.multiple_of(at_q * lanes, lanes), lanes)
                l_ref[:, cols] = (piece * left_presence(at_q)).astype(bf16)
            return carry

        lax.fori_loop(0, 4, transition, 0)

        def turn_back(i, carry):
            at_rows = pl.ds(pl.multiple_of(i * residues, residues), residues)
            for k in range(features // lanes):
                here = s["by_lane"][k, pl.ds(i, residues, stride=rows)]
                s["again"][at_rows, k * lanes : (k + 1) * lanes] = here
                om_ref[i, :, k * lanes : (k + 1) * lanes] = here.astype(bf16)
            return carry

        lax.fori_loop(0, rows, turn_back, 0)
        for v in range(rows // per):
            some_rows = s["again"][v * lanes : (v + 1) * lanes]
            s["apart"][v] = lax.dot_general(
                fw_ref[...], normal(some_rows), (((1,), (1,)), ((), ())), preferred_element_type=f32
            )[side:]
            pieces = [s["apart"][v, pl.ds(m, 8, stride=per)] for m in range(per)]
            for n in range(per):
                piece = jnp.zeros((8, lanes), f32)
                for m in range(per):
                    shift = (side * (m - n)) % lanes
                    turned = pltpu.roll(pieces[m], shift, 1) if shift else pieces[m]
                    piece = jnp.where(lane_at == m, turned, piece)
                s["joined"][(v * per + n) * 8 : (v * per + n + 1) * 8] = piece
        for q in range(wide // lanes):
            cols = slice(q * lanes, (q + 1) * lanes)
            right = s["joined"][pl.ds(q, rows, stride=8)] * right_presence
            r_ref[:, cols] = right.astype(bf16)

        def to_chip(d, coming):
            block = back(d) * 2 + core if coming else b
            peer = back(d) if coming else lax.rem(chip + d, chips)
            return remote(l_ref, put(ol, block), s["ls"].at[d], s["lr"].at[d], on_core(peer))

        def to_twin(d, coming):
            block = put(ol, back(d) * 2 + (1 - core if coming else core))
            return remote(block, block, s["ts"].at[d], s["tr_"].at[d], twin)

        def forward(k, other, src):
            return remote(src, put(orr, b), s["fs"].at[k, other], s["fr"].at[b], (x, k, other, z))

        def forward_all(k, src):
            for other in range(2):
                mine = jnp.logical_and(own, jnp.logical_and(k == ro, x == other))

                @pl.when(jnp.logical_not(mine))
                def _():
                    forward(k, other, src).start()

                @pl.when(mine)
                def _():
                    put(orr, b)[...] = src[...]

        def start(d, carry):
            for copy in along.copies(d, False):
                copy.start()
            to_chip(d, False).start()
            return carry

        lax.fori_loop(1, RING, start, 0)
        first = remote(l_ref, put(ol, b), s["ts"].at[0], s["tr_"].at[0], twin)
        first.start()
        forward_all(z, r_ref)
        put(ol, b)[...] = l_ref[...]

        def relay(d, carry):
            along.arrive(d)
            k = along.sender(d)
            forward_all(k, s["stage"].at[k])
            to_chip(d, True).wait_recv()
            to_twin(d, False).start()
            return carry

        lax.fori_loop(1, RING, relay, 0)

        def left_in(d, carry):
            to_twin(d, True).wait_recv()
            return carry

        lax.fori_loop(0, RING, left_in, 0)

        def come(k, other):
            sender = other * RING + k
            there = put(orr, sender)
            remote(r_ref, there, s["fs"].at[k, other], s["fr"].at[sender], (other, k, br, z)).wait_recv()

        senders(come)

        lane_of = lax.broadcasted_iota(jnp.int32, (channels, lanes), 1) // side
        contract = (((0,), (0,)), ((), ()))

        def channel_push(k, g, d, coming):
            src, dst = (s["tl"], s["l1"]) if k == 0 else (s["tr"], s["r1"])
            cols = pl.ds(pl.multiple_of(g * chunk, chunk), chunk)
            peer = along.sender(d) if coming else lax.rem(z + d, RING)
            return remote(
                src.at[z if coming else peer, :, cols],
                dst.at[peer if coming else z, :, cols],
                s["p1s"].at[k, g, d],
                s["p1r"].at[k, g, d],
                (br, ro, x, peer),
            )

        def front(g, carry):
            cols = pl.ds(pl.multiple_of(g * chunk, chunk), chunk)
            outer = lax.dot_general(ol[:, cols], orr[...], contract, preferred_element_type=f32)
            outer = (outer * (1.0 / (GROUP * rows))).astype(bf16)
            stacked = jnp.concatenate(
                [
                    jnp.concatenate(
                        [
                            outer[i * side : (i + 1) * side, q * lanes : (q + 1) * lanes]
                            for q in range(wide // lanes)
                        ],
                        axis=0,
                    )
                    for i in range(chunk // side)
                ],
                axis=1,
            )
            mixed = lax.dot_general(mix_ref[...], stacked, contract, preferred_element_type=f32)
            pieces = []
            for h in range(chunk // lanes):
                piece = jnp.zeros((channels, lanes), f32)
                for i in range(per):
                    at_lane = (h * per + i) * lanes
                    total = None
                    for y in range(per):
                        part = mixed[y * channels : (y + 1) * channels, at_lane : at_lane + lanes]
                        shift = (side * (i - y)) % lanes
                        part = pltpu.roll(part, shift, 1) if shift else part
                        total = part if total is None else total + part
                    piece = jnp.where(lane_of == i, total, piece)
                pieces.append(piece)
            opm = jnp.transpose(p_ref[cols].astype(f32)) + jnp.concatenate(pieces, axis=1)
            s["opm"][:, cols] = opm
            normed = norm_channels(opm).astype(bf16)
            projected = lax.dot_general(in_ref[...], normed, contract, preferred_element_type=f32)
            block = lambda k: projected[k * channels : (k + 1) * channels]
            here = k_ref[:, cols]
            tri_left = (here * jax.nn.sigmoid(block(0)) * block(1)).astype(bf16)
            tri_right = (here * jax.nn.sigmoid(block(2)) * block(3)).astype(bf16)
            s["tl"][:, :, cols] = tri_left.reshape(RING, deep, chunk)
            s["tr"][:, :, cols] = tri_right.reshape(RING, deep, chunk)
            s["gate"][:, cols] = jax.nn.sigmoid(block(4))

            def push(d, carry):
                for k in range(2):
                    channel_push(k, g, d, False).start()
                return carry

            lax.fori_loop(1, RING, push, 0)
            return carry

        lax.fori_loop(0, chunks, front, 0)
        turn = s["turn"]

        def regroup(src, dst):
            outer, inner, _ = src.shape

            def one(v, carry):
                cols = pl.ds(pl.multiple_of(v * lanes, lanes), lanes)
                for g in range(outer):
                    turn[v, g * inner : (g + 1) * inner] = src[g, :, cols].astype(f32)
                for g in range(inner):
                    dst[g, :, cols] = turn[v, pl.ds(g, outer, stride=inner)].astype(bf16)
                return carry

            lax.fori_loop(0, tokens // lanes, one, 0)

        s["l1"][z] = s["tl"][z]
        s["r1"][z] = s["tr"][z]
        for k, ref in ((0, "l1"), (1, "r1")):

            def arrive(d, carry):
                for g in range(chunks):
                    channel_push(k, g, d, True).wait_recv()
                return carry

            lax.fori_loop(1, RING, arrive, 0)
            to = s["l2"] if k == 0 else s["r2"]
            regroup(s[ref], to)

        def over(d, coming):
            there = s["r3"].at[1 - x if coming else x, to_channel.sender(d)]
            return remote(there, there, s["xs"].at[d], s["xr"].at[d], cross)

        to_channel.start()
        first_over = remote(s["r2"].at[b], s["r3"].at[x, b], s["xs"].at[0], s["xr"].at[0], cross)
        first_over.start()

        def hand(d, carry):
            to_channel.arrive(d)
            over(d, False).start()
            return carry

        lax.fori_loop(1, GROUP, hand, 0)
        lane = lax.broadcasted_iota(jnp.int32, (few, lanes), 1) // side

        def unfold(block, put_line):
            def one(v, carry):
                t = block(pl.ds(pl.multiple_of(v * lanes, lanes), lanes)).astype(f32)
                t = t.reshape(GROUP * few, lanes)
                turned = [t] + [pltpu.roll(t, side * n, 1) for n in range(1, per)]
                for n in range(per):
                    line = []
                    for q in range(GROUP // per):
                        piece = jnp.zeros((few, lanes), f32)
                        for m in range(per):
                            k = (q * per + m) * few
                            piece = jnp.where(lane == m, turned[(m - n) % per][k : k + few], piece)
                        line.append(piece)
                    put_line(v * per + n, jnp.concatenate(line, axis=1))
                return carry

            lax.fori_loop(0, side // per, one, 0)

        lines = lambda i: pl.ds(pl.multiple_of(i * few, few), few)

        def put_left(i, line):
            s["a"][lines(i)] = line

        unfold(lambda cols: s["l3"][:, :, cols], put_left)
        a = s["a"][...].astype(bf16)
        to = lax.broadcasted_iota(jnp.int32, (tall, tall), 0)
        of = lax.broadcasted_iota(jnp.int32, (tall, tall), 1)
        order = (of == lax.rem(to, side) * few + to // side).astype(f32).astype(bf16)

        def multiply(h, carry):
            def put_right(j, line):
                s["b"][h, lines(j)] = line

            unfold(lambda cols: s["r3"][h, :, :, cols], put_right)
            t = jnp.dot(order, s["b"][h].astype(bf16), preferred_element_type=f32).astype(bf16)
            s["y"][:, pl.ds(pl.multiple_of(h * tall, tall), tall)] = lax.dot_general(
                a, t, (((1,), (1,)), ((), ())), preferred_element_type=f32
            )
            return carry

        multiply(x, 0)

        def over_in(d, carry):
            over(d, True).wait_recv()
            return carry

        lax.fori_loop(0, GROUP, over_in, 0)
        multiply(1 - x, 0)

        def fold(v, carry):
            cols = pl.ds(pl.multiple_of(v * lanes, lanes), lanes)
            y = s["y"][pl.ds(pl.multiple_of(v * per * few, per * few), per * few)]
            for q in range(across_k // lanes):
                t = y[:, q * lanes : (q + 1) * lanes]
                turned = [t] + [pltpu.roll(t, side * n, 1) for n in range(1, per)]
                for m in range(per):
                    piece = jnp.zeros((few, lanes), f32)
                    for n in range(per):
                        piece = jnp.where(
                            lane == n, turned[(n - m) % per][n * few : (n + 1) * few], piece
                        )
                    s["m0"][q * per + m, :, cols] = piece.astype(bf16)
            return carry

        lax.fori_loop(0, side // per, fold, 0)
        from_channel.start()
        from_channel.finish()
        regroup(s["m1"], s["m2"])
        from_ring.start()
        from_ring.finish()

        def end(g, carry):
            cols = pl.ds(pl.multiple_of(g * chunk, chunk), chunk)
            mixed = s["m3"][:, :, cols].astype(f32).reshape(channels, chunk)
            mixed = norm_channels(mixed).astype(bf16)
            mixed = lax.dot_general(out_ref[...], mixed, contract, preferred_element_type=f32)
            state = s["opm"][:, cols] + s["gate"][:, cols] * mixed
            normed = norm_channels(state).astype(bf16)
            hidden = lax.dot_general(up_ref[...], normed, contract, preferred_element_type=f32)
            hidden = jnp.maximum(hidden, 0.0).astype(bf16)
            update = lax.dot_general(hidden, down_ref[...], contract, preferred_element_type=f32)
            o_ref[cols] = (jnp.transpose(state) + update).astype(bf16)
            return carry

        lax.fori_loop(0, chunks, end, 0)

        def sent(d, carry):
            along.sent(d)
            for r in range(2):
                row_push(r, d, False).wait_send()
            to_chip(d, False).wait_send()
            to_twin(d, False).wait_send()
            for k in range(2):
                for g in range(chunks):
                    channel_push(k, g, d, False).wait_send()
            return carry

        lax.fori_loop(1, RING, sent, 0)
        first.wait_send()

        def forwarded(k, other):
            mine = jnp.logical_and(own, jnp.logical_and(k == ro, x == other))

            @pl.when(jnp.logical_not(mine))
            def _():
                forward(k, other, r_ref).wait_send()

        each(forwarded)

        def handed(d, carry):
            to_channel.sent(d)
            over(d, False).wait_send()
            return carry

        lax.fori_loop(1, GROUP, handed, 0)
        first_over.wait_send()

    scratch = [pltpu.VMEM(*v) for v in buffers.values()]
    scratch += [pltpu.SemaphoreType.DMA(v) for v in sems.values()]
    scratch += first_scratch
    return call_exchange(
        kernel,
        [jax.ShapeDtypeStruct(entries.shape, bf16), jax.ShapeDtypeStruct((tokens, channels), bf16)],
        scratch, 6, 4 << 20,
        [IN_VMEM] * 2 + [IN_SMEM] + [IN_PLACE] * 8 + [IN_VMEM] + [IN_PLACE] * 3 + [IN_VMEM] + [IN_PLACE] * 3,
        bias_weights, same, chain_bias, row_weights, row_merge, entries, col_weights, col_merge, expand,
        contract_weights, factor_weights, presence, pair, outer_weights, tri_in, keep, tri_out, up, down,
    )


def on_device(
    homolog_embedding,
    pair_representation,
    alignment_entry_mask,
    residue_presence_mask,
    residue_chain_index,
    row_projection_weights,
    horizontal_attend_merge,
    pair_bias_matrix,
    same_chain_bias,
    column_projection_weights,
    vertical_attend_merge,
    homolog_mlp_expand,
    homolog_mlp_contract,
    tensor_product_linear,
    outer_output_matrix,
    triangle_input_weights,
    triangle_output_matrix,
    pair_up_weight,
    pair_down_weight,
):
    device_local_rows, residue_total, channel_count = homolog_embedding.shape
    pair_cols = pair_representation.shape[1]
    row_place = lax.axis_index(COL)
    col_place = lax.axis_index(("branch", "row"))
    chain_here = lax.dynamic_slice_in_dim(
        residue_chain_index, row_place * residue_total, residue_total
    )
    chain_there = lax.dynamic_slice_in_dim(residue_chain_index, col_place * pair_cols, pair_cols)
    residue_keep = residue_presence_mask.astype(jnp.float32)
    keep_here = lax.dynamic_slice_in_dim(residue_keep, row_place * residue_total, residue_total)
    keep_there = lax.dynamic_slice_in_dim(residue_keep, col_place * pair_cols, pair_cols)
    low_first = jnp.transpose(chain_here.reshape(residue_total // 8, 8))
    same_chain = (low_first[:, :, None] == chain_there[None, None, :]).astype(jnp.float32)
    tokens = residue_total * pair_cols
    pair_keep = (keep_here[:, None] * keep_there[None, :]).reshape(1, tokens)
    msa_out, updated_pair_state = whole_block(
        jnp.transpose(pair_bias_matrix),
        same_chain.reshape(8, residue_total // 8 * pair_cols),
        same_chain_bias,
        row_projection_weights,
        horizontal_attend_merge,
        homolog_embedding,
        column_projection_weights,
        vertical_attend_merge,
        homolog_mlp_expand,
        homolog_mlp_contract,
        jnp.transpose(tensor_product_linear),
        alignment_entry_mask,
        pair_representation.reshape(tokens, CZ),
        outer_output_matrix,
        triangle_input_weights,
        pair_keep,
        triangle_output_matrix,
        pair_up_weight,
        pair_down_weight,
    )
    updated_pair_state = updated_pair_state.reshape(residue_total, pair_cols, CZ)
    return (msa_out, updated_pair_state)


def solution(mesh):
    split = Mesh(
        mesh.devices.reshape(mesh.shape["branch"], mesh.shape["row"], 2, 8),
        ("branch", "row", "col_0", "col_1"),
    )
    in_specs = (
        P(("branch", "row"), COL, None),
        P(COL, ("branch", "row"), None),
        P(("branch", "row"), COL),
        P(),
        P(),
        P(),
        P(),
        P(),
        P(),
        P(),
        P(),
        P(),
        P(),
        P(),
        P(),
        P(),
        P(),
        P(),
        P(),
    )
    out_specs = (P(("branch", "row"), COL, None), P(COL, ("branch", "row"), None))
    return jax.shard_map(
        on_device, mesh=split, in_specs=in_specs, out_specs=out_specs, check_vma=False
    )
```

```python
import jax
import jax.numpy as jnp
from jax import lax
from jax.experimental import pallas as pl
from jax.experimental.pallas import tpu as pltpu
from jax.sharding import Mesh
from jax.sharding import PartitionSpec as P

HEADS = 8
PER_HEAD_WIDTH = 32
CZ = 128
PRODUCT_FEATURES = 32
COL = ("col_0", "col_1")


EPSILON = 1e-05
NEGATIVE = -1000000000.0


MESH = pl.DeviceIdType.MESH
GROUP = 16
RING = 8
SIZES = {"b": 16, "c": 16, "z": 8}


def place():
    axes = [lax.axis_index(a) for a in ("branch", "row", *COL)]
    return (*axes, axes[0] * 8 + axes[1], axes[2] * 8 + axes[3])


def across(b, c):
    return (b // 8, lax.rem(b, 8), c // 8, lax.rem(c, 8))


def remote(src, dst, send, recv, to):
    return pltpu.make_async_remote_copy(
        src_ref=src, dst_ref=dst, send_sem=send, recv_sem=recv, device_id=to, device_id_type=MESH
    )


IN_VMEM = pl.BlockSpec(memory_space=pltpu.VMEM)
IN_SMEM = pl.BlockSpec(memory_space=pltpu.SMEM)
IN_PLACE = pl.BlockSpec(memory_space=pl.ANY)


def call_exchange(kernel, out_shape, scratch, collective_id, sent, specs, *args):
    return pl.pallas_call(
        kernel,
        out_shape=out_shape,
        in_specs=specs,
        out_specs=jax.tree.map(lambda _: IN_VMEM, out_shape),
        scratch_shapes=scratch,
        compiler_params=pltpu.CompilerParams(
            collective_id=collective_id, has_side_effects=True, vmem_limit_bytes=62 << 20
        ),
        cost_estimate=pl.CostEstimate(flops=0, bytes_accessed=2 * sent, transcendentals=0),
    )(*args)


class Pushes:
    def __init__(self, over, ins, outs, picks, puts, send, recv):
        br, ro, x, z, b, c = place()
        self.count = SIZES[over]
        self.me, self.device = {
            "b": (b, lambda k: across(k, c)),
            "c": (c, lambda k: across(b, k)),
            "z": (z, lambda k: (br, ro, x, k)),
        }[over]
        self.parts = list(zip(ins, outs, picks, puts))
        self.send, self.recv = send, recv

    def greet(self, barrier):
        def one(d, carry):
            to = self.device(lax.rem(self.me + d, self.count))
            pl.semaphore_signal(barrier, inc=1, device_id=to, device_id_type=MESH)
            return carry

        lax.fori_loop(1, self.count, one, 0)

    def sender(self, d):
        return lax.rem(self.me + (self.count - d), self.count)

    def copies(self, d, coming):
        peer = self.sender(d) if coming else lax.rem(self.me + d, self.count)
        for k, (src, dst, pick, put) in enumerate(self.parts):
            yield remote(
                pick(src, self.me if coming else peer),
                put(dst, peer if coming else self.me),
                self.send.at[k, d],
                self.recv.at[k, d],
                self.device(peer),
            )

    def start(self):
        def one(d, carry):
            for copy in self.copies(d, False):
                copy.start()
            return carry

        lax.fori_loop(1, self.count, one, 0, unroll=True)
        for src, dst, pick, put in self.parts:
            put(dst, self.me)[...] = pick(src, self.me)[...]

    def arrive(self, d):
        for copy in self.copies(d, True):
            copy.wait_recv()

    def sent(self, d):
        for copy in self.copies(d, False):
            copy.wait_send()

    def finish(self):
        def one(d, carry):
            self.arrive(d)
            self.sent(d)
            return carry

        lax.fori_loop(1, self.count, one, 0, unroll=True)


def crosswise():
    br, ro, x, z = place()[:4]
    return (br, ro, 1 - x, z)


def normal(x):
    x = x.astype(jnp.float32)
    centre = x - jnp.mean(x, axis=-1, keepdims=True)
    spread = jnp.mean(centre * centre, axis=-1, keepdims=True)
    return (centre * lax.rsqrt(spread + EPSILON)).astype(jnp.bfloat16)


def bias_and_rows(pair, weights, entries, residues):
    some, others = residues, residues
    pair_channels = pair.shape[1]
    heads = weights.shape[0]
    msa_rows, _, channels = entries.shape
    carried = heads // 2
    tall = some + 8
    lanes = 128
    fold = lanes // others
    n_copies = 32

    def kernel(
        p_ref, w_ref, s_ref, h_ref, e_ref, k_ref, pair_ready, entries_ready, entered,
        ob_ref, or_ref, om_ref, m_ref, turn, tile, tiles, rows, bsend, brecv, psend, precv, xsend, xrecv, rsend, rrecv,
    ):
        br, ro, x, z, _, c = place()
        core = lax.rem(ro, 2)
        right = (br, ro, x, lax.rem(z + 1, RING))
        left = (br, ro, x, lax.rem(z + RING - 1, RING))
        twin = (br, ro + 1 - 2 * core, x, z)
        cross = crosswise()
        at = lambda ref, k: ref.at[k]
        put = lambda ref, k: ref.at[:, x * RING + k]
        spread = Pushes(
            "b", (tile, m_ref), (tiles, om_ref), [lambda ref, k: ref, lambda ref, k: ref.at[k // 4]], [at] * 2, bsend, brecv
        )
        pushes = Pushes("z", (rows,), (or_ref,), [lambda ref, k: ref.at[:, k]], [put], psend, precv)
        barrier = pltpu.get_barrier_semaphore()
        spread.greet(barrier)
        pushes.greet(barrier)
        pl.semaphore_signal(barrier, inc=1, device_id=cross, device_id_type=MESH)

        present = k_ref[...].astype(jnp.float32)
        spot = lax.broadcasted_iota(jnp.int32, (msa_rows, lanes), 0)
        wide_lane = lax.broadcasted_iota(jnp.int32, (msa_rows, lanes), 1)
        copies_of = (lax.rem(wide_lane, msa_rows) == spot).astype(jnp.float32)
        by_residue = lax.dot_general(
            present, copies_of, (((0,), (0,)), ((), ())), preferred_element_type=jnp.float32
        )
        mine = lax.broadcasted_iota(jnp.int32, (some, lanes), 1) // msa_rows == lax.rem(br * 8 + ro, 8)
        by_residue = jnp.where(mine, by_residue, 0.0).astype(jnp.bfloat16)
        for k in range(some // 8):
            m_ref[k] = by_residue[k * 8 : (k + 1) * 8]
        spot = lax.broadcasted_iota(jnp.int32, (some, channels), 0)
        wide_lane = lax.broadcasted_iota(jnp.int32, (some, channels), 1)
        here = jnp.logical_and(lax.rem(wide_lane, some) == spot, wide_lane // some == z)
        by_row = jnp.dot(present, here.astype(jnp.float32), preferred_element_type=jnp.float32)
        head_of = lax.broadcasted_iota(jnp.int32, (heads, lanes), 0)
        chain = jnp.zeros((heads, lanes), jnp.float32)
        for head in range(heads):
            chain = jnp.where(head_of == head, h_ref[head], chain)
        pair_ready()
        normed = normal(p_ref[...].reshape(some * others, pair_channels))
        for low in range(8):
            tokens = jnp.concatenate(
                [normed[(high * 8 + low) * others :][:others] for high in range(fold)], axis=0
            )
            bias = lax.dot_general(
                w_ref[...], tokens, (((1,), (1,)), ((), ())), preferred_element_type=jnp.float32
            )
            turn[low * heads : (low + 1) * heads] = bias + chain * s_ref[low : low + 1]
        for head in range(heads):
            tile[head] = turn[pl.ds(head, 8, stride=heads)].astype(jnp.bfloat16)
        entered()
        spread.start()
        entries_ready()
        normed = normal(e_ref[...].reshape(msa_rows * some, channels))
        for half in range(2):
            for k in range(RING):
                row = half * RING + k
                rows[half, k, :some] = normed[row * some : (row + 1) * some]
                rows[half, k, some:] = jnp.broadcast_to(by_row[row : row + 1], (8, channels)).astype(jnp.bfloat16)
        pushes.start()
        first = remote(rows.at[:, z], or_ref.at[:, c], xsend.at[0], xrecv.at[0], cross)
        first.start()
        spread.finish()
        lane = lax.broadcasted_iota(jnp.int32, (8, lanes), 1) // others

        def set_out(head, carry):
            t = tiles[:, head].astype(jnp.float32).reshape(GROUP * 8, lanes)
            turned = [t] + [pltpu.roll(t, others * s, 1) for s in range(1, fold)]
            lines = []
            for n in range(fold):
                line = []
                for q in range(GROUP // fold):
                    piece = jnp.zeros((8, lanes), jnp.float32)
                    for m in range(fold):
                        k = (q * fold + m) * 8
                        piece = jnp.where(lane == m, turned[(m - n) % fold][k : k + 8], piece)
                    line.append(piece)
                lines.append(jnp.concatenate(line, axis=1))
            whole = jnp.concatenate(lines, axis=0).astype(jnp.bfloat16)
            ob_ref[head, pl.ds(pl.multiple_of(z * some, some), some)] = whole
            return carry

        lax.fori_loop(0, heads, set_out, 0)

        def view(block, half, mine):
            at_head, count = mine * carried, carried
            if half is not None:
                count = carried // 2
                at_head = at_head + half * count
            rows_at = pl.multiple_of(lax.rem(block + RING, RING) * some, some)
            return ob_ref.at[pl.ds(at_head, count), pl.ds(rows_at, some)]

        copies, handed = [], []

        def push(block, half, to):
            k = len(copies)
            there = view(block, half, core)
            copies.append(remote(there, there, rsend.at[k], rrecv.at[k], to))
            copies[-1].start()
            return k

        def arrived(k, block, half):
            there = view(block, half, core)
            remote(there, there, rsend.at[k], rrecv.at[k], right).wait_recv()

        def hand(block, half):
            handed.append((push(block, half, twin), block, half))

        def over(d, coming):
            k = pushes.sender(d)
            there = or_ref.at[:, (1 - x if coming else x) * RING + k]
            return remote(there, there, xsend.at[d], xrecv.at[d], cross)

        for step in (1, 2, 3):
            for d in (step, RING - step):
                pushes.arrive(d)
                over(d, False).start()
            if step == 1:
                going = {+1: push(z, None, right), -1: push(z, None, left)}
            coming = {}
            for way, to in ((+1, right), (-1, left)):
                block = z - way * step
                arrived(going[way], block, None)
                half = None if step < 3 else (0 if way > 0 else 1)
                coming[way] = push(block, half, to)
                hand(block, None)
            going = coming
        pushes.arrive(4)
        over(4, False).start()
        for way in (+1, -1):
            half = 0 if way > 0 else 1
            arrived(going[way], z - way * 4, half)
            hand(z - way * 4, half)
        for k, block, half in handed:
            there = view(block, half, 1 - core)
            remote(there, there, rsend.at[k], rrecv.at[k], twin).wait_recv()
        for d in range(RING):
            over(d, True).wait_recv()
        for copy in copies:
            copy.wait_send()
        first.wait_send()
        for d in range(1, RING):
            pushes.sent(d)
            over(d, False).wait_send()

    wide = GROUP * others
    bf16 = jnp.bfloat16
    arrays = [
        ((heads, RING * some, wide), bf16),
        ((2, GROUP, tall, channels), bf16),
        ((GROUP, 8, lanes), bf16),
        ((some // 8, 8, lanes), bf16),
        ((8 * heads, lanes), jnp.float32),
        ((heads, 8, lanes), bf16),
        ((GROUP, heads, 8, lanes), bf16),
        ((2, RING, tall, channels), bf16),
    ]
    scratch = [pltpu.VMEM(*v) for v in arrays]
    scratch += [pltpu.SemaphoreType.DMA((2, GROUP))] * 2
    scratch += [pltpu.SemaphoreType.DMA((1, RING))] * 2
    scratch += [pltpu.SemaphoreType.DMA((RING,))] * 2
    scratch += [pltpu.SemaphoreType.DMA((n_copies,))] * 2
    return kernel, scratch


def heads_attend(queries, keys, values, present, bias_of):
    lanes = 128
    per = lanes // PER_HEAD_WIDTH
    lane = lax.broadcasted_iota(jnp.int32, (1, lanes), 1) // PER_HEAD_WIDTH
    blocks = []
    for block in range(HEADS // per):
        cols = slice(block * lanes, (block + 1) * lanes)
        total = jnp.zeros((queries.shape[0], lanes), jnp.float32)
        for h in range(per):
            here = (lane == h).astype(jnp.float32)
            query = queries[:, cols] * here.astype(jnp.bfloat16)
            scores = lax.dot_general(
                query, keys[:, cols], (((1,), (1,)), ((), ())), preferred_element_type=jnp.float32
            )
            if bias_of is not None:
                scores = scores + bias_of(block * per + h).astype(jnp.float32)
            scores = jnp.where(present, scores, NEGATIVE)
            powers = jnp.exp(scores - jnp.max(scores, axis=-1, keepdims=True))
            totals = jnp.sum(powers, axis=-1, keepdims=True)
            summed = jnp.dot(
                powers.astype(jnp.bfloat16), values[:, cols], preferred_element_type=jnp.float32
            )
            total = total + (summed / totals) * here
        blocks.append(total)
    return jnp.concatenate(blocks, axis=1)


def norm_channels(x):
    centre = x - jnp.mean(x, axis=0, keepdims=True)
    spread = jnp.mean(centre * centre, axis=0, keepdims=True)
    return centre * lax.rsqrt(spread + EPSILON)


def whole_block(
    bias_weights, same, chain_bias, row_weights, row_merge, entries, col_weights, col_merge, expand,
    contract_weights, factor_weights, presence, pair, outer_weights, tri_in, keep, tri_out, up, down,
):
    rows, residues, features = entries.shape
    wide = residues * PRODUCT_FEATURES
    entry_count = rows * residues
    columns = residues // GROUP
    queries = RING * residues
    keys_count = GROUP * residues
    step = 128
    tokens, channels = pair.shape
    lanes = 128
    side = PRODUCT_FEATURES
    per = lanes // side
    chips = GROUP // 2
    few = RING
    deep = channels // RING
    chunk = 8 * side
    chunks = wide // chunk
    tall = few * side
    across_k = GROUP * side
    bf16, f32 = jnp.bfloat16, jnp.float32
    inputs = dict(
        p=pair, e=entries, wr=row_weights, ow=outer_weights, rm=row_merge, wc=col_weights,
        cm=col_merge, ex=expand, co=contract_weights, fw=factor_weights, tri_in=tri_in, tri_out=tri_out, up=up,
        down=down,
    )
    buffers = {
        **{"in_" + name: (value.shape, value.dtype) for name, value in inputs.items()},
        "mix": ((PRODUCT_FEATURES * PRODUCT_FEATURES // 4, 4 * channels), bf16),
        "outer_f32": (outer_weights.shape, f32),
        "there": ((8, 2 * lanes), f32),
        "q": ((queries, features), bf16),
        "g": ((queries, features), f32),
        "row_out": ((2, RING, residues, features), bf16),
        "row_in": ((2, RING, residues, features), bf16),
        "by_lane": ((features // 128, entry_count, 128), f32),
        "state": ((entry_count, features), f32),
        "again": ((entry_count, features), f32),
        "col_sent": ((residues, rows, features), bf16),
        "cols": ((columns, GROUP * rows, features), bf16),
        "col_out": ((columns, GROUP * rows, features), bf16),
        "col_in": ((residues, rows, features), bf16),
        "apart": ((rows // 4, PRODUCT_FEATURES, 128), f32),
        "joined": ((rows * 8, 128), f32),
        "left": ((rows, wide), bf16),
        "right": ((rows, wide), bf16),
        "stage": ((RING, rows, wide), bf16),
        "all_left": ((GROUP * rows, wide), bf16),
        "all_right": ((GROUP * rows, wide), bf16),
        "opm": ((channels, tokens), f32),
        "gate": ((channels, tokens), f32),
        "tl": ((RING, deep, tokens), bf16),
        "tr": ((RING, deep, tokens), bf16),
        "l1": ((RING, deep, tokens), bf16),
        "r1": ((RING, deep, tokens), bf16),
        "turn": ((tokens // lanes, channels, lanes), f32),
        "l2": ((GROUP, few, tokens), bf16),
        "r2": ((GROUP, few, tokens), bf16),
        "l3": ((GROUP, few, tokens), bf16),
        "r3": ((2, GROUP, few, tokens), bf16),
        "a": ((tall, across_k), f32),
        "b": ((2, tall, across_k), f32),
        "y": ((tall, across_k), f32),
        "m0": ((GROUP, few, tokens), bf16),
        "m1": ((GROUP, few, tokens), bf16),
        "m2": ((RING, deep, tokens), bf16),
        "m3": ((RING, deep, tokens), bf16),
    }
    sems = {
        "load": (len(inputs),),
        "rs": (2, RING), "rr": (2, RING), "c1s": (1, GROUP), "c1r": (1, GROUP),
        "c2s": (1, GROUP), "c2r": (1, GROUP), "c3s": (1, GROUP), "c3r": (1, GROUP),
        "zs": (1, RING), "zr": (1, RING), "ls": (RING,), "lr": (RING,), "ts": (RING,), "tr_": (RING,),
        "fs": (RING, 2), "fr": (GROUP,), "p1s": (2, chunks, RING), "p1r": (2, chunks, RING),
        "p2s": (2, GROUP), "p2r": (2, GROUP), "xs": (GROUP,), "xr": (GROUP,),
        "p3s": (1, GROUP), "p3r": (1, GROUP), "p4s": (1, RING), "p4r": (1, RING),
    }
    names = [*buffers, *sems]
    first_part, first_scratch = bias_and_rows(pair, bias_weights, entries, residues)

    def kernel(
        bw_ref, same_ref, chain_ref, wr_in, rm_in, e_in, wc_in, cm_in, ex_in, co_in, fw_in, pr_ref,
        p_in, ow_in, in_in, k_ref, out_in, up_in, down_in, om_ref, o_ref, *scratch,
    ):
        s = dict(zip(names, scratch))
        loads = {}
        for n, (name, ref) in enumerate(
            dict(
                p=p_in, e=e_in, wr=wr_in, ow=ow_in, rm=rm_in, wc=wc_in, cm=cm_in, ex=ex_in,
                co=co_in, fw=fw_in, tri_in=in_in, tri_out=out_in, up=up_in, down=down_in,
            ).items()
        ):
            loads[name] = pltpu.make_async_copy(ref, s["in_" + name], s["load"].at[n])
            loads[name].start()
        wr_ref, ow_ref, e_ref, rm_ref, wc_ref, cm_ref, ex_ref, co_ref, fw_ref, p_ref = (
            s["in_" + n] for n in ("wr", "ow", "e", "rm", "wc", "cm", "ex", "co", "fw", "p")
        )
        of_first = scratch[len(names) :]
        b_ref, w_ref, cp_ref = of_first[:3]
        in_ref, out_ref, up_ref, down_ref = (s["in_" + n] for n in ("tri_in", "tri_out", "up", "down"))
        mix_ref = s["mix"]

        def ready(*wanted):
            for name in wanted:
                loads[name].wait()

        l_ref, r_ref = s["left"], s["right"]
        br, ro, x, z, b, _ = place()
        core = lax.rem(ro, 2)
        chip = b // 2
        twin = (br, ro + 1 - 2 * core, x, z)
        cross = crosswise()
        put = lambda ref, k: ref.at[pl.ds(pl.multiple_of(k * rows, rows), rows)]
        at = lambda ref, k: ref.at[k]
        whole = lambda ref, k: ref
        ol, orr = s["all_left"], s["all_right"]
        along = Pushes("z", (r_ref,), (s["stage"],), [whole], [at], s["zs"], s["zr"])
        on_core = lambda k: across(k * 2 + core, x * RING + z)
        back = lambda d: lax.rem(chip + chips - d, chips)
        own = br == x

        def each(act):
            def one(d, carry):
                for other in range(2):
                    act(lax.rem(ro + d, RING), other)
                return carry

            lax.fori_loop(0, RING, one, 0)

        def senders(act):
            def one(k, other):
                @pl.when(jnp.logical_not(jnp.logical_and(own, jnp.logical_and(k == ro, br == other))))
                def _():
                    act(k, other)

            each(one)

        to_channel = Pushes(
            "b", (s["l2"], s["r2"]), (s["l3"], s["r3"]), [at] * 2, [at, lambda ref, k: ref.at[x, k]],
            s["p2s"], s["p2r"],
        )
        from_channel = Pushes("b", (s["m0"],), (s["m1"],), [at], [at], s["p3s"], s["p3r"])
        from_ring = Pushes("z", (s["m2"],), (s["m3"],), [at], [at], s["p4s"], s["p4r"])

        barrier = pltpu.get_barrier_semaphore()
        along.greet(barrier)
        to_channel.greet(barrier)

        def signal(to):
            pl.semaphore_signal(barrier, inc=1, device_id=to, device_id_type=MESH)

        signal(cross)
        senders(lambda k, other: signal((other, k, br, z)))
        lane_at = lax.broadcasted_iota(jnp.int32, (1, lanes), 1) // side

        def entered():
            others = jnp.where(own, GROUP - 1, GROUP)
            pl.semaphore_wait(barrier, 2 * (RING - 1 + GROUP - 1 + 1) + others)

        first_part(
            p_ref, bw_ref, same_ref, chain_ref, e_ref, pr_ref,
            lambda: ready("p"), lambda: ready("e"), entered, *of_first,
        )

        def row_push(r, d, coming):
            peer = along.sender(d) if coming else lax.rem(z + d, RING)
            return remote(
                s["row_out"].at[r, z if coming else peer],
                s["row_in"].at[r, peer if coming else z],
                s["rs"].at[r, d],
                s["rr"].at[r, d],
                (br, ro, x, peer),
            )

        ready("wr")
        for r in range(2):
            whole_row = w_ref[r, :, :residues].reshape(keys_count, features)
            keys_values = jnp.dot(
                whole_row, wr_ref[:, features : 3 * features], preferred_element_type=f32
            ).astype(bf16)
            keys, values = keys_values[:, :features], keys_values[:, features:]
            half_row = w_ref[r, pl.ds(x * RING, RING), :residues].reshape(queries, features)
            q = jnp.dot(half_row, wr_ref[:, :features], preferred_element_type=f32)
            s["q"][...] = (q * PER_HEAD_WIDTH ** (-0.5)).astype(bf16)
            gate = jnp.dot(half_row, wr_ref[:, 3 * features :], preferred_element_type=f32)
            s["g"][...] = jax.nn.sigmoid(gate)
            present = []
            for half in range(2):
                total = jnp.zeros((8, features), f32)
                for k in range(RING):
                    total = total + w_ref[r, half * RING + k, residues:].astype(f32)
                present.append(total[:1])
            present = jnp.concatenate(present, axis=1) > 0

            def row_block(t, carry):
                t = lax.rem(t + 1 - z // 4, 2)
                rows_at = pl.ds(pl.multiple_of(t * step, step), step)
                attended = heads_attend(
                    s["q"][rows_at], keys, values, present, lambda h: b_ref[h, rows_at, :]
                )
                gated = (attended * s["g"][rows_at]).astype(bf16)
                some = step // residues
                s["row_out"][r, pl.ds(t * some, some)] = gated.reshape(some, residues, features)

                def push(k, carry):
                    d = lax.rem(t * some + k - z + RING, RING)

                    @pl.when(d != 0)
                    def _():
                        row_push(r, d, False).start()

                    return carry

                lax.fori_loop(0, some, push, 0, unroll=True)
                return carry

            lax.fori_loop(0, queries // step, row_block, 0)
            s["row_in"][r, z] = s["row_out"][r, z]

        ready("ow", "rm", "wc", "fw")
        s["outer_f32"][...] = ow_ref[...].astype(f32)
        for q in range(PRODUCT_FEATURES // 4):
            for y in range(4):
                mix_ref[q * side : (q + 1) * side, y * channels : (y + 1) * channels] = s["outer_f32"][
                    pl.ds(q * 4 + y, side, stride=PRODUCT_FEATURES)
                ].astype(bf16)
        copied = lax.broadcasted_iota(jnp.int32, (2 * side, lanes), 0)
        copied_to = lax.rem(lax.broadcasted_iota(jnp.int32, (2 * side, lanes), 1), side)
        copied = (copied == copied_to).astype(f32).astype(bf16)
        left_weights = lax.dot_general(
            copied, fw_ref[...], (((0,), (0,)), ((), ())), preferred_element_type=f32
        ).astype(bf16)
        present = pr_ref[...].astype(f32)
        spot = lax.broadcasted_iota(jnp.int32, (residues, lanes), 0)
        wide_lane = lax.broadcasted_iota(jnp.int32, (residues, lanes), 1)
        beside = (lax.rem(wide_lane, residues) == spot).astype(f32)
        right_presence = jnp.dot(present, beside, preferred_element_type=f32)

        def left_presence(q):
            spread = jnp.logical_and(spot // per == q, wide_lane // side == lax.rem(spot, per))
            return jnp.dot(present, spread.astype(f32), preferred_element_type=f32)

        def row_arrive(d, carry):
            for r in range(2):
                row_push(r, d, True).wait_recv()
            return carry

        lax.fori_loop(1, RING, row_arrive, 0)

        part = entry_count // 4

        def merge_rows(g, carry):
            at_rows = pl.ds(pl.multiple_of(g * part, part), part)
            few_rows = part // residues
            half = few_rows * g // RING
            first_at = lax.rem(few_rows * g, RING)
            gated = s["row_in"][half, pl.ds(first_at, few_rows)].reshape(part, features)
            here = e_ref[pl.ds(g * few_rows, few_rows)].reshape(part, features).astype(f32)
            here = here + jnp.dot(gated, rm_ref[...], preferred_element_type=f32)
            for k in range(features // lanes):
                s["by_lane"][k, at_rows] = here[:, k * lanes : (k + 1) * lanes]
            return carry

        lax.fori_loop(0, 4, merge_rows, 0)

        def turn_rows(g, carry):
            some = part // rows
            for i in range(some):
                at_rows = pl.ds(pl.multiple_of(g * part + i * rows, rows), rows)
                for k in range(features // lanes):
                    s["state"][at_rows, k * lanes : (k + 1) * lanes] = s["by_lane"][
                        k, pl.ds(g * some + i, rows, stride=residues)
                    ]
            here = normal(s["state"][pl.ds(pl.multiple_of(g * part, part), part)])
            s["col_sent"][pl.ds(g * some, some)] = here.reshape(some, rows, features)
            return carry

        lax.fori_loop(0, 4, turn_rows, 0)
        pair_of = lambda ref, k: ref.at[pl.ds(k * columns, columns)]
        rows_of = lambda ref, k: ref.at[:, pl.ds(pl.multiple_of(k * rows, rows), rows)]
        to_cols = Pushes("b", (s["col_sent"],), (s["cols"],), [pair_of], [rows_of], s["c1s"], s["c1r"])
        to_cols.start()
        halves = []
        for half in range(2):
            total = jnp.zeros((8, lanes), f32)
            for k in range(RING):
                total = total + cp_ref[half * RING + k].astype(f32)
            halves.append(total)
        s["there"][...] = jnp.concatenate(halves, axis=1)
        to_cols.finish()
        returns = []
        for r in range(columns):
            projected = jnp.dot(s["cols"][r], wc_ref[...], preferred_element_type=f32)
            s["q"][...] = (projected[:, :features] * PER_HEAD_WIDTH ** (-0.5)).astype(bf16)
            col_keys = projected[:, features : 2 * features].astype(bf16)
            col_values = projected[:, 2 * features : 3 * features].astype(bf16)
            s["g"][...] = jax.nn.sigmoid(projected[:, 3 * features :])
            col_present = s["there"][pl.ds(lax.rem(b, 4) * columns + r, 1)] > 0

            def col_block(t, carry):
                rows_at = pl.ds(pl.multiple_of(t * step, step), step)
                attended = heads_attend(s["q"][rows_at], col_keys, col_values, col_present, None)
                s["col_out"][r, rows_at] = (attended * s["g"][rows_at]).astype(bf16)
                return carry

            lax.fori_loop(0, GROUP * rows // step, col_block, 0)
            returns.append(
                Pushes(
                    "b",
                    (s["col_out"],),
                    (s["col_in"],),
                    [lambda ref, k, r=r: ref.at[r, pl.ds(pl.multiple_of(k * rows, rows), rows)]],
                    [lambda ref, k, r=r: ref.at[k * columns + r]],
                    s["c2s" if r == 0 else "c3s"],
                    s["c2r" if r == 0 else "c3r"],
                )
            )
            returns[-1].start()
        for back_again in returns:
            back_again.finish()

        ready("cm", "ex", "co", "tri_in", "tri_out", "up", "down")

        def transition(g, carry):
            at_rows = pl.ds(pl.multiple_of(g * part, part), part)
            some = part // rows
            gated = s["col_in"][pl.ds(g * some, some)].reshape(part, features)
            here = s["state"][at_rows] + jnp.dot(gated, cm_ref[...], preferred_element_type=f32)
            hidden = jnp.dot(normal(here), ex_ref[...], preferred_element_type=f32)
            hidden = jnp.maximum(hidden, 0.0).astype(bf16)
            here = here + jnp.dot(hidden, co_ref[...], preferred_element_type=f32)
            for k in range(features // lanes):
                s["by_lane"][k, at_rows] = here[:, k * lanes : (k + 1) * lanes]
            factor = lax.dot_general(
                normal(here), left_weights, (((1,), (1,)), ((), ())), preferred_element_type=f32
            )
            for q in range(some // per):
                piece = jnp.zeros((rows, lanes), f32)
                for m in range(per):
                    k = (q * per + m) * rows
                    piece = jnp.where(lane_at == m, factor[k : k + rows], piece)
                at_q = g * (some // per) + q
                cols = pl.ds(pl.multiple_of(at_q * lanes, lanes), lanes)
                l_ref[:, cols] = (piece * left_presence(at_q)).astype(bf16)
            return carry

        lax.fori_loop(0, 4, transition, 0)

        def turn_back(i, carry):
            at_rows = pl.ds(pl.multiple_of(i * residues, residues), residues)
            for k in range(features // lanes):
                here = s["by_lane"][k, pl.ds(i, residues, stride=rows)]
                s["again"][at_rows, k * lanes : (k + 1) * lanes] = here
                om_ref[i, :, k * lanes : (k + 1) * lanes] = here.astype(bf16)
            return carry

        lax.fori_loop(0, rows, turn_back, 0)
        for v in range(rows // per):
            some_rows = s["again"][v * lanes : (v + 1) * lanes]
            s["apart"][v] = lax.dot_general(
                fw_ref[...], normal(some_rows), (((1,), (1,)), ((), ())), preferred_element_type=f32
            )[side:]
            pieces = [s["apart"][v, pl.ds(m, 8, stride=per)] for m in range(per)]
            for n in range(per):
                piece = jnp.zeros((8, lanes), f32)
                for m in range(per):
                    shift = (side * (m - n)) % lanes
                    turned = pltpu.roll(pieces[m], shift, 1) if shift else pieces[m]
                    piece = jnp.where(lane_at == m, turned, piece)
                s["joined"][(v * per + n) * 8 : (v * per + n + 1) * 8] = piece
        for q in range(wide // lanes):
            cols = slice(q * lanes, (q + 1) * lanes)
            right = s["joined"][pl.ds(q, rows, stride=8)] * right_presence
            r_ref[:, cols] = right.astype(bf16)

        def to_chip(d, coming):
            block = back(d) * 2 + core if coming else b
            peer = back(d) if coming else lax.rem(chip + d, chips)
            return remote(l_ref, put(ol, block), s["ls"].at[d], s["lr"].at[d], on_core(peer))

        def to_twin(d, coming):
            block = put(ol, back(d) * 2 + (1 - core if coming else core))
            return remote(block, block, s["ts"].at[d], s["tr_"].at[d], twin)

        def forward(k, other, src):
            return remote(src, put(orr, b), s["fs"].at[k, other], s["fr"].at[b], (x, k, other, z))

        def forward_all(k, src):
            for other in range(2):
                mine = jnp.logical_and(own, jnp.logical_and(k == ro, x == other))

                @pl.when(jnp.logical_not(mine))
                def _():
                    forward(k, other, src).start()

                @pl.when(mine)
                def _():
                    put(orr, b)[...] = src[...]

        def start(d, carry):
            for copy in along.copies(d, False):
                copy.start()
            to_chip(d, False).start()
            return carry

        lax.fori_loop(1, RING, start, 0, unroll=True)
        first = remote(l_ref, put(ol, b), s["ts"].at[0], s["tr_"].at[0], twin)
        first.start()
        forward_all(z, r_ref)
        put(ol, b)[...] = l_ref[...]

        def relay(d, carry):
            along.arrive(d)
            k = along.sender(d)
            forward_all(k, s["stage"].at[k])
            to_chip(d, True).wait_recv()
            to_twin(d, False).start()
            return carry

        lax.fori_loop(1, RING, relay, 0, unroll=True)

        def left_in(d, carry):
            to_twin(d, True).wait_recv()
            return carry

        lax.fori_loop(0, RING, left_in, 0)

        def come(k, other):
            sender = other * RING + k
            there = put(orr, sender)
            remote(r_ref, there, s["fs"].at[k, other], s["fr"].at[sender], (other, k, br, z)).wait_recv()

        senders(come)

        lane_of = lax.broadcasted_iota(jnp.int32, (channels, lanes), 1) // side
        contract = (((0,), (0,)), ((), ()))

        def channel_push(k, g, d, coming):
            src, dst = (s["tl"], s["l1"]) if k == 0 else (s["tr"], s["r1"])
            cols = pl.ds(pl.multiple_of(g * chunk, chunk), chunk)
            peer = along.sender(d) if coming else lax.rem(z + d, RING)
            return remote(
                src.at[z if coming else peer, :, cols],
                dst.at[peer if coming else z, :, cols],
                s["p1s"].at[k, g, d],
                s["p1r"].at[k, g, d],
                (br, ro, x, peer),
            )

        def front(g, carry):
            cols = pl.ds(pl.multiple_of(g * chunk, chunk), chunk)
            outer = lax.dot_general(ol[:, cols], orr[...], contract, preferred_element_type=f32)
            outer = (outer * (1.0 / (GROUP * rows))).astype(bf16)
            stacked = jnp.concatenate(
                [
                    jnp.concatenate(
                        [
                            outer[i * side : (i + 1) * side, q * lanes : (q + 1) * lanes]
                            for q in range(wide // lanes)
                        ],
                        axis=0,
                    )
                    for i in range(chunk // side)
                ],
                axis=1,
            )
            mixed = lax.dot_general(mix_ref[...], stacked, contract, preferred_element_type=f32)
            pieces = []
            for h in range(chunk // lanes):
                piece = jnp.zeros((channels, lanes), f32)
                for i in range(per):
                    at_lane = (h * per + i) * lanes
                    total = None
                    for y in range(per):
                        part = mixed[y * channels : (y + 1) * channels, at_lane : at_lane + lanes]
                        shift = (side * (i - y)) % lanes
                        part = pltpu.roll(part, shift, 1) if shift else part
                        total = part if total is None else total + part
                    piece = jnp.where(lane_of == i, total, piece)
                pieces.append(piece)
            opm = jnp.transpose(p_ref[cols].astype(f32)) + jnp.concatenate(pieces, axis=1)
            s["opm"][:, cols] = opm
            normed = norm_channels(opm).astype(bf16)
            projected = lax.dot_general(in_ref[...], normed, contract, preferred_element_type=f32)
            block = lambda k: projected[k * channels : (k + 1) * channels]
            here = k_ref[:, cols]
            tri_left = (here * jax.nn.sigmoid(block(0)) * block(1)).astype(bf16)
            tri_right = (here * jax.nn.sigmoid(block(2)) * block(3)).astype(bf16)
            s["tl"][:, :, cols] = tri_left.reshape(RING, deep, chunk)
            s["tr"][:, :, cols] = tri_right.reshape(RING, deep, chunk)
            s["gate"][:, cols] = jax.nn.sigmoid(block(4))

            def push(d, carry):
                for k in range(2):
                    channel_push(k, g, d, False).start()
                return carry

            lax.fori_loop(1, RING, push, 0, unroll=True)
            return carry

        lax.fori_loop(0, chunks, front, 0)
        turn = s["turn"]

        def regroup(src, dst):
            outer, inner, _ = src.shape

            def one(v, carry):
                cols = pl.ds(pl.multiple_of(v * lanes, lanes), lanes)
                for g in range(outer):
                    turn[v, g * inner : (g + 1) * inner] = src[g, :, cols].astype(f32)
                for g in range(inner):
                    dst[g, :, cols] = turn[v, pl.ds(g, outer, stride=inner)].astype(bf16)
                return carry

            lax.fori_loop(0, tokens // lanes, one, 0)

        s["l1"][z] = s["tl"][z]
        s["r1"][z] = s["tr"][z]
        for k, ref in ((0, "l1"), (1, "r1")):

            def arrive(d, carry):
                for g in range(chunks):
                    channel_push(k, g, d, True).wait_recv()
                return carry

            lax.fori_loop(1, RING, arrive, 0)
            to = s["l2"] if k == 0 else s["r2"]
            regroup(s[ref], to)

        def over(d, coming):
            there = s["r3"].at[1 - x if coming else x, to_channel.sender(d)]
            return remote(there, there, s["xs"].at[d], s["xr"].at[d], cross)

        to_channel.start()
        first_over = remote(s["r2"].at[b], s["r3"].at[x, b], s["xs"].at[0], s["xr"].at[0], cross)
        first_over.start()

        def hand(d, carry):
            to_channel.arrive(d)
            over(d, False).start()
            return carry

        lax.fori_loop(1, GROUP, hand, 0, unroll=True)
        lane = lax.broadcasted_iota(jnp.int32, (few, lanes), 1) // side

        def unfold(block, put_line):
            def one(v, carry):
                t = block(pl.ds(pl.multiple_of(v * lanes, lanes), lanes)).astype(f32)
                t = t.reshape(GROUP * few, lanes)
                turned = [t] + [pltpu.roll(t, side * n, 1) for n in range(1, per)]
                for n in range(per):
                    line = []
                    for q in range(GROUP // per):
                        piece = jnp.zeros((few, lanes), f32)
                        for m in range(per):
                            k = (q * per + m) * few
                            piece = jnp.where(lane == m, turned[(m - n) % per][k : k + few], piece)
                        line.append(piece)
                    put_line(v * per + n, jnp.concatenate(line, axis=1))
                return carry

            lax.fori_loop(0, side // per, one, 0)

        lines = lambda i: pl.ds(pl.multiple_of(i * few, few), few)

        def put_left(i, line):
            s["a"][lines(i)] = line

        unfold(lambda cols: s["l3"][:, :, cols], put_left)
        a = s["a"][...].astype(bf16)
        to = lax.broadcasted_iota(jnp.int32, (tall, tall), 0)
        of = lax.broadcasted_iota(jnp.int32, (tall, tall), 1)
        order = (of == lax.rem(to, side) * few + to // side).astype(f32).astype(bf16)

        def multiply(h, carry):
            def put_right(j, line):
                s["b"][h, lines(j)] = line

            unfold(lambda cols: s["r3"][h, :, :, cols], put_right)
            t = jnp.dot(order, s["b"][h].astype(bf16), preferred_element_type=f32).astype(bf16)
            s["y"][:, pl.ds(pl.multiple_of(h * tall, tall), tall)] = lax.dot_general(
                a, t, (((1,), (1,)), ((), ())), preferred_element_type=f32
            )
            return carry

        multiply(x, 0)

        def over_in(d, carry):
            over(d, True).wait_recv()
            return carry

        lax.fori_loop(0, GROUP, over_in, 0)
        multiply(1 - x, 0)

        def fold(v, carry):
            cols = pl.ds(pl.multiple_of(v * lanes, lanes), lanes)
            y = s["y"][pl.ds(pl.multiple_of(v * per * few, per * few), per * few)]
            for q in range(across_k // lanes):
                t = y[:, q * lanes : (q + 1) * lanes]
                turned = [t] + [pltpu.roll(t, side * n, 1) for n in range(1, per)]
                for m in range(per):
                    piece = jnp.zeros((few, lanes), f32)
                    for n in range(per):
                        piece = jnp.where(
                            lane == n, turned[(n - m) % per][n * few : (n + 1) * few], piece
                        )
                    s["m0"][q * per + m, :, cols] = piece.astype(bf16)
            return carry

        lax.fori_loop(0, side // per, fold, 0)
        from_channel.start()
        from_channel.finish()
        regroup(s["m1"], s["m2"])
        from_ring.start()
        from_ring.finish()

        def end(g, carry):
            cols = pl.ds(pl.multiple_of(g * chunk, chunk), chunk)
            mixed = s["m3"][:, :, cols].astype(f32).reshape(channels, chunk)
            mixed = norm_channels(mixed).astype(bf16)
            mixed = lax.dot_general(out_ref[...], mixed, contract, preferred_element_type=f32)
            state = s["opm"][:, cols] + s["gate"][:, cols] * mixed
            normed = norm_channels(state).astype(bf16)
            hidden = lax.dot_general(up_ref[...], normed, contract, preferred_element_type=f32)
            hidden = jnp.maximum(hidden, 0.0).astype(bf16)
            update = lax.dot_general(hidden, down_ref[...], contract, preferred_element_type=f32)
            o_ref[cols] = (jnp.transpose(state) + update).astype(bf16)
            return carry

        lax.fori_loop(0, chunks, end, 0)

        def sent(d, carry):
            along.sent(d)
            for r in range(2):
                row_push(r, d, False).wait_send()
            to_chip(d, False).wait_send()
            to_twin(d, False).wait_send()
            for k in range(2):
                for g in range(chunks):
                    channel_push(k, g, d, False).wait_send()
            return carry

        lax.fori_loop(1, RING, sent, 0)
        first.wait_send()

        def forwarded(k, other):
            mine = jnp.logical_and(own, jnp.logical_and(k == ro, x == other))

            @pl.when(jnp.logical_not(mine))
            def _():
                forward(k, other, r_ref).wait_send()

        each(forwarded)

        def handed(d, carry):
            to_channel.sent(d)
            over(d, False).wait_send()
            return carry

        lax.fori_loop(1, GROUP, handed, 0)
        first_over.wait_send()

    scratch = [pltpu.VMEM(*v) for v in buffers.values()]
    scratch += [pltpu.SemaphoreType.DMA(v) for v in sems.values()]
    scratch += first_scratch
    return call_exchange(
        kernel,
        [jax.ShapeDtypeStruct(entries.shape, bf16), jax.ShapeDtypeStruct((tokens, channels), bf16)],
        scratch, 6, 4 << 20,
        [IN_VMEM] * 2 + [IN_SMEM] + [IN_PLACE] * 8 + [IN_VMEM] + [IN_PLACE] * 3 + [IN_VMEM] + [IN_PLACE] * 3,
        bias_weights, same, chain_bias, row_weights, row_merge, entries, col_weights, col_merge, expand,
        contract_weights, factor_weights, presence, pair, outer_weights, tri_in, keep, tri_out, up, down,
    )


def on_device(
    homolog_embedding,
    pair_representation,
    alignment_entry_mask,
    residue_presence_mask,
    residue_chain_index,
    row_projection_weights,
    horizontal_attend_merge,
    pair_bias_matrix,
    same_chain_bias,
    column_projection_weights,
    vertical_attend_merge,
    homolog_mlp_expand,
    homolog_mlp_contract,
    tensor_product_linear,
    outer_output_matrix,
    triangle_input_weights,
    triangle_output_matrix,
    pair_up_weight,
    pair_down_weight,
):
    device_local_rows, residue_total, channel_count = homolog_embedding.shape
    pair_cols = pair_representation.shape[1]
    row_place = lax.axis_index(COL)
    col_place = lax.axis_index(("branch", "row"))
    chain_here = lax.dynamic_slice_in_dim(
        residue_chain_index, row_place * residue_total, residue_total
    )
    chain_there = lax.dynamic_slice_in_dim(residue_chain_index, col_place * pair_cols, pair_cols)
    residue_keep = residue_presence_mask.astype(jnp.float32)
    keep_here = lax.dynamic_slice_in_dim(residue_keep, row_place * residue_total, residue_total)
    keep_there = lax.dynamic_slice_in_dim(residue_keep, col_place * pair_cols, pair_cols)
    low_first = jnp.transpose(chain_here.reshape(residue_total // 8, 8))
    same_chain = (low_first[:, :, None] == chain_there[None, None, :]).astype(jnp.float32)
    tokens = residue_total * pair_cols
    pair_keep = (keep_here[:, None] * keep_there[None, :]).reshape(1, tokens)
    msa_out, updated_pair_state = whole_block(
        jnp.transpose(pair_bias_matrix),
        same_chain.reshape(8, residue_total // 8 * pair_cols),
        same_chain_bias,
        row_projection_weights,
        horizontal_attend_merge,
        homolog_embedding,
        column_projection_weights,
        vertical_attend_merge,
        homolog_mlp_expand,
        homolog_mlp_contract,
        jnp.transpose(tensor_product_linear),
        alignment_entry_mask,
        pair_representation.reshape(tokens, CZ),
        outer_output_matrix,
        triangle_input_weights,
        pair_keep,
        triangle_output_matrix,
        pair_up_weight,
        pair_down_weight,
    )
    updated_pair_state = updated_pair_state.reshape(residue_total, pair_cols, CZ)
    return (msa_out, updated_pair_state)


def solution(mesh):
    split = Mesh(
        mesh.devices.reshape(mesh.shape["branch"], mesh.shape["row"], 2, 8),
        ("branch", "row", "col_0", "col_1"),
    )
    in_specs = (
        P(("branch", "row"), COL, None),
        P(COL, ("branch", "row"), None),
        P(("branch", "row"), COL),
        P(),
        P(),
        P(),
        P(),
        P(),
        P(),
        P(),
        P(),
        P(),
        P(),
        P(),
        P(),
        P(),
        P(),
        P(),
        P(),
    )
    out_specs = (P(("branch", "row"), COL, None), P(COL, ("branch", "row"), None))
    return jax.shard_map(
        on_device, mesh=split, in_specs=in_specs, out_specs=out_specs, check_vma=False
    )
```
